32 devices in a mesh: ctx: 8 (over z, y), grp: 2 (over core), head: 2 (over x).
Axes of the slice: x: 2, y: 2, z: 4, core: 2. Of those that a mesh axis runs over, the one named last changes fastest.
Arguments:
- residual: bfloat16 [2048, 2880], P(('ctx', 'grp')), may hold values from -10 to 10
- queries: bfloat16 [2048, 2048], P(('ctx', 'grp'), 'head'), may hold values from -32 to 32
- keys: bfloat16 [2048, 256], P(('ctx', 'grp'), 'head'), may hold values from -32 to 32
- values: bfloat16 [2048, 256], P(('ctx', 'grp'), 'head'), may hold values from -12 to 12
- out_weight: bfloat16 [2048, 2880], P('head'), may hold values from -0.125 to 0.125
- norm_gain: float32 [2880], replicated, may hold values from 0.5 to 1.5
- routes: int32 [2048, 4], P(('ctx', 'grp')), may hold values from 0 to 7, all different within a row; in each aligned block of 128 rows (0 to 127, 128 to 255, ...) at most 72 rows name the same one
- expert_weight: bfloat16 [8, 2880, 2, 1536], P('ctx', None, None, 'head'), may hold values from -0.109375 to 0.109375
Outputs:
- hidden: bfloat16 [2048, 2880], P(('ctx', 'grp'), 'head')
- active: bfloat16 [8, 2, 576, 1536], P('ctx', 'grp', None, 'head')
The draws below stay inside these ranges and needn't reach their ends.
Inputs may be any that keep to these rules, and one draw needn't show every extreme that they name: `routes`: each token names 4 different experts; the 128 rows of one device name any one expert at most 72 times.
All inputs are finite; a program needn't handle non-finite values.
Results may differ from the reference program's by a relative error of at most 0.017.
Values may be sent and summed in bfloat16 or wider, within the bound.
A program may use at most 128 MiB of HBM per device.

```python
import math
import jax
import jax.numpy as jnp
import numpy as np
from jax import lax

D = 2880
HD = 64
HEADS = 32
KV_HEADS = 4
FFW = 1536
TOP = 4
TOK_DEV = 128
EXPERTS = 8
CAP = 72
CYCLE = 1
WINDOW = 256
TOKENS = 2048
N_CTX = 8
N_GRP = 2
N_HEAD = 2


def draw_queries(key, part):
    drawn_key = jax.random.fold_in(key, 1)
    drawn = jnp.clip(jax.random.normal(drawn_key, (TOKENS, HEADS * HD)), -4.0, 4.0)
    return drawn.astype(jnp.bfloat16)


def draw_keys(key, part):
    drawn_key = jax.random.fold_in(key, 2)
    drawn = jnp.clip(jax.random.normal(drawn_key, (TOKENS, KV_HEADS * HD)), -4.0, 4.0)
    return drawn.astype(jnp.bfloat16)


def draw_residual(key, part):
    row_key, value_key, column_key = jax.random.split(jax.random.fold_in(key, 3), 3)
    row_scale = jnp.exp(jax.random.uniform(row_key, (TOKENS, 1), minval=jnp.log(0.1), maxval=0.0))
    places = jnp.arange(D, dtype=jnp.float32) / (D - 1)
    jitter = jnp.exp(jax.random.uniform(column_key, (1, D), minval=jnp.log(0.7), maxval=jnp.log(1.4)))
    column_scale = jnp.exp(places * jnp.log(3.0))[None, :] / 1.7 * jitter
    entries = jnp.clip(jax.random.normal(value_key, (TOKENS, D)), -4.0, 4.0)
    return (entries * row_scale * column_scale).astype(jnp.bfloat16)


def steps_of(key, dims, pieces, low, largest):
    factor_of = 1.0
    for position, shards_of in pieces:
        heights = jax.random.uniform(jax.random.fold_in(jax.random.fold_in(key, 6), position), (shards_of,), jnp.float32, low / len(pieces), largest / len(pieces))
        factor_of = factor_of * jnp.repeat(jnp.exp(heights), dims[position] // shards_of).reshape((-1,) + (1,) * (len(dims) - 1 - position))
    return factor_of


def shared_out(rng, own, number, rows, count, top, reach, slope):
    order = jax.random.permutation(rng, count)
    packed, usual = shares(count, rows * top, reach, slope, True), shares(count, rows * top, reach, slope, False)
    places = jnp.arange(count)

    def named(lengths, turn):
        used = int((lengths > 0).sum())
        fixed = max(1, used // 4)
        passed = fixed + (places - fixed + turn * (used - fixed)) % max(1, count - fixed)
        return jnp.zeros((count,), jnp.int32).at[order[jnp.where(places < fixed, places, passed)]].set(jnp.asarray(lengths, jnp.int32))

    lengths = jnp.where(number % 4 == 0, named(packed, number // 4), named(usual, number - number // 4 - 1))
    mixed = jax.random.permutation(jax.random.fold_in(own, 3), count)
    giver, sink = mixed[0:count // 2 * 2:2], mixed[1:count // 2 * 2:2]
    margin = jnp.minimum(lengths[giver] - 1, reach - lengths[sink]) // 2
    margin = jnp.where((giver == order[0]) | (sink == order[0]) | (lengths[sink] == 0), 0, jnp.maximum(margin, 0))
    passed = jax.random.randint(jax.random.fold_in(own, 4), (count // 2,), 0, 1 << 20) % (margin + 1)
    lengths = lengths.at[giver].add(-passed).at[sink].add(passed)
    members = jnp.searchsorted(jnp.cumsum(lengths), jnp.arange(rows * top), side="right").astype(jnp.int32)
    table = members.reshape(top, rows).T
    table = table[jax.random.permutation(jax.random.fold_in(own, 1), rows)]
    turn = jax.random.randint(jax.random.fold_in(own, 2), (rows, 1), 0, top)
    return jnp.take_along_axis(table, (jnp.arange(top)[None, :] + turn) % top, axis=1)


def shares(number_of, total, bound, skew, full):
    portions = [(1 << 20) // math.isqrt(grade ** skew) + 1 for grade in range(1, number_of + 1)]
    largest = bound if full else min(bound, max(-(-total // number_of), total * portions[0] // sum(portions)))
    least = 1 if total - largest >= number_of - 1 else 0
    counts, surplus = [largest] + [least] * (number_of - 1), total - largest - least * (number_of - 1)
    while surplus > 0:
        candidates = [i for i in range(1, number_of) if counts[i] < largest] or [i for i in range(1, number_of) if counts[i] < bound]
        pool, remaining = sum([portions[i] for i in candidates]), surplus
        for i in candidates:
            extra = min(bound - counts[i], max(1, remaining * portions[i] // pool), surplus)
            counts[i] = counts[i] + extra
            surplus = surplus - extra
    return np.array(counts)


def gaussian(rng, shape, width, most, shards=(), kind=jnp.bfloat16):
    drawn = width * jax.random.normal(rng, shape, jnp.float32)
    if shards:
        drawn = drawn * steps_of(rng, shape, shards, -0.22, 0.18)
    return jnp.clip(drawn, -most, most).astype(kind)


def setup_inputs(seed: int = 0) -> dict:
    key_list = jax.random.split(jax.random.key(seed), 9)
    residual = draw_residual(jax.random.fold_in(key_list[8], 71), 0)
    queries = draw_queries(jax.random.fold_in(key_list[8], 71), 0)
    keys = draw_keys(jax.random.fold_in(key_list[8], 71), 0)
    values = gaussian(key_list[3], (TOKENS, KV_HEADS * HD), 2.0, 12.0, ((0, 16), (1, 2)))
    out_weight = gaussian(key_list[4], (HEADS * HD, D), (HEADS * HD) ** -0.5, 0.125, ((0, 2),))
    norm_gain = jnp.clip(1.0 + 0.1 * jax.random.normal(key_list[5], (D,), jnp.float32), 0.5, 1.5)
    routes_keys = jax.random.split(jax.random.fold_in(key_list[6], 1), TOKENS // TOK_DEV)
    routes_turns = jax.random.permutation(jax.random.fold_in(key_list[6], 3), TOKENS // TOK_DEV)
    routes = jax.vmap(lambda own, number: shared_out(jax.random.fold_in(key_list[6], 2), own, number, TOK_DEV, EXPERTS, TOP, CAP, 1))(routes_keys, routes_turns).reshape((TOKENS, TOP))
    expert_weight = gaussian(key_list[7], (EXPERTS, D, 2, FFW), D ** -0.5, 0.109375, ((0, 8), (3, 2)))
    return dict(residual=residual, queries=queries, keys=keys, values=values, out_weight=out_weight, norm_gain=norm_gain, routes=routes, expert_weight=expert_weight)


def attend_rows(query_block, key_window, value_window, query_place, key_place):
    scores = jnp.einsum('bgd,wd->gbw', query_block.astype(jnp.float32), key_window.astype(jnp.float32)) * HD ** (-0.5)
    allowed = (key_place[None, :] <= query_place[:, None]) & (query_place[:, None] - key_place[None, :] < WINDOW) & (key_place[None, :] >= 0)
    scores = jnp.where(allowed[None], scores, -1e+30)
    row_max = lax.optimization_barrier(jnp.max(scores, axis=-1, keepdims=True))
    weights = jnp.where(allowed[None], jnp.exp(scores - row_max), 0.0)
    row_total = lax.optimization_barrier(jnp.sum(weights, axis=-1))
    rounded = lax.optimization_barrier(weights.astype(jnp.bfloat16))
    mixed = jnp.einsum('gbw,wd->gbd', rounded.astype(jnp.float32), value_window.astype(jnp.float32))
    return mixed / row_total[..., None]

def reference(residual, queries, keys, values, out_weight, norm_gain, routes, expert_weight):
    per_group = HEADS // KV_HEADS
    block_len = TOK_DEV * N_GRP
    reach_len = CYCLE * block_len
    pad_keys = jnp.concatenate([jnp.zeros((reach_len, KV_HEADS * HD), keys.dtype), keys], 0)
    pad_values = jnp.concatenate([jnp.zeros((reach_len, KV_HEADS * HD), values.dtype), values], 0)

    def one_block(block_index):
        first_row = (block_index * block_len).astype(jnp.int32)
        query_block = lax.dynamic_slice_in_dim(queries, first_row, block_len, 0).reshape(block_len, KV_HEADS, per_group, HD)
        key_window = lax.dynamic_slice_in_dim(pad_keys, first_row, reach_len + block_len, 0).reshape(reach_len + block_len, KV_HEADS, HD)
        value_window = lax.dynamic_slice_in_dim(pad_values, first_row, reach_len + block_len, 0).reshape(reach_len + block_len, KV_HEADS, HD)
        query_place = first_row + jnp.arange(block_len, dtype=jnp.int32)
        key_place = first_row - reach_len + jnp.arange(reach_len + block_len, dtype=jnp.int32)

        def one_head(operands):
            head_queries, head_keys, head_values = operands
            return attend_rows(head_queries, head_keys, head_values, query_place, key_place)
        heads_out = lax.map(one_head, (jnp.moveaxis(query_block, 1, 0), jnp.moveaxis(key_window, 1, 0), jnp.moveaxis(value_window, 1, 0)))
        return jnp.transpose(heads_out, (2, 0, 1, 3)).reshape(block_len, HEADS * HD).astype(jnp.bfloat16)
    attended = lax.map(one_block, jnp.arange(N_CTX, dtype=jnp.int32)).reshape(TOKENS, HEADS * HD)
    slice_len = HEADS * HD // N_HEAD
    projected = jnp.zeros((TOKENS, D), jnp.float32)
    for head_part in range(N_HEAD):
        partial_value = jnp.dot(attended[:, head_part * slice_len:(head_part + 1) * slice_len], out_weight[head_part * slice_len:(head_part + 1) * slice_len], preferred_element_type=jnp.float32)
        projected = projected + lax.optimization_barrier(partial_value.astype(jnp.bfloat16)).astype(jnp.float32)
    hidden = (residual.astype(jnp.float32) + projected).astype(jnp.bfloat16)
    devices_all = TOKENS // TOK_DEV
    per_device = routes.astype(jnp.int32).reshape(devices_all, TOK_DEV * TOP)
    expert_ids = jnp.arange(EXPERTS, dtype=jnp.int32)

    def ranks_of(device_routes):
        expert_hits = (device_routes[:, None] == expert_ids[None, :]).astype(jnp.int32)
        before = (jnp.cumsum(expert_hits, axis=0) - expert_hits).astype(jnp.int32)
        return lax.optimization_barrier(jnp.sum(before * expert_hits, axis=1)).astype(jnp.int32)
    slot_index = lax.map(ranks_of, per_device).reshape(TOKENS, TOP).astype(jnp.int32)
    token_ids = jnp.arange(TOKENS, dtype=jnp.int32)
    source = token_ids // TOK_DEV
    source_grp = (source % N_GRP).astype(jnp.int32)
    source_ctx = (source // N_GRP).astype(jnp.int32)
    row_index = (source_ctx[:, None] * CAP + slot_index).astype(jnp.int32)
    slot_table = jnp.full((EXPERTS, N_GRP, N_CTX * CAP), TOKENS, jnp.int32)
    slot_table = slot_table.at[routes.astype(jnp.int32), jnp.broadcast_to(source_grp[:, None], (TOKENS, TOP)), row_index].set(jnp.broadcast_to(token_ids[:, None], (TOKENS, TOP)))
    padded = jnp.concatenate([hidden, jnp.zeros((1, D), hidden.dtype)], 0)

    def expert_rows(operands):
        expert_table, weight = operands
        route_rows = padded[expert_table.reshape(-1)].astype(jnp.float32)
        squares = lax.optimization_barrier(jnp.sum(route_rows * route_rows, axis=1))
        scaled = (route_rows * norm_gain[None, :]).astype(jnp.bfloat16)
        gate_up = jnp.dot(scaled, weight.reshape(D, 2 * FFW), preferred_element_type=jnp.float32)
        inverse_rms = lax.rsqrt(squares / D + 1e-05)
        gate_part = gate_up[:, :FFW] * inverse_rms[:, None]
        up_part = gate_up[:, FFW:] * inverse_rms[:, None]
        result = (gate_part * jax.nn.sigmoid(1.702 * gate_part) * (up_part + 1.0)).astype(jnp.bfloat16)
        return result.reshape(N_GRP, N_CTX * CAP, FFW)
    active = lax.map(expert_rows, (slot_table, expert_weight))
    return (hidden, active)
```

```python
import functools
import jax
import jax.numpy as jnp
from jax import lax
from jax.experimental import pallas as pl
from jax.experimental.pallas import tpu as pltpu
from jax.sharding import PartitionSpec as P

D = 2880
HD = 64
TOP = 4


MESH = pl.DeviceIdType.MESH
F32 = jnp.float32
BF16 = jnp.bfloat16


def turn_of(step, count):
    return 1 + lax.rem(step + count // 2 - 1, count - 1)


def in_pair(values, group, lanes):
    zeros = jnp.zeros((values.shape[0], HD), values.dtype)
    if values.shape[1] == HD:
        return jnp.concatenate([values, zeros], 1), jnp.concatenate([zeros, values], 1)
    first = group % 2 == 0
    base = group // 2 * 2 * HD
    pair = values[:, base : base + 2 * HD]
    swapped = jnp.concatenate([pair[:, HD:], pair[:, :HD]], 1)
    low = jnp.where(lanes < HD, pair if first else swapped, jnp.zeros_like(pair))
    high = jnp.where(lanes >= HD, swapped if first else pair, jnp.zeros_like(pair))
    return low, high


def attend(block, reach, q_ref, kbuf, vbuf, att_ref):
    tokens = q_ref.shape[0]
    window = kbuf.shape[0]
    kv_local = kbuf.shape[1] // HD
    pairs = q_ref.shape[1] // (2 * HD * kv_local)
    rows = pairs * tokens
    place = lax.rem(lax.broadcasted_iota(jnp.int32, (rows, window), 0), tokens)
    column = lax.broadcasted_iota(jnp.int32, (rows, window), 1)
    ahead = place + reach * tokens - column
    allowed = (ahead >= 0) & (ahead < reach * tokens) & (column >= (reach - block) * tokens)
    lanes = lax.broadcasted_iota(jnp.int32, (window, 2 * HD), 1)
    left = lax.broadcasted_iota(jnp.int32, (rows, 2 * HD), 1) < HD
    for group in range(kv_local):
        key_pair = in_pair(kbuf[...], group, lanes)
        value_pair = in_pair(vbuf[...], group, lanes)
        first = group * pairs
        queries = jnp.concatenate(
            [
                q_ref[:, (first + p) * 2 * HD : (first + p + 1) * 2 * HD]
                for p in range(pairs)
            ],
            0,
        )
        mixed = jnp.zeros((rows, 2 * HD), F32)
        totals = []
        for side in range(2):
            scores = lax.dot_general(
                queries,
                key_pair[side],
                (((1,), (1,)), ((), ())),
                preferred_element_type=F32,
            )
            scores = jnp.where(allowed, scores * HD ** (-0.5), -1e30)
            row_max = jnp.max(scores, axis=1, keepdims=True)
            weights = jnp.where(allowed, jnp.exp(scores - row_max), 0.0)
            totals.append(jnp.sum(weights, axis=1, keepdims=True))
            mixed = mixed + jnp.dot(
                weights.astype(BF16), value_pair[side], preferred_element_type=F32
            )
        attended = (mixed / jnp.where(left, totals[0], totals[1])).astype(BF16)
        for p in range(pairs):
            att_ref[:, (first + p) * 2 * HD : (first + p + 1) * 2 * HD] = attended[
                p * tokens : (p + 1) * tokens
            ]


def layer_kernel(
    count,
    cap,
    reach,
    q_ref,
    k_ref,
    v_ref,
    res_ref,
    routes_ref,
    gain_ref,
    ow_hbm,
    w_hbm,
    hid_ref,
    act_ref,
    kbuf,
    vbuf,
    att_ref,
    ow,
    paired,
    w,
    psend,
    precv,
    hits_ref,
    before_ref,
    sbuf,
    rbuf,
    ksend_sem,
    krecv_sem,
    ow_sem,
    w_sem,
    psend_sem,
    precv_sem,
    send_sem,
    recv_sem,
    xsend_sem,
    xrecv_sem,
):
    me = lax.axis_index("ctx")
    head = lax.axis_index("head")
    heads = rbuf.shape[0]
    others = [lax.rem(head + j, heads) for j in range(1, heads)]
    half, tokens = hid_ref.shape
    width = act_ref.shape[2]

    def ow_copy(which, slot):
        rows = pl.ds(pl.multiple_of(which * half, 16), half)
        return pltpu.make_async_copy(ow_hbm.at[rows], ow.at[slot], ow_sem.at[slot])

    for j in range(1, heads):
        ow_copy(others[j - 1], j).start()
    ow_copy(head, 0).start()
    pltpu.make_async_copy(w_hbm, paired, w_sem).start()

    barrier = pltpu.get_barrier_semaphore()
    for other in others:
        pl.semaphore_signal(barrier, inc=1, device_id={"head": other}, device_id_type=MESH)

    def greet(step, carry):
        peer = lax.rem(me + step, count)
        pl.semaphore_signal(barrier, inc=1, device_id={"ctx": peer}, device_id_type=MESH)
        return carry

    lax.fori_loop(1, count, greet, 0)

    groups = lax.axis_size("grp")
    block = me * groups + lax.axis_index("grp")
    blocks = count * groups

    def at_block(index):
        return {"ctx": index // groups, "grp": lax.rem(index, groups)}

    for j in range(1, reach + 1):
        for peer in (lax.rem(block + j, blocks), lax.rem(block + blocks - j, blocks)):
            pl.semaphore_signal(barrier, inc=1, device_id=at_block(peer), device_id_type=MESH)

    def window_copies(j):
        place = pl.ds((reach - j) * tokens, tokens)
        target = at_block(lax.rem(block + j, blocks))
        return [
            pltpu.make_async_remote_copy(
                src_ref=source,
                dst_ref=buffer.at[place],
                send_sem=ksend_sem.at[n, j - 1],
                recv_sem=krecv_sem.at[n, j - 1],
                device_id=target,
                device_id_type=MESH,
            )
            for n, (source, buffer) in enumerate(((k_ref, kbuf), (v_ref, vbuf)))
        ]

    pl.semaphore_wait(barrier, count - 1 + heads - 1 + 2 * reach)
    for j in range(1, reach + 1):

        @pl.when(block + j < blocks)
        def _(j=j):
            for copy in window_copies(j):
                copy.start()

    kbuf[reach * tokens :, :] = k_ref[...]
    vbuf[reach * tokens :, :] = v_ref[...]

    def project(slot):
        return lax.dot_general(
            ow[slot], att_ref[...], (((1,), (1,)), ((), ())), preferred_element_type=F32
        ).astype(BF16)

    def exchange(j):
        return pltpu.make_async_remote_copy(
            src_ref=psend.at[j - 1],
            dst_ref=precv.at[j - 1],
            send_sem=psend_sem.at[j - 1],
            recv_sem=precv_sem.at[j - 1],
            device_id={"head": others[j - 1]},
            device_id_type=MESH,
        )

    for j in range(1, reach + 1):

        @pl.when(block >= j)
        def _(j=j):
            for copy in window_copies(j):
                copy.wait_recv()

        @pl.when(block < j)
        def _(j=j):
            place = pl.ds((reach - j) * tokens, tokens)
            kbuf[place, :] = jnp.zeros((tokens, kbuf.shape[1]), BF16)
            vbuf[place, :] = jnp.zeros((tokens, vbuf.shape[1]), BF16)

        @pl.when(block + j < blocks)
        def _(j=j):
            for copy in window_copies(j):
                copy.wait_send()

    attend(block, reach, q_ref, kbuf, vbuf, att_ref)

    for j in range(1, heads):
        ow_copy(others[j - 1], j).wait()
        psend[j - 1] = project(j)
        exchange(j).start()
    ow_copy(head, 0).wait()
    projected = project(0).astype(F32)

    expert_ids = lax.broadcasted_iota(jnp.int32, (count, tokens), 0)
    hits = jnp.zeros((count, tokens), F32)
    for k in range(routes_ref.shape[0]):
        hits = hits + jnp.where(routes_ref[k : k + 1, :] == expert_ids, 1.0, 0.0)
    earlier = jnp.where(
        lax.broadcasted_iota(jnp.int32, (tokens, tokens), 0)
        < lax.broadcasted_iota(jnp.int32, (tokens, tokens), 1),
        1.0,
        0.0,
    ).astype(BF16)
    hits_ref[...] = hits
    before_ref[...] = jnp.dot(hits.astype(BF16), earlier, preferred_element_type=F32)
    residual = res_ref[pl.ds(pl.multiple_of(head * half, 16), half), :].astype(F32)

    for j in range(1, heads):
        exchange(j).wait()
        projected = projected + precv[j - 1].astype(F32)
    hid_ref[...] = (residual + projected).astype(BF16)

    slots = lax.broadcasted_iota(jnp.int32, (cap, tokens), 0).astype(F32)

    def rows_for(expert):
        wanted = hits_ref[pl.ds(expert, 1), :] > 0.5
        picks = jnp.where((slots == before_ref[pl.ds(expert, 1), :]) & wanted, 1.0, 0.0)
        return lax.dot_general(
            picks.astype(BF16),
            hid_ref[...],
            (((1,), (1,)), ((), ())),
            preferred_element_type=F32,
        ).astype(BF16)

    def routed(step):
        turn = turn_of(step, count)
        return pltpu.make_async_remote_copy(
            src_ref=sbuf.at[turn],
            dst_ref=rbuf.at[head, me],
            send_sem=send_sem.at[turn],
            recv_sem=recv_sem.at[me],
            device_id={"ctx": lax.rem(me + turn, count)},
            device_id_type=MESH,
        )

    def landed(source):
        return pltpu.make_async_remote_copy(
            src_ref=rbuf.at[head, source],
            dst_ref=rbuf.at[head, source],
            send_sem=send_sem.at[0],
            recv_sem=recv_sem.at[source],
            device_id={"head": others[0]},
            device_id_type=MESH,
        )

    def crossed(j, source):
        return pltpu.make_async_remote_copy(
            src_ref=rbuf.at[head, source],
            dst_ref=rbuf.at[head, source],
            send_sem=xsend_sem.at[j - 1, source],
            recv_sem=xrecv_sem.at[j - 1, source],
            device_id={"head": others[j - 1]},
            device_id_type=MESH,
        )

    def cross(source):
        for j in range(1, heads):
            crossed(j, source).start()

    def mirror(source):
        for j in range(1, heads):
            origin = lax.rem(head + heads - j, heads)
            pltpu.make_async_remote_copy(
                src_ref=rbuf.at[origin, source],
                dst_ref=rbuf.at[origin, source],
                send_sem=xsend_sem.at[j - 1, source],
                recv_sem=xrecv_sem.at[j - 1, source],
                device_id={"head": others[j - 1]},
                device_id_type=MESH,
            ).wait_recv()

    def dispatch(step, carry):
        turn = turn_of(step, count)
        sbuf[turn] = rows_for(lax.rem(me + turn, count))
        routed(step).start()
        return carry

    lax.fori_loop(0, count - 1, dispatch, 0)
    rbuf[head, me] = rows_for(me)
    cross(me)
    pltpu.make_async_copy(w_hbm, paired, w_sem).wait()

    def unpair(step, carry):
        rows = pl.ds(pl.multiple_of(step * 32, 32), 32)
        pair = paired[rows]
        w[rows, :width] = pair[:, 0, :]
        w[rows, width:] = pair[:, 1, :]
        return carry

    lax.fori_loop(0, w.shape[0] // 32, unpair, 0)

    def expert(source):
        squares = jnp.zeros((cap, 1), F32)
        parts = []
        for part in range(heads):
            rows = rbuf[part, source].astype(F32)
            squares = squares + jnp.sum(rows * rows, axis=1, keepdims=True)
            parts.append((rows * gain_ref[part : part + 1, :]).astype(BF16))
        inverse_rms = lax.rsqrt(squares / (heads * half) + 1e-05)

        def product(low):
            total = jnp.zeros((cap, width), F32)
            for part in range(heads):
                total = total + jnp.dot(
                    parts[part],
                    w[part * half : (part + 1) * half, low : low + width],
                    preferred_element_type=F32,
                )
            return total

        gate = product(0) * inverse_rms
        up = product(width) * inverse_rms
        act_ref[source] = (gate * jax.nn.sigmoid(1.702 * gate) * (up + 1.0)).astype(BF16)

    def receive(step, carry):
        source = lax.rem(me + count - turn_of(step, count), count)
        landed(source).wait_recv()
        cross(source)
        before = jnp.where(
            step == 0, me, lax.rem(me + count - turn_of(jnp.maximum(step - 1, 0), count), count)
        )
        mirror(before)
        expert(before)
        return carry

    lax.fori_loop(0, count - 1, receive, 0)
    last = lax.rem(me + count - turn_of(count - 2, count), count)
    mirror(last)
    expert(last)

    def drain(step, carry):
        routed(step).wait_send()
        for j in range(1, heads):
            crossed(j, lax.rem(me + step + 1, count)).wait_send()
        return carry

    lax.fori_loop(0, count - 1, drain, 0)
    for j in range(1, heads):
        crossed(j, me).wait_send()


def line_kernel(
    count,
    cap,
    reach,
    chunks,
    q_hbm,
    k_hbm,
    v_hbm,
    res_hbm,
    routes_ref,
    gain_ref,
    ow_hbm,
    w_hbm,
    hid_hbm,
    act_hbm,
    q_ref,
    kbuf,
    vbuf,
    res_ref,
    att_ref,
    ow,
    paired,
    w,
    gains,
    psend,
    precv,
    meta,
    zbuf,
    ysend,
    rows,
    cross,
    acc,
    sums,
    out,
    in_sem,
    ksend_sem,
    krecv_sem,
    ow_sem,
    w_sem,
    psend_sem,
    precv_sem,
    msend_sem,
    mrecv_sem,
    zsend_sem,
    zrecv_sem,
    ysend_sem,
    yrecv_sem,
    xsend_sem,
    xrecv_sem,
    hid_sem,
    out_sem,
):
    me = lax.axis_index("ctx")
    head = lax.axis_index("head")
    other = 1 - head
    length = count // 2
    place = me // 2
    side = lax.rem(me, 2)
    half, tokens = hid_hbm.shape
    width = act_hbm.shape[2]
    piece = half // chunks
    groups = lax.axis_size("grp")
    block = me * groups + lax.axis_index("grp")
    blocks = count * groups

    def at_block(index):
        return {"ctx": index // groups, "grp": lax.rem(index, groups)}

    def on_line(position):
        return {"ctx": position * 2 + side}

    partner = {"ctx": place * 2 + 1 - side}
    across = {"head": other}

    barrier = pltpu.get_barrier_semaphore()
    peers = [on_line(lax.rem(place + j, length)) for j in range(1, length)]
    peers += [partner, across]
    for j in range(1, reach + 1):
        peers += [at_block(lax.rem(block + j, blocks)), at_block(lax.rem(block + blocks - j, blocks))]
    for peer in peers:
        pl.semaphore_signal(barrier, inc=1, device_id=peer, device_id_type=MESH)

    def own_rows(which):
        return pl.ds(pl.multiple_of(which * half, 16), half)

    mine = pl.ds(reach * tokens, tokens)
    local = [
        pltpu.make_async_copy(k_hbm, kbuf.at[mine], in_sem.at[0]),
        pltpu.make_async_copy(v_hbm, vbuf.at[mine], in_sem.at[1]),
        pltpu.make_async_copy(q_hbm, q_ref, in_sem.at[2]),
        pltpu.make_async_copy(res_hbm.at[own_rows(head)], res_ref, in_sem.at[3]),
    ]
    ow_copies = [
        pltpu.make_async_copy(ow_hbm.at[own_rows(which)], ow.at[n], ow_sem.at[n])
        for n, which in enumerate((other, head))
    ]
    w_copies = [
        pltpu.make_async_copy(w_hbm.at[own_rows(which)], paired.at[pl.ds(n * half, half)], w_sem.at[n])
        for n, which in enumerate((head, other))
    ]
    for copy in local + ow_copies + w_copies:
        copy.start()

    def remote(source, target, send, recv, device):
        return pltpu.make_async_remote_copy(
            src_ref=source,
            dst_ref=target,
            send_sem=send,
            recv_sem=recv,
            device_id=device,
            device_id_type=MESH,
        )

    def window_copies(j):
        rows_at = pl.ds((reach - j) * tokens, tokens)
        target = at_block(lax.rem(block + j, blocks))
        return [
            remote(source, buffer.at[rows_at], ksend_sem.at[n, j - 1], krecv_sem.at[n, j - 1], target)
            for n, (source, buffer) in enumerate(((k_hbm, kbuf), (v_hbm, vbuf)))
        ]

    expert_ids = lax.broadcasted_iota(jnp.int32, (count, tokens), 0)
    hits = jnp.zeros((count, tokens), F32)
    for k in range(routes_ref.shape[0]):
        hits = hits + jnp.where(routes_ref[k : k + 1, :] == expert_ids, 1.0, 0.0)
    earlier = jnp.where(
        lax.broadcasted_iota(jnp.int32, (tokens, tokens), 0)
        < lax.broadcasted_iota(jnp.int32, (tokens, tokens), 1),
        1.0,
        0.0,
    ).astype(BF16)
    before = jnp.dot(hits.astype(BF16), earlier, preferred_element_type=F32)
    meta[place] = jnp.where(hits > 0.5, before, -1.0)

    gain = gain_ref[...]
    low, high = gain[:, :half], gain[:, half:]
    gains[0:1, :] = jnp.where(head == 0, low, high)
    gains[1:2, :] = jnp.where(head == 0, high, low)

    pl.semaphore_wait(barrier, len(peers))
    for j in range(1, reach + 1):

        @pl.when(block + j < blocks)
        def _(j=j):
            for copy in window_copies(j):
                copy.start()

    def meta_copy(j):
        return remote(
            meta.at[place],
            meta.at[place],
            msend_sem.at[j - 1],
            mrecv_sem.at[place],
            on_line(lax.rem(place + j, length)),
        )

    def meta_landed(j):
        source = lax.rem(place + length - j, length)
        return remote(
            meta.at[source], meta.at[source], msend_sem.at[j - 1], mrecv_sem.at[source], across
        )

    for j in range(1, length):
        meta_copy(j).start()

    for j in range(1, reach + 1):

        @pl.when(block < j)
        def _(j=j):
            rows_at = pl.ds((reach - j) * tokens, tokens)
            kbuf[rows_at, :] = jnp.zeros((tokens, kbuf.shape[1]), BF16)
            vbuf[rows_at, :] = jnp.zeros((tokens, vbuf.shape[1]), BF16)

    for copy in local:
        copy.wait()
    for j in range(1, reach + 1):

        @pl.when(block >= j)
        def _(j=j):
            for copy in window_copies(j):
                copy.wait_recv()

    attend(block, reach, q_ref, kbuf, vbuf, att_ref)

    def part(index):
        return pl.ds(index * piece, piece)

    def project(slot, index):
        return lax.dot_general(
            ow[slot, index * piece : (index + 1) * piece, :],
            att_ref[...],
            (((1,), (1,)), ((), ())),
            preferred_element_type=F32,
        ).astype(BF16)

    def exchange(index):
        return remote(
            psend.at[part(index)],
            precv.at[part(index)],
            psend_sem.at[index],
            precv_sem.at[index],
            across,
        )

    ow_copies[0].wait()
    for n in range(chunks):
        psend[n * piece : (n + 1) * piece, :] = project(0, n)
        exchange(n).start()
    ow_copies[1].wait()
    for n in range(chunks):
        span = slice(n * piece, (n + 1) * piece)
        zbuf[place, span, :] = project(1, n)

    def line_copy(owner, index, up):
        to = jnp.where(up == 1, place + 1, place - 1)
        spot = zbuf.at[owner, part(index)]
        return remote(
            spot, spot, zsend_sem.at[up, owner, index], zrecv_sem.at[owner, index], on_line(to)
        )

    def has_next(up):
        return jnp.where(up == 1, place + 1 < length, place > 0)

    for copy in w_copies:
        copy.wait()

    def unpair(step, carry):
        at = pl.ds(pl.multiple_of(step * 32, 32), 32)
        pair = paired[at]
        w[at, :width] = pair[:, 0, :]
        w[at, width:] = pair[:, 1, :]
        return carry

    lax.fori_loop(0, w.shape[0] // 32, unpair, 0)

    for n in range(chunks):
        span = slice(n * piece, (n + 1) * piece)
        exchange(n).wait_recv()
        total = zbuf[place, span, :].astype(F32) + precv[span, :].astype(F32)
        zbuf[place, span, :] = (res_ref[span, :].astype(F32) + total).astype(BF16)
        for up in range(2):

            @pl.when(has_next(up))
            def _(n=n, up=up):
                line_copy(place, n, up).start()

    hid_copy = pltpu.make_async_copy(zbuf.at[place], hid_hbm, hid_sem)
    hid_copy.start()

    for j in range(1, length):
        meta_landed(j).wait_recv()

    slots = lax.broadcasted_iota(jnp.int32, (cap, tokens), 0).astype(F32)

    def y_copy(owner):
        return remote(
            ysend.at[owner], rows.at[owner, 1], ysend_sem.at[owner], yrecv_sem.at[owner], partner
        )

    def x_copy(owner, which):
        return remote(
            rows.at[owner, which],
            cross.at[owner, which],
            xsend_sem.at[owner, which],
            xrecv_sem.at[owner, which],
            across,
        )

    def pick(owner):
        def picks(expert):
            wanted = meta[owner, pl.ds(expert, 1), :]
            return jnp.where(slots == wanted, 1.0, 0.0)

        both = jnp.concatenate([picks(place * 2 + 1 - side), picks(me)], 0).astype(BF16)
        found = lax.dot_general(
            both, zbuf[owner], (((1,), (1,)), ((), ())), preferred_element_type=F32
        )
        ysend[owner] = found[:cap].astype(BF16)
        y_copy(owner).start()
        rows[owner, 0] = found[cap:].astype(BF16)
        x_copy(owner, 0).start()

    def scaled(buffer, owner, n):
        raw = buffer[owner].astype(F32).reshape(2 * cap, half)
        squares = jnp.sum(raw * raw, axis=1, keepdims=True)
        return squares, (raw * gains[n : n + 1, :]).astype(BF16)

    def first(owner):
        squares, left = scaled(rows, owner, 0)
        sums[owner] = jnp.broadcast_to(squares, (2 * cap, sums.shape[2]))
        for low in (0, width):
            acc[owner, :, low : low + width] = jnp.dot(
                left, w[:half, low : low + width], preferred_element_type=F32
            )

    def result(owner, which):
        source = owner * 2 + jnp.where(which == 0, side, 1 - side)
        return pltpu.make_async_copy(out.at[owner, which], act_hbm.at[source], out_sem.at[owner, which])

    def second(owner):
        squares, right = scaled(cross, owner, 1)
        squares = squares + sums[owner][:, :1]
        inverse_rms = lax.rsqrt(squares / (2 * half) + 1e-05)

        def product(low):
            return (
                acc[owner, :, low : low + width]
                + jnp.dot(right, w[half:, low : low + width], preferred_element_type=F32)
            ) * inverse_rms

        gate = product(0)
        up = product(width)
        active = gate * jax.nn.sigmoid(1.702 * gate) * (up + 1.0)
        out[owner] = active.reshape(2, cap, width).astype(BF16)
        for which in range(2):
            result(owner, which).start()

    def owner_of(step, up):
        return jnp.where(up == 1, place + step, place - step)

    def exists(step, up):
        owner = owner_of(step, up)
        return (owner >= 0) & (owner < length) & (step + 1 - up > 0)

    def each(step, action):
        def one(up, carry):
            @pl.when(exists(step, up))
            def _():
                action(owner_of(step, up), up)

            return carry

        lax.fori_loop(0, 2, one, 0)

    def arrive(owner, up):
        @pl.when(owner != place)
        def _():
            for n in range(chunks):
                line_copy(owner, n, 1 - up).wait_recv()

                @pl.when(has_next(1 - up))
                def _(n=n):
                    line_copy(owner, n, 1 - up).start()

    def meet(owner, up):
        y_copy(owner).wait_recv()
        x_copy(owner, 1).start()
        first(owner)

    def finish(owner, up):
        for which in range(2):
            x_copy(owner, which).wait_recv()
        second(owner)

    def advance(step, carry):
        each(step, arrive)
        each(step, lambda owner, up: pick(owner))

        @pl.when(step > 0)
        def _():
            each(step - 1, finish)

        each(step, meet)
        return carry

    lax.fori_loop(0, length, advance, 0)
    each(length - 1, finish)

    def drain(owner, carry):
        y_copy(owner).wait_send()
        for which in range(2):
            x_copy(owner, which).wait_send()
            result(owner, which).wait()
        for n in range(chunks):
            for up in range(2):
                came = jnp.where(up == 1, owner <= place, owner >= place)

                @pl.when(has_next(up) & came)
                def _(n=n, up=up):
                    line_copy(owner, n, up).wait_send()

        return carry

    lax.fori_loop(0, length, drain, 0)
    hid_copy.wait()
    for j in range(1, length):
        meta_copy(j).wait_send()
    for n in range(chunks):
        exchange(n).wait_send()
    for j in range(1, reach + 1):

        @pl.when(block + j < blocks)
        def _(j=j):
            for copy in window_copies(j):
                copy.wait_send()


def along_line(
    count, cap, reach, queries, keys, values, residual, routes, norm_gain, out_weight, expert_weight
):
    tokens = queries.shape[0]
    width_all = residual.shape[1]
    half = width_all // 2
    length = count // 2
    width = expert_weight.shape[3]
    chunks = max(n for n in range(1, 4) if half % (16 * n) == 0)
    in_vmem = pl.BlockSpec(memory_space=pltpu.VMEM)
    in_hbm = pl.BlockSpec(memory_space=pl.ANY)
    dma = pltpu.SemaphoreType.DMA
    return pl.pallas_call(
        functools.partial(line_kernel, count, cap, reach, chunks),
        out_shape=(
            jax.ShapeDtypeStruct((half, tokens), BF16),
            jax.ShapeDtypeStruct((count, cap, width), BF16),
        ),
        in_specs=[in_hbm] * 4 + [in_vmem] * 2 + [in_hbm] * 2,
        out_specs=(in_hbm, in_hbm),
        scratch_shapes=[
            pltpu.VMEM(queries.shape, BF16),
            pltpu.VMEM(((reach + 1) * tokens, keys.shape[1]), BF16),
            pltpu.VMEM(((reach + 1) * tokens, values.shape[1]), BF16),
            pltpu.VMEM((half, tokens), BF16),
            pltpu.VMEM(queries.shape, BF16),
            pltpu.VMEM((2, half, out_weight.shape[0]), BF16),
            pltpu.VMEM((width_all, 2, width), BF16),
            pltpu.VMEM((width_all, 2 * width), BF16),
            pltpu.VMEM((2, half), F32),
            pltpu.VMEM((half, tokens), BF16),
            pltpu.VMEM((half, tokens), BF16),
            pltpu.VMEM((length, count, tokens), F32),
            pltpu.VMEM((length, half, tokens), BF16),
            pltpu.VMEM((length, cap, half), BF16),
            pltpu.VMEM((length, 2, cap, half), BF16),
            pltpu.VMEM((length, 2, cap, half), BF16),
            pltpu.VMEM((length, 2 * cap, 2 * width), F32),
            pltpu.VMEM((length, 2 * cap, 128), F32),
            pltpu.VMEM((length, 2, cap, width), BF16),
            dma((4,)),
            dma((2, reach)),
            dma((2, reach)),
            dma((2,)),
            dma((2,)),
            dma((chunks,)),
            dma((chunks,)),
            dma((length - 1,)),
            dma((length,)),
            dma((2, length, chunks)),
            dma((length, chunks)),
            dma((length,)),
            dma((length,)),
            dma((length, 2)),
            dma((length, 2)),
            dma,
            dma((length, 2)),
        ],
        compiler_params=pltpu.CompilerParams(
            collective_id=1, has_side_effects=True, vmem_limit_bytes=60 * 1024 * 1024
        ),
    )(
        queries,
        keys,
        values,
        residual.T,
        routes.T,
        norm_gain.reshape(1, width_all),
        out_weight.T,
        expert_weight[0],
    )


def body(residual, queries, keys, values, out_weight, norm_gain, routes, expert_weight):
    tokens_here = queries.shape[0]
    heads_count = lax.axis_size("head")
    reach = max(1, lax.axis_size("ctx") // 16) * lax.axis_size("grp")
    width_all = residual.shape[1]
    half = width_all // heads_count
    count = lax.axis_size("ctx")
    experts_all = expert_weight.shape[0] * count
    routed = tokens_here * TOP
    cap = min(tokens_here, routed // experts_all + max(1, routed // (8 * experts_all)))
    hidden_width = expert_weight.shape[3]
    if heads_count == 2 and count % 2 == 0 and experts_all == count and 2 * cap >= tokens_here:
        hidden, active = along_line(
            count,
            cap,
            reach,
            queries,
            keys,
            values,
            residual,
            routes,
            norm_gain,
            out_weight,
            expert_weight,
        )
        return (hidden.T, active.reshape(1, 1, count * cap, hidden_width))
    in_vmem = pl.BlockSpec(memory_space=pltpu.VMEM)
    in_hbm = pl.BlockSpec(memory_space=pl.ANY)
    hidden, active = pl.pallas_call(
        functools.partial(layer_kernel, count, cap, reach),
        out_shape=(
            jax.ShapeDtypeStruct((half, tokens_here), BF16),
            jax.ShapeDtypeStruct((count, cap, hidden_width), BF16),
        ),
        in_specs=[in_vmem] * 6 + [in_hbm] * 2,
        out_specs=(in_vmem, in_vmem),
        scratch_shapes=[
            pltpu.VMEM(((reach + 1) * tokens_here, keys.shape[1]), BF16),
            pltpu.VMEM(((reach + 1) * tokens_here, values.shape[1]), BF16),
            pltpu.VMEM(queries.shape, BF16),
            pltpu.VMEM((heads_count, half, out_weight.shape[0]), BF16),
            pltpu.VMEM((width_all, 2, hidden_width), BF16),
            pltpu.VMEM((width_all, 2 * hidden_width), BF16),
            pltpu.VMEM((heads_count - 1, half, tokens_here), BF16),
            pltpu.VMEM((heads_count - 1, half, tokens_here), BF16),
            pltpu.VMEM((count, tokens_here), F32),
            pltpu.VMEM((count, tokens_here), F32),
            pltpu.VMEM((count, cap, half), BF16),
            pltpu.VMEM((heads_count, count, cap, half), BF16),
            pltpu.SemaphoreType.DMA((2, reach)),
            pltpu.SemaphoreType.DMA((2, reach)),
            pltpu.SemaphoreType.DMA((heads_count,)),
            pltpu.SemaphoreType.DMA,
            pltpu.SemaphoreType.DMA((heads_count - 1,)),
            pltpu.SemaphoreType.DMA((heads_count - 1,)),
            pltpu.SemaphoreType.DMA((count,)),
            pltpu.SemaphoreType.DMA((count,)),
            pltpu.SemaphoreType.DMA((heads_count - 1, count)),
            pltpu.SemaphoreType.DMA((heads_count - 1, count)),
        ],
        compiler_params=pltpu.CompilerParams(
            collective_id=0, has_side_effects=True, vmem_limit_bytes=60 * 1024 * 1024
        ),
    )(
        queries,
        keys,
        values,
        residual.T,
        routes.T,
        norm_gain.reshape(heads_count, half),
        out_weight.T,
        expert_weight[0],
    )
    return (hidden.T, active.reshape(1, 1, count * cap, hidden_width))


def solution(mesh):
    in_specs = (
        P(("ctx", "grp"), None),
        P(("ctx", "grp"), "head"),
        P(("ctx", "grp"), "head"),
        P(("ctx", "grp"), "head"),
        P("head", None),
        P(),
        P(("ctx", "grp"), None),
        P("ctx", None, None, "head"),
    )
    out_specs = (P(("ctx", "grp"), "head"), P("ctx", "grp", None, "head"))
    return jax.shard_map(body, mesh=mesh, in_specs=in_specs, out_specs=out_specs, check_vma=False)
```

```python
import functools
import jax
import jax.numpy as jnp
from jax import lax
from jax.experimental import pallas as pl
from jax.experimental.pallas import tpu as pltpu
from jax.sharding import PartitionSpec as P

D = 2880
HD = 64
TOP = 4


MESH = pl.DeviceIdType.MESH
F32 = jnp.float32
BF16 = jnp.bfloat16


def turn_of(step, count):
    return 1 + lax.rem(step + count // 2 - 1, count - 1)


def in_pair(values, group, lanes):
    zeros = jnp.zeros((values.shape[0], HD), values.dtype)
    if values.shape[1] == HD:
        return jnp.concatenate([values, zeros], 1), jnp.concatenate([zeros, values], 1)
    first = group % 2 == 0
    base = group // 2 * 2 * HD
    pair = values[:, base : base + 2 * HD]
    swapped = jnp.concatenate([pair[:, HD:], pair[:, :HD]], 1)
    low = jnp.where(lanes < HD, pair if first else swapped, jnp.zeros_like(pair))
    high = jnp.where(lanes >= HD, swapped if first else pair, jnp.zeros_like(pair))
    return low, high


def attend(block, reach, q_ref, kbuf, vbuf, att_ref):
    tokens = q_ref.shape[0]
    window = kbuf.shape[0]
    kv_local = kbuf.shape[1] // HD
    pairs = q_ref.shape[1] // (2 * HD * kv_local)
    rows = pairs * tokens
    place = lax.rem(lax.broadcasted_iota(jnp.int32, (rows, window), 0), tokens)
    column = lax.broadcasted_iota(jnp.int32, (rows, window), 1)
    ahead = place + reach * tokens - column
    allowed = (ahead >= 0) & (ahead < reach * tokens) & (column >= (reach - block) * tokens)
    lanes = lax.broadcasted_iota(jnp.int32, (window, 2 * HD), 1)
    left = lax.broadcasted_iota(jnp.int32, (rows, 2 * HD), 1) < HD
    for group in range(kv_local):
        key_pair = in_pair(kbuf[...], group, lanes)
        value_pair = in_pair(vbuf[...], group, lanes)
        first = group * pairs
        queries = jnp.concatenate(
            [
                q_ref[:, (first + p) * 2 * HD : (first + p + 1) * 2 * HD]
                for p in range(pairs)
            ],
            0,
        )
        mixed = jnp.zeros((rows, 2 * HD), F32)
        totals = []
        for side in range(2):
            scores = lax.dot_general(
                queries,
                key_pair[side],
                (((1,), (1,)), ((), ())),
                preferred_element_type=F32,
            )
            scores = jnp.where(allowed, scores * HD ** (-0.5), -1e30)
            row_max = jnp.max(scores, axis=1, keepdims=True)
            weights = jnp.where(allowed, jnp.exp(scores - row_max), 0.0)
            totals.append(jnp.sum(weights, axis=1, keepdims=True))
            mixed = mixed + jnp.dot(
                weights.astype(BF16), value_pair[side], preferred_element_type=F32
            )
        attended = (mixed / jnp.where(left, totals[0], totals[1])).astype(BF16)
        for p in range(pairs):
            att_ref[:, (first + p) * 2 * HD : (first + p + 1) * 2 * HD] = attended[
                p * tokens : (p + 1) * tokens
            ]


def layer_kernel(
    count,
    cap,
    reach,
    q_ref,
    k_ref,
    v_ref,
    res_ref,
    routes_ref,
    gain_ref,
    ow_hbm,
    w_hbm,
    hid_ref,
    act_ref,
    kbuf,
    vbuf,
    att_ref,
    ow,
    paired,
    w,
    psend,
    precv,
    hits_ref,
    before_ref,
    sbuf,
    rbuf,
    ksend_sem,
    krecv_sem,
    ow_sem,
    w_sem,
    psend_sem,
    precv_sem,
    send_sem,
    recv_sem,
    xsend_sem,
    xrecv_sem,
):
    me = lax.axis_index("ctx")
    head = lax.axis_index("head")
    heads = rbuf.shape[0]
    others = [lax.rem(head + j, heads) for j in range(1, heads)]
    half, tokens = hid_ref.shape
    width = act_ref.shape[2]

    def ow_copy(which, slot):
        rows = pl.ds(pl.multiple_of(which * half, 16), half)
        return pltpu.make_async_copy(ow_hbm.at[rows], ow.at[slot], ow_sem.at[slot])

    for j in range(1, heads):
        ow_copy(others[j - 1], j).start()
    ow_copy(head, 0).start()
    pltpu.make_async_copy(w_hbm, paired, w_sem).start()

    barrier = pltpu.get_barrier_semaphore()
    for other in others:
        pl.semaphore_signal(barrier, inc=1, device_id={"head": other}, device_id_type=MESH)

    def greet(step, carry):
        peer = lax.rem(me + step, count)
        pl.semaphore_signal(barrier, inc=1, device_id={"ctx": peer}, device_id_type=MESH)
        return carry

    lax.fori_loop(1, count, greet, 0)

    groups = lax.axis_size("grp")
    block = me * groups + lax.axis_index("grp")
    blocks = count * groups

    def at_block(index):
        return {"ctx": index // groups, "grp": lax.rem(index, groups)}

    for j in range(1, reach + 1):
        for peer in (lax.rem(block + j, blocks), lax.rem(block + blocks - j, blocks)):
            pl.semaphore_signal(barrier, inc=1, device_id=at_block(peer), device_id_type=MESH)

    def window_copies(j):
        place = pl.ds((reach - j) * tokens, tokens)
        target = at_block(lax.rem(block + j, blocks))
        return [
            pltpu.make_async_remote_copy(
                src_ref=source,
                dst_ref=buffer.at[place],
                send_sem=ksend_sem.at[n, j - 1],
                recv_sem=krecv_sem.at[n, j - 1],
                device_id=target,
                device_id_type=MESH,
            )
            for n, (source, buffer) in enumerate(((k_ref, kbuf), (v_ref, vbuf)))
        ]

    pl.semaphore_wait(barrier, count - 1 + heads - 1 + 2 * reach)
    for j in range(1, reach + 1):

        @pl.when(block + j < blocks)
        def _(j=j):
            for copy in window_copies(j):
                copy.start()

    kbuf[reach * tokens :, :] = k_ref[...]
    vbuf[reach * tokens :, :] = v_ref[...]

    def project(slot):
        return lax.dot_general(
            ow[slot], att_ref[...], (((1,), (1,)), ((), ())), preferred_element_type=F32
        ).astype(BF16)

    def exchange(j):
        return pltpu.make_async_remote_copy(
            src_ref=psend.at[j - 1],
            dst_ref=precv.at[j - 1],
            send_sem=psend_sem.at[j - 1],
            recv_sem=precv_sem.at[j - 1],
            device_id={"head": others[j - 1]},
            device_id_type=MESH,
        )

    for j in range(1, reach + 1):

        @pl.when(block >= j)
        def _(j=j):
            for copy in window_copies(j):
                copy.wait_recv()

        @pl.when(block < j)
        def _(j=j):
            place = pl.ds((reach - j) * tokens, tokens)
            kbuf[place, :] = jnp.zeros((tokens, kbuf.shape[1]), BF16)
            vbuf[place, :] = jnp.zeros((tokens, vbuf.shape[1]), BF16)

        @pl.when(block + j < blocks)
        def _(j=j):
            for copy in window_copies(j):
                copy.wait_send()

    attend(block, reach, q_ref, kbuf, vbuf, att_ref)

    for j in range(1, heads):
        ow_copy(others[j - 1], j).wait()
        psend[j - 1] = project(j)
        exchange(j).start()
    ow_copy(head, 0).wait()
    projected = project(0).astype(F32)

    expert_ids = lax.broadcasted_iota(jnp.int32, (count, tokens), 0)
    hits = jnp.zeros((count, tokens), F32)
    for k in range(routes_ref.shape[0]):
        hits = hits + jnp.where(routes_ref[k : k + 1, :] == expert_ids, 1.0, 0.0)
    earlier = jnp.where(
        lax.broadcasted_iota(jnp.int32, (tokens, tokens), 0)
        < lax.broadcasted_iota(jnp.int32, (tokens, tokens), 1),
        1.0,
        0.0,
    ).astype(BF16)
    hits_ref[...] = hits
    before_ref[...] = jnp.dot(hits.astype(BF16), earlier, preferred_element_type=F32)
    residual = res_ref[pl.ds(pl.multiple_of(head * half, 16), half), :].astype(F32)

    for j in range(1, heads):
        exchange(j).wait()
        projected = projected + precv[j - 1].astype(F32)
    hid_ref[...] = (residual + projected).astype(BF16)

    slots = lax.broadcasted_iota(jnp.int32, (cap, tokens), 0).astype(F32)

    def rows_for(expert):
        wanted = hits_ref[pl.ds(expert, 1), :] > 0.5
        picks = jnp.where((slots == before_ref[pl.ds(expert, 1), :]) & wanted, 1.0, 0.0)
        return lax.dot_general(
            picks.astype(BF16),
            hid_ref[...],
            (((1,), (1,)), ((), ())),
            preferred_element_type=F32,
        ).astype(BF16)

    def routed(step):
        turn = turn_of(step, count)
        return pltpu.make_async_remote_copy(
            src_ref=sbuf.at[turn],
            dst_ref=rbuf.at[head, me],
            send_sem=send_sem.at[turn],
            recv_sem=recv_sem.at[me],
            device_id={"ctx": lax.rem(me + turn, count)},
            device_id_type=MESH,
        )

    def landed(source):
        return pltpu.make_async_remote_copy(
            src_ref=rbuf.at[head, source],
            dst_ref=rbuf.at[head, source],
            send_sem=send_sem.at[0],
            recv_sem=recv_sem.at[source],
            device_id={"head": others[0]},
            device_id_type=MESH,
        )

    def crossed(j, source):
        return pltpu.make_async_remote_copy(
            src_ref=rbuf.at[head, source],
            dst_ref=rbuf.at[head, source],
            send_sem=xsend_sem.at[j - 1, source],
            recv_sem=xrecv_sem.at[j - 1, source],
            device_id={"head": others[j - 1]},
            device_id_type=MESH,
        )

    def cross(source):
        for j in range(1, heads):
            crossed(j, source).start()

    def mirror(source):
        for j in range(1, heads):
            origin = lax.rem(head + heads - j, heads)
            pltpu.make_async_remote_copy(
                src_ref=rbuf.at[origin, source],
                dst_ref=rbuf.at[origin, source],
                send_sem=xsend_sem.at[j - 1, source],
                recv_sem=xrecv_sem.at[j - 1, source],
                device_id={"head": others[j - 1]},
                device_id_type=MESH,
            ).wait_recv()

    def dispatch(step, carry):
        turn = turn_of(step, count)
        sbuf[turn] = rows_for(lax.rem(me + turn, count))
        routed(step).start()
        return carry

    lax.fori_loop(0, count - 1, dispatch, 0)
    rbuf[head, me] = rows_for(me)
    cross(me)
    pltpu.make_async_copy(w_hbm, paired, w_sem).wait()

    def unpair(step, carry):
        rows = pl.ds(pl.multiple_of(step * 32, 32), 32)
        pair = jnp.swapaxes(paired[rows], 0, 1)
        w[rows, :width] = pair[0]
        w[rows, width:] = pair[1]
        return carry

    lax.fori_loop(0, w.shape[0] // 32, unpair, 0)

    def expert(source):
        squares = jnp.zeros((cap, 1), F32)
        parts = []
        for part in range(heads):
            rows = rbuf[part, source].astype(F32)
            squares = squares + jnp.sum(rows * rows, axis=1, keepdims=True)
            parts.append((rows * gain_ref[part : part + 1, :]).astype(BF16))
        inverse_rms = lax.rsqrt(squares / (heads * half) + 1e-05)

        def product(low):
            total = jnp.zeros((cap, width), F32)
            for part in range(heads):
                total = total + jnp.dot(
                    parts[part],
                    w[part * half : (part + 1) * half, low : low + width],
                    preferred_element_type=F32,
                )
            return total

        gate = product(0) * inverse_rms
        up = product(width) * inverse_rms
        act_ref[source] = (gate * jax.nn.sigmoid(1.702 * gate) * (up + 1.0)).astype(BF16)

    def receive(step, carry):
        source = lax.rem(me + count - turn_of(step, count), count)
        landed(source).wait_recv()
        cross(source)
        before = jnp.where(
            step == 0, me, lax.rem(me + count - turn_of(jnp.maximum(step - 1, 0), count), count)
        )
        mirror(before)
        expert(before)
        return carry

    lax.fori_loop(0, count - 1, receive, 0)
    last = lax.rem(me + count - turn_of(count - 2, count), count)
    mirror(last)
    expert(last)

    def drain(step, carry):
        routed(step).wait_send()
        for j in range(1, heads):
            crossed(j, lax.rem(me + step + 1, count)).wait_send()
        return carry

    lax.fori_loop(0, count - 1, drain, 0)
    for j in range(1, heads):
        crossed(j, me).wait_send()


def line_kernel(
    count,
    cap,
    reach,
    chunks,
    q_hbm,
    k_hbm,
    v_hbm,
    res_hbm,
    routes_ref,
    gain_ref,
    ow_hbm,
    w_hbm,
    hid_hbm,
    act_hbm,
    q_ref,
    kbuf,
    vbuf,
    res_ref,
    att_ref,
    ow,
    paired,
    w,
    gains,
    psend,
    precv,
    meta,
    zbuf,
    ysend,
    rows,
    cross,
    acc,
    sums,
    out,
    in_sem,
    ksend_sem,
    krecv_sem,
    ow_sem,
    w_sem,
    psend_sem,
    precv_sem,
    msend_sem,
    mrecv_sem,
    zsend_sem,
    zrecv_sem,
    ysend_sem,
    yrecv_sem,
    xsend_sem,
    xrecv_sem,
    hid_sem,
    out_sem,
):
    me = lax.axis_index("ctx")
    head = lax.axis_index("head")
    other = 1 - head
    length = count // 2
    place = me // 2
    side = lax.rem(me, 2)
    half, tokens = hid_hbm.shape
    width = act_hbm.shape[2]
    piece = half // chunks
    groups = lax.axis_size("grp")
    block = me * groups + lax.axis_index("grp")
    blocks = count * groups

    def at_block(index):
        return {"ctx": index // groups, "grp": lax.rem(index, groups)}

    def on_line(position):
        return {"ctx": position * 2 + side}

    partner = {"ctx": place * 2 + 1 - side}
    across = {"head": other}

    barrier = pltpu.get_barrier_semaphore()
    peers = [on_line(lax.rem(place + j, length)) for j in range(1, length)]
    peers += [partner, across]
    for j in range(1, reach + 1):
        peers += [at_block(lax.rem(block + j, blocks)), at_block(lax.rem(block + blocks - j, blocks))]
    for peer in peers:
        pl.semaphore_signal(barrier, inc=1, device_id=peer, device_id_type=MESH)

    def own_rows(which):
        return pl.ds(pl.multiple_of(which * half, 16), half)

    mine = pl.ds(reach * tokens, tokens)
    local = [
        pltpu.make_async_copy(k_hbm, kbuf.at[mine], in_sem.at[0]),
        pltpu.make_async_copy(v_hbm, vbuf.at[mine], in_sem.at[1]),
        pltpu.make_async_copy(q_hbm, q_ref, in_sem.at[2]),
        pltpu.make_async_copy(res_hbm.at[own_rows(head)], res_ref, in_sem.at[3]),
    ]
    ow_copies = [
        pltpu.make_async_copy(ow_hbm.at[own_rows(which)], ow.at[n], ow_sem.at[n])
        for n, which in enumerate((other, head))
    ]
    w_copies = [
        pltpu.make_async_copy(w_hbm.at[own_rows(which)], paired.at[pl.ds(n * half, half)], w_sem.at[n])
        for n, which in enumerate((head, other))
    ]
    for copy in local + ow_copies + w_copies:
        copy.start()

    def remote(source, target, send, recv, device):
        return pltpu.make_async_remote_copy(
            src_ref=source,
            dst_ref=target,
            send_sem=send,
            recv_sem=recv,
            device_id=device,
            device_id_type=MESH,
        )

    def window_copies(j):
        rows_at = pl.ds((reach - j) * tokens, tokens)
        target = at_block(lax.rem(block + j, blocks))
        return [
            remote(source, buffer.at[rows_at], ksend_sem.at[n, j - 1], krecv_sem.at[n, j - 1], target)
            for n, (source, buffer) in enumerate(((k_hbm, kbuf), (v_hbm, vbuf)))
        ]

    expert_ids = lax.broadcasted_iota(jnp.int32, (count, tokens), 0)
    hits = jnp.zeros((count, tokens), F32)
    for k in range(routes_ref.shape[0]):
        hits = hits + jnp.where(routes_ref[k : k + 1, :] == expert_ids, 1.0, 0.0)
    earlier = jnp.where(
        lax.broadcasted_iota(jnp.int32, (tokens, tokens), 0)
        < lax.broadcasted_iota(jnp.int32, (tokens, tokens), 1),
        1.0,
        0.0,
    ).astype(BF16)
    before = jnp.dot(hits.astype(BF16), earlier, preferred_element_type=F32)
    meta[place] = jnp.where(hits > 0.5, before, -1.0)

    gain = gain_ref[...]
    low, high = gain[:, :half], gain[:, half:]
    gains[0:1, :] = jnp.where(head == 0, low, high)
    gains[1:2, :] = jnp.where(head == 0, high, low)

    pl.semaphore_wait(barrier, len(peers))
    for j in range(1, reach + 1):

        @pl.when(block + j < blocks)
        def _(j=j):
            for copy in window_copies(j):
                copy.start()

    def meta_copy(j):
        return remote(
            meta.at[place],
            meta.at[place],
            msend_sem.at[j - 1],
            mrecv_sem.at[place],
            on_line(lax.rem(place + j, length)),
        )

    def meta_landed(j):
        source = lax.rem(place + length - j, length)
        return remote(
            meta.at[source], meta.at[source], msend_sem.at[j - 1], mrecv_sem.at[source], across
        )

    for j in range(1, length):
        meta_copy(j).start()

    for j in range(1, reach + 1):

        @pl.when(block < j)
        def _(j=j):
            rows_at = pl.ds((reach - j) * tokens, tokens)
            kbuf[rows_at, :] = jnp.zeros((tokens, kbuf.shape[1]), BF16)
            vbuf[rows_at, :] = jnp.zeros((tokens, vbuf.shape[1]), BF16)

    for copy in local:
        copy.wait()
    for j in range(1, reach + 1):

        @pl.when(block >= j)
        def _(j=j):
            for copy in window_copies(j):
                copy.wait_recv()

    attend(block, reach, q_ref, kbuf, vbuf, att_ref)

    def part(index):
        return pl.ds(index * piece, piece)

    def project(slot, index):
        return lax.dot_general(
            ow[slot, index * piece : (index + 1) * piece, :],
            att_ref[...],
            (((1,), (1,)), ((), ())),
            preferred_element_type=F32,
        ).astype(BF16)

    def exchange(index):
        return remote(
            psend.at[part(index)],
            precv.at[part(index)],
            psend_sem.at[index],
            precv_sem.at[index],
            across,
        )

    ow_copies[0].wait()
    for n in range(chunks):
        psend[n * piece : (n + 1) * piece, :] = project(0, n)
        exchange(n).start()
    ow_copies[1].wait()
    for n in range(chunks):
        span = slice(n * piece, (n + 1) * piece)
        zbuf[place, span, :] = project(1, n)

    def line_copy(owner, index, up):
        to = jnp.where(up == 1, place + 1, place - 1)
        spot = zbuf.at[owner, part(index)]
        return remote(
            spot, spot, zsend_sem.at[up, owner, index], zrecv_sem.at[owner, index], on_line(to)
        )

    def has_next(up):
        return jnp.where(up == 1, place + 1 < length, place > 0)

    for copy in w_copies:
        copy.wait()

    def unpair(step, carry):
        at = pl.ds(pl.multiple_of(step * 32, 32), 32)
        pair = jnp.swapaxes(paired[at], 0, 1)
        w[at, :width] = pair[0]
        w[at, width:] = pair[1]
        return carry

    lax.fori_loop(0, w.shape[0] // 32, unpair, 0)

    for n in range(chunks):
        span = slice(n * piece, (n + 1) * piece)
        exchange(n).wait_recv()
        total = zbuf[place, span, :].astype(F32) + precv[span, :].astype(F32)
        zbuf[place, span, :] = (res_ref[span, :].astype(F32) + total).astype(BF16)
        for up in range(2):

            @pl.when(has_next(up))
            def _(n=n, up=up):
                line_copy(place, n, up).start()

    hid_copy = pltpu.make_async_copy(zbuf.at[place], hid_hbm, hid_sem)
    hid_copy.start()

    for j in range(1, length):
        meta_landed(j).wait_recv()

    slots = lax.broadcasted_iota(jnp.int32, (cap, tokens), 0).astype(F32)

    def y_copy(owner):
        return remote(
            ysend.at[owner], rows.at[owner, 1], ysend_sem.at[owner], yrecv_sem.at[owner], partner
        )

    def x_copy(owner, which):
        return remote(
            rows.at[owner, which],
            cross.at[owner, which],
            xsend_sem.at[owner, which],
            xrecv_sem.at[owner, which],
            across,
        )

    def pick(owner):
        def picks(expert):
            wanted = meta[owner, pl.ds(expert, 1), :]
            return jnp.where(slots == wanted, 1.0, 0.0)

        both = jnp.concatenate([picks(place * 2 + 1 - side), picks(me)], 0).astype(BF16)
        found = lax.dot_general(
            both, zbuf[owner], (((1,), (1,)), ((), ())), preferred_element_type=F32
        )
        ysend[owner] = found[:cap].astype(BF16)
        y_copy(owner).start()
        rows[owner, 0] = found[cap:].astype(BF16)
        x_copy(owner, 0).start()

    def scaled(buffer, owner, n):
        raw = buffer[owner].astype(F32).reshape(2 * cap, half)
        squares = jnp.sum(raw * raw, axis=1, keepdims=True)
        return squares, (raw * gains[n : n + 1, :]).astype(BF16)

    def first(owner):
        squares, left = scaled(rows, owner, 0)
        sums[owner] = jnp.broadcast_to(squares, (2 * cap, sums.shape[2]))
        for low in (0, width):
            acc[owner, :, low : low + width] = jnp.dot(
                left, w[:half, low : low + width], preferred_element_type=F32
            )

    def result(owner, which):
        source = owner * 2 + jnp.where(which == 0, side, 1 - side)
        return pltpu.make_async_copy(out.at[owner, which], act_hbm.at[source], out_sem.at[owner, which])

    def second(owner):
        squares, right = scaled(cross, owner, 1)
        squares = squares + sums[owner][:, :1]
        inverse_rms = lax.rsqrt(squares / (2 * half) + 1e-05)

        def product(low):
            return (
                acc[owner, :, low : low + width]
                + jnp.dot(right, w[half:, low : low + width], preferred_element_type=F32)
            ) * inverse_rms

        gate = product(0)
        up = product(width)
        active = gate * jax.nn.sigmoid(1.702 * gate) * (up + 1.0)
        out[owner] = active.reshape(2, cap, width).astype(BF16)
        for which in range(2):
            result(owner, which).start()

    def owner_of(step, up):
        return jnp.where(up == 1, place + step, place - step)

    def exists(step, up):
        owner = owner_of(step, up)
        return (owner >= 0) & (owner < length) & (step + 1 - up > 0)

    def each(step, action):
        def one(up, carry):
            @pl.when(exists(step, up))
            def _():
                action(owner_of(step, up), up)

            return carry

        lax.fori_loop(0, 2, one, 0)

    def arrive(owner, up):
        @pl.when(owner != place)
        def _():
            for n in range(chunks):
                line_copy(owner, n, 1 - up).wait_recv()

                @pl.when(has_next(1 - up))
                def _(n=n):
                    line_copy(owner, n, 1 - up).start()

    def meet(owner, up):
        y_copy(owner).wait_recv()
        x_copy(owner, 1).start()
        first(owner)

    def finish(owner, up):
        for which in range(2):
            x_copy(owner, which).wait_recv()
        second(owner)

    def advance(step, carry):
        each(step, arrive)
        each(step, lambda owner, up: pick(owner))

        @pl.when(step > 0)
        def _():
            each(step - 1, finish)

        each(step, meet)
        return carry

    lax.fori_loop(0, length + 1, advance, 0)

    def drain(owner, carry):
        y_copy(owner).wait_send()
        for which in range(2):
            x_copy(owner, which).wait_send()
            result(owner, which).wait()
        for n in range(chunks):
            for up in range(2):
                came = jnp.where(up == 1, owner <= place, owner >= place)

                @pl.when(has_next(up) & came)
                def _(n=n, up=up):
                    line_copy(owner, n, up).wait_send()

        return carry

    lax.fori_loop(0, length, drain, 0)
    hid_copy.wait()
    for j in range(1, length):
        meta_copy(j).wait_send()
    for n in range(chunks):
        exchange(n).wait_send()
    for j in range(1, reach + 1):

        @pl.when(block + j < blocks)
        def _(j=j):
            for copy in window_copies(j):
                copy.wait_send()


def along_line(
    count, cap, reach, queries, keys, values, residual, routes, norm_gain, out_weight, expert_weight
):
    tokens = queries.shape[0]
    width_all = residual.shape[1]
    half = width_all // 2
    length = count // 2
    width = expert_weight.shape[3]
    chunks = max(n for n in range(1, 4) if half % (16 * n) == 0)
    in_vmem = pl.BlockSpec(memory_space=pltpu.VMEM)
    in_hbm = pl.BlockSpec(memory_space=pl.ANY)
    dma = pltpu.SemaphoreType.DMA
    return pl.pallas_call(
        functools.partial(line_kernel, count, cap, reach, chunks),
        out_shape=(
            jax.ShapeDtypeStruct((half, tokens), BF16),
            jax.ShapeDtypeStruct((count, cap, width), BF16),
        ),
        in_specs=[in_hbm] * 4 + [in_vmem] * 2 + [in_hbm] * 2,
        out_specs=(in_hbm, in_hbm),
        scratch_shapes=[
            pltpu.VMEM(queries.shape, BF16),
            pltpu.VMEM(((reach + 1) * tokens, keys.shape[1]), BF16),
            pltpu.VMEM(((reach + 1) * tokens, values.shape[1]), BF16),
            pltpu.VMEM((half, tokens), BF16),
            pltpu.VMEM(queries.shape, BF16),
            pltpu.VMEM((2, half, out_weight.shape[0]), BF16),
            pltpu.VMEM((width_all, 2, width), BF16),
            pltpu.VMEM((width_all, 2 * width), BF16),
            pltpu.VMEM((2, half), F32),
            pltpu.VMEM((half, tokens), BF16),
            pltpu.VMEM((half, tokens), BF16),
            pltpu.VMEM((length, count, tokens), F32),
            pltpu.VMEM((length, half, tokens), BF16),
            pltpu.VMEM((length, cap, half), BF16),
            pltpu.VMEM((length, 2, cap, half), BF16),
            pltpu.VMEM((length, 2, cap, half), BF16),
            pltpu.VMEM((length, 2 * cap, 2 * width), F32),
            pltpu.VMEM((length, 2 * cap, 128), F32),
            pltpu.VMEM((length, 2, cap, width), BF16),
            dma((4,)),
            dma((2, reach)),
            dma((2, reach)),
            dma((2,)),
            dma((2,)),
            dma((chunks,)),
            dma((chunks,)),
            dma((length - 1,)),
            dma((length,)),
            dma((2, length, chunks)),
            dma((length, chunks)),
            dma((length,)),
            dma((length,)),
            dma((length, 2)),
            dma((length, 2)),
            dma,
            dma((length, 2)),
        ],
        compiler_params=pltpu.CompilerParams(
            collective_id=1, has_side_effects=True, vmem_limit_bytes=60 * 1024 * 1024
        ),
    )(
        queries,
        keys,
        values,
        residual.T,
        routes.T,
        norm_gain.reshape(1, width_all),
        out_weight.T,
        expert_weight[0],
    )


def body(residual, queries, keys, values, out_weight, norm_gain, routes, expert_weight):
    tokens_here = queries.shape[0]
    heads_count = lax.axis_size("head")
    reach = max(1, lax.axis_size("ctx") // 16) * lax.axis_size("grp")
    width_all = residual.shape[1]
    half = width_all // heads_count
    count = lax.axis_size("ctx")
    experts_all = expert_weight.shape[0] * count
    routed = tokens_here * TOP
    cap = min(tokens_here, routed // experts_all + max(1, routed // (8 * experts_all)))
    hidden_width = expert_weight.shape[3]
    if heads_count == 2 and count % 2 == 0 and experts_all == count and 2 * cap >= tokens_here:
        hidden, active = along_line(
            count,
            cap,
            reach,
            queries,
            keys,
            values,
            residual,
            routes,
            norm_gain,
            out_weight,
            expert_weight,
        )
        return (hidden.T, active.reshape(1, 1, count * cap, hidden_width))
    in_vmem = pl.BlockSpec(memory_space=pltpu.VMEM)
    in_hbm = pl.BlockSpec(memory_space=pl.ANY)
    hidden, active = pl.pallas_call(
        functools.partial(layer_kernel, count, cap, reach),
        out_shape=(
            jax.ShapeDtypeStruct((half, tokens_here), BF16),
            jax.ShapeDtypeStruct((count, cap, hidden_width), BF16),
        ),
        in_specs=[in_vmem] * 6 + [in_hbm] * 2,
        out_specs=(in_vmem, in_vmem),
        scratch_shapes=[
            pltpu.VMEM(((reach + 1) * tokens_here, keys.shape[1]), BF16),
            pltpu.VMEM(((reach + 1) * tokens_here, values.shape[1]), BF16),
            pltpu.VMEM(queries.shape, BF16),
            pltpu.VMEM((heads_count, half, out_weight.shape[0]), BF16),
            pltpu.VMEM((width_all, 2, hidden_width), BF16),
            pltpu.VMEM((width_all, 2 * hidden_width), BF16),
            pltpu.VMEM((heads_count - 1, half, tokens_here), BF16),
            pltpu.VMEM((heads_count - 1, half, tokens_here), BF16),
            pltpu.VMEM((count, tokens_here), F32),
            pltpu.VMEM((count, tokens_here), F32),
            pltpu.VMEM((count, cap, half), BF16),
            pltpu.VMEM((heads_count, count, cap, half), BF16),
            pltpu.SemaphoreType.DMA((2, reach)),
            pltpu.SemaphoreType.DMA((2, reach)),
            pltpu.SemaphoreType.DMA((heads_count,)),
            pltpu.SemaphoreType.DMA,
            pltpu.SemaphoreType.DMA((heads_count - 1,)),
            pltpu.SemaphoreType.DMA((heads_count - 1,)),
            pltpu.SemaphoreType.DMA((count,)),
            pltpu.SemaphoreType.DMA((count,)),
            pltpu.SemaphoreType.DMA((heads_count - 1, count)),
            pltpu.SemaphoreType.DMA((heads_count - 1, count)),
        ],
        compiler_params=pltpu.CompilerParams(
            collective_id=0, has_side_effects=True, vmem_limit_bytes=60 * 1024 * 1024
        ),
    )(
        queries,
        keys,
        values,
        residual.T,
        routes.T,
        norm_gain.reshape(heads_count, half),
        out_weight.T,
        expert_weight[0],
    )
    return (hidden.T, active.reshape(1, 1, count * cap, hidden_width))


def solution(mesh):
    in_specs = (
        P(("ctx", "grp"), None),
        P(("ctx", "grp"), "head"),
        P(("ctx", "grp"), "head"),
        P(("ctx", "grp"), "head"),
        P("head", None),
        P(),
        P(("ctx", "grp"), None),
        P("ctx", None, None, "head"),
    )
    out_specs = (P(("ctx", "grp"), "head"), P("ctx", "grp", None, "head"))
    return jax.shard_map(body, mesh=mesh, in_specs=in_specs, out_specs=out_specs, check_vma=False)
```

```python
import functools
import jax
import jax.numpy as jnp
from jax import lax
from jax.experimental import pallas as pl
from jax.experimental.pallas import tpu as pltpu
from jax.sharding import PartitionSpec as P

D = 2880
HD = 64
TOP = 4


MESH = pl.DeviceIdType.MESH
F32 = jnp.float32
BF16 = jnp.bfloat16


def turn_of(step, count):
    return 1 + lax.rem(step + count // 2 - 1, count - 1)


def in_pair(values, group, lanes):
    zeros = jnp.zeros((values.shape[0], HD), values.dtype)
    if values.shape[1] == HD:
        return jnp.concatenate([values, zeros], 1), jnp.concatenate([zeros, values], 1)
    first = group % 2 == 0
    base = group // 2 * 2 * HD
    pair = values[:, base : base + 2 * HD]
    swapped = jnp.concatenate([pair[:, HD:], pair[:, :HD]], 1)
    low = jnp.where(lanes < HD, pair if first else swapped, jnp.zeros_like(pair))
    high = jnp.where(lanes >= HD, swapped if first else pair, jnp.zeros_like(pair))
    return low, high


def attend(block, reach, q_ref, kbuf, vbuf, att_ref):
    tokens = q_ref.shape[0]
    window = kbuf.shape[0]
    kv_local = kbuf.shape[1] // HD
    pairs = q_ref.shape[1] // (2 * HD * kv_local)
    rows = pairs * tokens
    place = lax.rem(lax.broadcasted_iota(jnp.int32, (rows, window), 0), tokens)
    column = lax.broadcasted_iota(jnp.int32, (rows, window), 1)
    ahead = place + reach * tokens - column
    allowed = (ahead >= 0) & (ahead < reach * tokens) & (column >= (reach - block) * tokens)
    lanes = lax.broadcasted_iota(jnp.int32, (window, 2 * HD), 1)
    left = lax.broadcasted_iota(jnp.int32, (rows, 2 * HD), 1) < HD
    for group in range(kv_local):
        key_pair = in_pair(kbuf[...], group, lanes)
        value_pair = in_pair(vbuf[...], group, lanes)
        first = group * pairs
        queries = jnp.concatenate(
            [
                q_ref[:, (first + p) * 2 * HD : (first + p + 1) * 2 * HD]
                for p in range(pairs)
            ],
            0,
        )
        mixed = jnp.zeros((rows, 2 * HD), F32)
        totals = []
        for side in range(2):
            scores = lax.dot_general(
                queries,
                key_pair[side],
                (((1,), (1,)), ((), ())),
                preferred_element_type=F32,
            )
            scores = jnp.where(allowed, scores * HD ** (-0.5), -1e30)
            row_max = jnp.max(scores, axis=1, keepdims=True)
            weights = jnp.where(allowed, jnp.exp(scores - row_max), 0.0)
            totals.append(jnp.sum(weights, axis=1, keepdims=True))
            mixed = mixed + jnp.dot(
                weights.astype(BF16), value_pair[side], preferred_element_type=F32
            )
        attended = (mixed / jnp.where(left, totals[0], totals[1])).astype(BF16)
        for p in range(pairs):
            att_ref[:, (first + p) * 2 * HD : (first + p + 1) * 2 * HD] = attended[
                p * tokens : (p + 1) * tokens
            ]


def layer_kernel(
    count,
    cap,
    reach,
    q_ref,
    k_ref,
    v_ref,
    res_ref,
    routes_ref,
    gain_ref,
    ow_hbm,
    w_hbm,
    hid_ref,
    act_ref,
    kbuf,
    vbuf,
    att_ref,
    ow,
    paired,
    w,
    psend,
    precv,
    hits_ref,
    before_ref,
    sbuf,
    rbuf,
    ksend_sem,
    krecv_sem,
    ow_sem,
    w_sem,
    psend_sem,
    precv_sem,
    send_sem,
    recv_sem,
    xsend_sem,
    xrecv_sem,
):
    me = lax.axis_index("ctx")
    head = lax.axis_index("head")
    heads = rbuf.shape[0]
    others = [lax.rem(head + j, heads) for j in range(1, heads)]
    half, tokens = hid_ref.shape
    width = act_ref.shape[2]

    def ow_copy(which, slot):
        rows = pl.ds(pl.multiple_of(which * half, 16), half)
        return pltpu.make_async_copy(ow_hbm.at[rows], ow.at[slot], ow_sem.at[slot])

    for j in range(1, heads):
        ow_copy(others[j - 1], j).start()
    ow_copy(head, 0).start()
    pltpu.make_async_copy(w_hbm, paired, w_sem).start()

    barrier = pltpu.get_barrier_semaphore()
    for other in others:
        pl.semaphore_signal(barrier, inc=1, device_id={"head": other}, device_id_type=MESH)

    def greet(step, carry):
        peer = lax.rem(me + step, count)
        pl.semaphore_signal(barrier, inc=1, device_id={"ctx": peer}, device_id_type=MESH)
        return carry

    lax.fori_loop(1, count, greet, 0)

    groups = lax.axis_size("grp")
    block = me * groups + lax.axis_index("grp")
    blocks = count * groups

    def at_block(index):
        return {"ctx": index // groups, "grp": lax.rem(index, groups)}

    for j in range(1, reach + 1):
        for peer in (lax.rem(block + j, blocks), lax.rem(block + blocks - j, blocks)):
            pl.semaphore_signal(barrier, inc=1, device_id=at_block(peer), device_id_type=MESH)

    def window_copies(j):
        place = pl.ds((reach - j) * tokens, tokens)
        target = at_block(lax.rem(block + j, blocks))
        return [
            pltpu.make_async_remote_copy(
                src_ref=source,
                dst_ref=buffer.at[place],
                send_sem=ksend_sem.at[n, j - 1],
                recv_sem=krecv_sem.at[n, j - 1],
                device_id=target,
                device_id_type=MESH,
            )
            for n, (source, buffer) in enumerate(((k_ref, kbuf), (v_ref, vbuf)))
        ]

    pl.semaphore_wait(barrier, count - 1 + heads - 1 + 2 * reach)
    for j in range(1, reach + 1):

        @pl.when(block + j < blocks)
        def _(j=j):
            for copy in window_copies(j):
                copy.start()

    kbuf[reach * tokens :, :] = k_ref[...]
    vbuf[reach * tokens :, :] = v_ref[...]

    def project(slot):
        return lax.dot_general(
            ow[slot], att_ref[...], (((1,), (1,)), ((), ())), preferred_element_type=F32
        ).astype(BF16)

    def exchange(j):
        return pltpu.make_async_remote_copy(
            src_ref=psend.at[j - 1],
            dst_ref=precv.at[j - 1],
            send_sem=psend_sem.at[j - 1],
            recv_sem=precv_sem.at[j - 1],
            device_id={"head": others[j - 1]},
            device_id_type=MESH,
        )

    for j in range(1, reach + 1):

        @pl.when(block >= j)
        def _(j=j):
            for copy in window_copies(j):
                copy.wait_recv()

        @pl.when(block < j)
        def _(j=j):
            place = pl.ds((reach - j) * tokens, tokens)
            kbuf[place, :] = jnp.zeros((tokens, kbuf.shape[1]), BF16)
            vbuf[place, :] = jnp.zeros((tokens, vbuf.shape[1]), BF16)

        @pl.when(block + j < blocks)
        def _(j=j):
            for copy in window_copies(j):
                copy.wait_send()

    attend(block, reach, q_ref, kbuf, vbuf, att_ref)

    for j in range(1, heads):
        ow_copy(others[j - 1], j).wait()
        psend[j - 1] = project(j)
        exchange(j).start()
    ow_copy(head, 0).wait()
    projected = project(0).astype(F32)

    expert_ids = lax.broadcasted_iota(jnp.int32, (count, tokens), 0)
    hits = jnp.zeros((count, tokens), F32)
    for k in range(routes_ref.shape[0]):
        hits = hits + jnp.where(routes_ref[k : k + 1, :] == expert_ids, 1.0, 0.0)
    earlier = jnp.where(
        lax.broadcasted_iota(jnp.int32, (tokens, tokens), 0)
        < lax.broadcasted_iota(jnp.int32, (tokens, tokens), 1),
        1.0,
        0.0,
    ).astype(BF16)
    hits_ref[...] = hits
    before_ref[...] = jnp.dot(hits.astype(BF16), earlier, preferred_element_type=F32)
    residual = res_ref[pl.ds(pl.multiple_of(head * half, 16), half), :].astype(F32)

    for j in range(1, heads):
        exchange(j).wait()
        projected = projected + precv[j - 1].astype(F32)
    hid_ref[...] = (residual + projected).astype(BF16)

    slots = lax.broadcasted_iota(jnp.int32, (cap, tokens), 0).astype(F32)

    def rows_for(expert):
        wanted = hits_ref[pl.ds(expert, 1), :] > 0.5
        picks = jnp.where((slots == before_ref[pl.ds(expert, 1), :]) & wanted, 1.0, 0.0)
        return lax.dot_general(
            picks.astype(BF16),
            hid_ref[...],
            (((1,), (1,)), ((), ())),
            preferred_element_type=F32,
        ).astype(BF16)

    def routed(step):
        turn = turn_of(step, count)
        return pltpu.make_async_remote_copy(
            src_ref=sbuf.at[turn],
            dst_ref=rbuf.at[head, me],
            send_sem=send_sem.at[turn],
            recv_sem=recv_sem.at[me],
            device_id={"ctx": lax.rem(me + turn, count)},
            device_id_type=MESH,
        )

    def landed(source):
        return pltpu.make_async_remote_copy(
            src_ref=rbuf.at[head, source],
            dst_ref=rbuf.at[head, source],
            send_sem=send_sem.at[0],
            recv_sem=recv_sem.at[source],
            device_id={"head": others[0]},
            device_id_type=MESH,
        )

    def crossed(j, source):
        return pltpu.make_async_remote_copy(
            src_ref=rbuf.at[head, source],
            dst_ref=rbuf.at[head, source],
            send_sem=xsend_sem.at[j - 1, source],
            recv_sem=xrecv_sem.at[j - 1, source],
            device_id={"head": others[j - 1]},
            device_id_type=MESH,
        )

    def cross(source):
        for j in range(1, heads):
            crossed(j, source).start()

    def mirror(source):
        for j in range(1, heads):
            origin = lax.rem(head + heads - j, heads)
            pltpu.make_async_remote_copy(
                src_ref=rbuf.at[origin, source],
                dst_ref=rbuf.at[origin, source],
                send_sem=xsend_sem.at[j - 1, source],
                recv_sem=xrecv_sem.at[j - 1, source],
                device_id={"head": others[j - 1]},
                device_id_type=MESH,
            ).wait_recv()

    def dispatch(step, carry):
        turn = turn_of(step, count)
        sbuf[turn] = rows_for(lax.rem(me + turn, count))
        routed(step).start()
        return carry

    lax.fori_loop(0, count - 1, dispatch, 0)
    rbuf[head, me] = rows_for(me)
    cross(me)
    pltpu.make_async_copy(w_hbm, paired, w_sem).wait()

    def unpair(step, carry):
        rows = pl.ds(pl.multiple_of(step * 32, 32), 32)
        pair = jnp.swapaxes(paired[rows], 0, 1)
        w[rows, :width] = pair[0]
        w[rows, width:] = pair[1]
        return carry

    lax.fori_loop(0, w.shape[0] // 32, unpair, 0)

    def expert(source):
        squares = jnp.zeros((cap, 1), F32)
        parts = []
        for part in range(heads):
            rows = rbuf[part, source].astype(F32)
            squares = squares + jnp.sum(rows * rows, axis=1, keepdims=True)
            parts.append((rows * gain_ref[part : part + 1, :]).astype(BF16))
        inverse_rms = lax.rsqrt(squares / (heads * half) + 1e-05)

        def product(low):
            total = jnp.zeros((cap, width), F32)
            for part in range(heads):
                total = total + jnp.dot(
                    parts[part],
                    w[part * half : (part + 1) * half, low : low + width],
                    preferred_element_type=F32,
                )
            return total

        gate = product(0) * inverse_rms
        up = product(width) * inverse_rms
        act_ref[source] = (gate * jax.nn.sigmoid(1.702 * gate) * (up + 1.0)).astype(BF16)

    def receive(step, carry):
        source = lax.rem(me + count - turn_of(step, count), count)
        landed(source).wait_recv()
        cross(source)
        before = jnp.where(
            step == 0, me, lax.rem(me + count - turn_of(jnp.maximum(step - 1, 0), count), count)
        )
        mirror(before)
        expert(before)
        return carry

    lax.fori_loop(0, count - 1, receive, 0)
    last = lax.rem(me + count - turn_of(count - 2, count), count)
    mirror(last)
    expert(last)

    def drain(step, carry):
        routed(step).wait_send()
        for j in range(1, heads):
            crossed(j, lax.rem(me + step + 1, count)).wait_send()
        return carry

    lax.fori_loop(0, count - 1, drain, 0)
    for j in range(1, heads):
        crossed(j, me).wait_send()


def line_kernel(
    count,
    cap,
    reach,
    late,
    early,
    q_hbm,
    k_hbm,
    v_hbm,
    res_hbm,
    routes_ref,
    gain_ref,
    ow_hbm,
    w_hbm,
    hid_hbm,
    act_hbm,
    q_ref,
    kbuf,
    vbuf,
    res_ref,
    att_ref,
    ow,
    paired,
    w,
    gains,
    psend,
    precv,
    meta,
    zbuf,
    ysend,
    rows,
    cross,
    acc,
    sums,
    out,
    in_sem,
    ksend_sem,
    krecv_sem,
    ow_sem,
    w_sem,
    psend_sem,
    precv_sem,
    msend_sem,
    mrecv_sem,
    zsend_sem,
    zrecv_sem,
    ysend_sem,
    yrecv_sem,
    xsend_sem,
    xrecv_sem,
    hid_sem,
    out_sem,
):
    me = lax.axis_index("ctx")
    head = lax.axis_index("head")
    other = 1 - head
    length = count // 2
    place = me // 2
    side = lax.rem(me, 2)
    half, tokens = hid_hbm.shape
    width = act_hbm.shape[2]
    own_parts = late + early
    parts = own_parts + early
    piece = half // own_parts
    groups = lax.axis_size("grp")
    block = me * groups + lax.axis_index("grp")
    blocks = count * groups

    def at_block(index):
        return {"ctx": index // groups, "grp": lax.rem(index, groups)}

    def on_line(position):
        return {"ctx": position * 2 + side}

    partner = {"ctx": place * 2 + 1 - side}
    across = {"head": other}

    barrier = pltpu.get_barrier_semaphore()
    peers = [on_line(lax.rem(place + j, length)) for j in range(1, length)]
    peers += [partner, across]
    for j in range(1, reach + 1):
        peers += [at_block(lax.rem(block + j, blocks)), at_block(lax.rem(block + blocks - j, blocks))]
    for peer in peers:
        pl.semaphore_signal(barrier, inc=1, device_id=peer, device_id_type=MESH)

    def span(which, start, stop):
        return pl.ds(pl.multiple_of(which * half + start * piece, 16), (stop - start) * piece)

    mine = pl.ds(reach * tokens, tokens)
    own_spot = pl.ds(0, half)
    early_spot = pl.ds(half, early * piece)
    late_spot = pl.ds(parts * piece, late * piece)
    local = [
        pltpu.make_async_copy(k_hbm, kbuf.at[mine], in_sem.at[0]),
        pltpu.make_async_copy(v_hbm, vbuf.at[mine], in_sem.at[1]),
        pltpu.make_async_copy(q_hbm, q_ref, in_sem.at[2]),
    ]
    res_copies = [
        pltpu.make_async_copy(res_hbm.at[span(head, 0, own_parts)], res_ref.at[own_spot], in_sem.at[3]),
        pltpu.make_async_copy(
            res_hbm.at[span(other, late, own_parts)], res_ref.at[early_spot], in_sem.at[4]
        ),
    ]
    w_copies = [
        pltpu.make_async_copy(w_hbm.at[span(which, low, high)], paired.at[spot], w_sem.at[n])
        for n, (which, low, high, spot) in enumerate(
            (
                (head, 0, own_parts, own_spot),
                (other, late, own_parts, early_spot),
                (other, 0, late, late_spot),
            )
        )
    ]
    ow_copies = [
        pltpu.make_async_copy(ow_hbm.at[span(which, 0, own_parts)], ow.at[n], ow_sem.at[n])
        for n, which in enumerate((other, head))
    ]
    for copy in local + w_copies + ow_copies + res_copies:
        copy.start()

    def remote(source, target, send, recv, device):
        return pltpu.make_async_remote_copy(
            src_ref=source,
            dst_ref=target,
            send_sem=send,
            recv_sem=recv,
            device_id=device,
            device_id_type=MESH,
        )

    def window_copies(j):
        rows_at = pl.ds((reach - j) * tokens, tokens)
        target = at_block(lax.rem(block + j, blocks))
        return [
            remote(source, buffer.at[rows_at], ksend_sem.at[n, j - 1], krecv_sem.at[n, j - 1], target)
            for n, (source, buffer) in enumerate(((k_hbm, kbuf), (v_hbm, vbuf)))
        ]

    expert_ids = lax.broadcasted_iota(jnp.int32, (count, tokens), 0)
    hits = jnp.zeros((count, tokens), F32)
    for k in range(routes_ref.shape[0]):
        hits = hits + jnp.where(routes_ref[k : k + 1, :] == expert_ids, 1.0, 0.0)
    earlier = jnp.where(
        lax.broadcasted_iota(jnp.int32, (tokens, tokens), 0)
        < lax.broadcasted_iota(jnp.int32, (tokens, tokens), 1),
        1.0,
        0.0,
    ).astype(BF16)
    before = jnp.dot(hits.astype(BF16), earlier, preferred_element_type=F32)
    meta[place] = jnp.where(hits > 0.5, before, -1.0)

    gain = gain_ref[...].reshape(1, 2 * half)
    order = [(0, n) for n in range(own_parts)]
    order += [(1, n) for n in range(late, own_parts)] + [(1, n) for n in range(late)]
    for n, (far, index) in enumerate(order):
        left = gain[:, index * piece : (index + 1) * piece]
        right = gain[:, half + index * piece : half + (index + 1) * piece]
        gains[n : n + 1, :] = jnp.where(head == far, left, right)

    pl.semaphore_wait(barrier, len(peers))
    for j in range(1, reach + 1):

        @pl.when(block + j < blocks)
        def _(j=j):
            for copy in window_copies(j):
                copy.start()

    def meta_copy(j):
        return remote(
            meta.at[place],
            meta.at[place],
            msend_sem.at[j - 1],
            mrecv_sem.at[place],
            on_line(lax.rem(place + j, length)),
        )

    def meta_landed(j):
        source = lax.rem(place + length - j, length)
        return remote(
            meta.at[source], meta.at[source], msend_sem.at[j - 1], mrecv_sem.at[source], across
        )

    for j in range(1, length):
        meta_copy(j).start()

    for copy in w_copies:
        copy.wait()

    def unpair(step, carry):
        at = pl.ds(pl.multiple_of(step * 32, 32), 32)
        pair = jnp.swapaxes(paired[at], 0, 1)
        w[at, :width] = pair[0]
        w[at, width:] = pair[1]
        return carry

    lax.fori_loop(0, w.shape[0] // 32, unpair, 0)

    for j in range(1, reach + 1):

        @pl.when(block < j)
        def _(j=j):
            rows_at = pl.ds((reach - j) * tokens, tokens)
            kbuf[rows_at, :] = jnp.zeros((tokens, kbuf.shape[1]), BF16)
            vbuf[rows_at, :] = jnp.zeros((tokens, vbuf.shape[1]), BF16)

    for copy in local:
        copy.wait()
    for j in range(1, reach + 1):

        @pl.when(block >= j)
        def _(j=j):
            for copy in window_copies(j):
                copy.wait_recv()

    attend(block, reach, q_ref, kbuf, vbuf, att_ref)

    def part(index):
        return pl.ds(pl.multiple_of(index * piece, 16), piece)

    def project(slot, index):
        return lax.dot_general(
            ow[slot, part(index), :],
            att_ref[...],
            (((1,), (1,)), ((), ())),
            preferred_element_type=F32,
        ).astype(BF16)

    def exchange(index):
        return remote(
            psend.at[part(index)],
            precv.at[part(index)],
            psend_sem.at[index],
            precv_sem.at[index],
            across,
        )

    for copy in ow_copies:
        copy.wait()

    def offer(index, carry):
        far = index < own_parts
        psend[part(index), :] = project(
            jnp.where(far, 0, 1), jnp.where(far, index, index - early)
        )
        exchange(index).start()
        return carry

    lax.fori_loop(0, parts, offer, 0)

    def keep(index, carry):
        zbuf[place, part(index), :] = project(1, index)
        return carry

    lax.fori_loop(0, late, keep, 0)
    zbuf[place, late * piece : half, :] = psend[half:, :]
    zbuf[place, half:, :] = psend[late * piece : half, :]
    for copy in res_copies:
        copy.wait()

    def line_copy(owner, index, up):
        to = jnp.where(up == 1, place + 1, place - 1)
        spot = zbuf.at[owner, part(index)]
        return remote(
            spot, spot, zsend_sem.at[up, owner, index], zrecv_sem.at[owner, index], on_line(to)
        )

    def has_next(up):
        return jnp.where(up == 1, place + 1 < length, place > 0)

    def reduce(index):
        exchange(index).wait_recv()
        total = zbuf[place, part(index), :].astype(F32) + precv[part(index), :].astype(F32)
        zbuf[place, part(index), :] = (res_ref[part(index), :].astype(F32) + total).astype(BF16)
        for up in range(2):

            @pl.when(has_next(up))
            def _(up=up):
                line_copy(place, index, up).start()

    for j in range(1, length):
        meta_landed(j).wait_recv()

    slots = lax.broadcasted_iota(jnp.int32, (cap, tokens), 0).astype(F32)

    def y_copy(owner, index):
        return remote(
            ysend.at[owner, index],
            rows.at[owner, index, 1],
            ysend_sem.at[owner, index],
            yrecv_sem.at[owner, index],
            partner,
        )

    def x_copy(owner, index, which):
        return remote(
            rows.at[owner, index, which],
            cross.at[owner, index, which],
            xsend_sem.at[owner, index, which],
            xrecv_sem.at[owner, index, which],
            across,
        )

    def pick(owner, index):
        def picks(expert):
            wanted = meta[owner, pl.ds(expert, 1), :]
            return jnp.where(slots == wanted, 1.0, 0.0)

        both = jnp.concatenate([picks(place * 2 + 1 - side), picks(me)], 0).astype(BF16)
        found = lax.dot_general(
            both,
            zbuf[owner, part(index), :],
            (((1,), (1,)), ((), ())),
            preferred_element_type=F32,
        )
        ysend[owner, index] = found[:cap].astype(BF16)
        y_copy(owner, index).start()
        rows[owner, index, 0] = found[cap:].astype(BF16)

        @pl.when(index < late)
        def _():
            x_copy(owner, index, 0).start()

    def gather(buffer, owner, index, at, fresh):
        raw = buffer[owner, index].astype(F32).reshape(2 * cap, piece)
        squares = jnp.sum(raw * raw, axis=1, keepdims=True)
        left = (raw * gains[pl.ds(at, 1), :]).astype(BF16)
        sums[owner] = jnp.where(fresh, 0.0, sums[owner]) + squares
        for low in (0, width):
            product = jnp.dot(
                left, w[part(at), low : low + width], preferred_element_type=F32
            )
            held = acc[owner, :, low : low + width]
            acc[owner, :, low : low + width] = jnp.where(fresh, 0.0, held) + product

    def result(owner, which):
        source = owner * 2 + jnp.where(which == 0, side, 1 - side)
        return pltpu.make_async_copy(out.at[owner, which], act_hbm.at[source], out_sem.at[owner, which])

    def owner_of(step, up):
        return jnp.where(up == 1, place + step, place - step)

    def exists(step, up):
        owner = owner_of(step, up)
        return (owner >= 0) & (owner < length) & (step + 1 - up > 0)

    def each(step, action):
        def one(up, carry):
            @pl.when(exists(step, up))
            def _():
                action(owner_of(step, up), up)

            return carry

        lax.fori_loop(0, 2, one, 0)

    def meet(owner, index):
        y_copy(owner, index).wait_recv()

        @pl.when(index < late)
        def _():
            x_copy(owner, index, 1).start()

        gather(rows, owner, index, index, index == 0)

    def finish(owner):
        def add(index, carry):
            for which in range(2):
                x_copy(owner, index, which).wait_recv()
            gather(cross, owner, index, parts + index, False)
            return carry

        lax.fori_loop(0, late, add, 0)
        inverse_rms = lax.rsqrt(sums[owner][:, :1] / (2 * half) + 1e-05)
        gate = acc[owner, :, :width] * inverse_rms
        up = acc[owner, :, width:] * inverse_rms
        active = gate * jax.nn.sigmoid(1.702 * gate) * (up + 1.0)
        out[owner] = active.reshape(2, cap, width).astype(BF16)
        for which in range(2):
            result(owner, which).start()

    hid_copy = pltpu.make_async_copy(zbuf.at[place, own_spot], hid_hbm, hid_sem)

    turns = length * parts + 2

    def advance(turn, carry):
        step, index = turn // parts, lax.rem(turn, parts)

        @pl.when(step == 0)
        def _():
            reduce(index)

        @pl.when((step > 0) & (step < length))
        def _():
            def arrive(owner, up):
                line_copy(owner, index, 1 - up).wait_recv()

                @pl.when(has_next(1 - up))
                def _():
                    line_copy(owner, index, 1 - up).start()

            each(step, arrive)

        each(step, lambda owner, up: pick(owner, index))

        @pl.when(turn == parts)
        def _():
            hid_copy.start()

        @pl.when(turn >= 2)
        def _():
            last = turn - 2
            each(last // parts, lambda owner, up: meet(owner, lax.rem(last, parts)))

        done = jnp.where(step < length, index == parts - 1, turn == turns - 1)

        @pl.when((step > 0) & done)
        def _():
            each(jnp.minimum(step, length) - 1, lambda owner, up: finish(owner))

        return carry

    lax.fori_loop(0, turns, advance, 0)

    def drain(owner, carry):
        def settle(index, carry):
            y_copy(owner, index).wait_send()
            for up in range(2):
                came = jnp.where(up == 1, owner <= place, owner >= place)

                @pl.when(has_next(up) & came)
                def _(up=up):
                    line_copy(owner, index, up).wait_send()

            @pl.when(index < late)
            def _():
                for which in range(2):
                    x_copy(owner, index, which).wait_send()

            return carry

        lax.fori_loop(0, parts, settle, 0)
        for which in range(2):
            result(owner, which).wait()
        return carry

    lax.fori_loop(0, length, drain, 0)
    hid_copy.wait()
    for j in range(1, length):
        meta_copy(j).wait_send()

    def settle_exchange(index, carry):
        exchange(index).wait_send()
        return carry

    lax.fori_loop(0, parts, settle_exchange, 0)
    for j in range(1, reach + 1):

        @pl.when(block + j < blocks)
        def _(j=j):
            for copy in window_copies(j):
                copy.wait_send()


def place_kernel(hid_in, act_in, hid_out, act_out, hid, act, in_sem, out_sem):
    pieces = act_in.shape[0]
    parts = max(n for n in range(1, pieces + 1) if hid_in.shape[0] % (16 * n) == 0)
    size = hid_in.shape[0] // parts
    spots = [(hid_in, hid, hid_out, pl.ds(n * size, size)) for n in range(parts)]
    spots += [(act_in, act, act_out, n) for n in range(pieces)]
    loads = [
        pltpu.make_async_copy(source.at[at], held.at[at], in_sem.at[n])
        for n, (source, held, _, at) in enumerate(spots)
    ]
    stores = [
        pltpu.make_async_copy(held.at[at], target.at[at], out_sem.at[n])
        for n, (_, held, target, at) in enumerate(spots)
    ]
    for copy in loads:
        copy.start()
    for load, store in zip(loads, stores):
        load.wait()
        store.start()
    for copy in stores:
        copy.wait()


def placed(hidden, active):
    in_hbm = pl.BlockSpec(memory_space=pl.ANY)
    pieces = active.shape[0]
    return pl.pallas_call(
        place_kernel,
        out_shape=(
            jax.ShapeDtypeStruct(hidden.shape, hidden.dtype),
            jax.ShapeDtypeStruct(active.shape, active.dtype),
        ),
        in_specs=[in_hbm] * 2,
        out_specs=(in_hbm, in_hbm),
        scratch_shapes=[
            pltpu.VMEM(hidden.shape, hidden.dtype),
            pltpu.VMEM(active.shape, active.dtype),
            pltpu.SemaphoreType.DMA((2 * pieces,)),
            pltpu.SemaphoreType.DMA((2 * pieces,)),
        ],
    )(hidden, active)


def along_line(
    count, cap, reach, queries, keys, values, residual, routes, norm_gain, out_weight, expert_weight
):
    tokens = queries.shape[0]
    width_all = residual.shape[1]
    half = width_all // 2
    length = count // 2
    width = expert_weight.shape[3]
    pieces = max(n for n in range(1, 3 + 1) if half % (16 * n) == 0)
    early = min(1, pieces - 1)
    late = pieces - early
    parts = pieces + early
    piece = half // pieces
    in_vmem = pl.BlockSpec(memory_space=pltpu.VMEM)
    in_hbm = pl.BlockSpec(memory_space=pl.ANY)
    dma = pltpu.SemaphoreType.DMA
    return pl.pallas_call(
        functools.partial(line_kernel, count, cap, reach, late, early),
        out_shape=(
            jax.ShapeDtypeStruct((half, tokens), BF16),
            jax.ShapeDtypeStruct((count, cap, width), BF16),
        ),
        in_specs=[in_hbm] * 4 + [in_vmem] * 2 + [in_hbm] * 2,
        out_specs=(in_hbm, in_hbm),
        scratch_shapes=[
            pltpu.VMEM(queries.shape, BF16),
            pltpu.VMEM(((reach + 1) * tokens, keys.shape[1]), BF16),
            pltpu.VMEM(((reach + 1) * tokens, values.shape[1]), BF16),
            pltpu.VMEM((parts * piece, tokens), BF16),
            pltpu.VMEM(queries.shape, BF16),
            pltpu.VMEM((2, half, out_weight.shape[0]), BF16),
            pltpu.VMEM((width_all, 2, width), BF16),
            pltpu.VMEM((width_all, 2 * width), BF16),
            pltpu.VMEM((2 * pieces, piece), F32),
            pltpu.VMEM((parts * piece, tokens), BF16),
            pltpu.VMEM((parts * piece, tokens), BF16),
            pltpu.VMEM((length, count, tokens), F32),
            pltpu.VMEM((length, parts * piece, tokens), BF16),
            pltpu.VMEM((length, parts, cap, piece), BF16),
            pltpu.VMEM((length, parts, 2, cap, piece), BF16),
            pltpu.VMEM((length, late, 2, cap, piece), BF16),
            pltpu.VMEM((length, 2 * cap, 2 * width), F32),
            pltpu.VMEM((length, 2 * cap, 128), F32),
            pltpu.VMEM((length, 2, cap, width), BF16),
            dma((5,)),
            dma((2, reach)),
            dma((2, reach)),
            dma((2,)),
            dma((3,)),
            dma((parts,)),
            dma((parts,)),
            dma((length - 1,)),
            dma((length,)),
            dma((2, length, parts)),
            dma((length, parts)),
            dma((length, parts)),
            dma((length, parts)),
            dma((length, late, 2)),
            dma((length, late, 2)),
            dma,
            dma((length, 2)),
        ],
        compiler_params=pltpu.CompilerParams(
            collective_id=1, has_side_effects=True, vmem_limit_bytes=60 * 1024 * 1024
        ),
    )(
        queries,
        keys,
        values,
        residual.T,
        routes.T,
        norm_gain,
        out_weight.T,
        expert_weight[0],
    )


def body(residual, queries, keys, values, out_weight, norm_gain, routes, expert_weight):
    tokens_here = queries.shape[0]
    heads_count = lax.axis_size("head")
    reach = max(1, lax.axis_size("ctx") // 16) * lax.axis_size("grp")
    width_all = residual.shape[1]
    half = width_all // heads_count
    count = lax.axis_size("ctx")
    experts_all = expert_weight.shape[0] * count
    routed = tokens_here * TOP
    cap = min(tokens_here, routed // experts_all + max(1, routed // (8 * experts_all)))
    hidden_width = expert_weight.shape[3]
    if heads_count == 2 and count % 2 == 0 and experts_all == count and 2 * cap >= tokens_here:
        hidden, active = along_line(
            count,
            cap,
            reach,
            queries,
            keys,
            values,
            residual,
            routes,
            norm_gain,
            out_weight,
            expert_weight,
        )
        hidden, active = placed(hidden, active)
        return (hidden.T, active.reshape(1, 1, count * cap, hidden_width))
    in_vmem = pl.BlockSpec(memory_space=pltpu.VMEM)
    in_hbm = pl.BlockSpec(memory_space=pl.ANY)
    hidden, active = pl.pallas_call(
        functools.partial(layer_kernel, count, cap, reach),
        out_shape=(
            jax.ShapeDtypeStruct((half, tokens_here), BF16),
            jax.ShapeDtypeStruct((count, cap, hidden_width), BF16),
        ),
        in_specs=[in_vmem] * 6 + [in_hbm] * 2,
        out_specs=(in_vmem, in_vmem),
        scratch_shapes=[
            pltpu.VMEM(((reach + 1) * tokens_here, keys.shape[1]), BF16),
            pltpu.VMEM(((reach + 1) * tokens_here, values.shape[1]), BF16),
            pltpu.VMEM(queries.shape, BF16),
            pltpu.VMEM((heads_count, half, out_weight.shape[0]), BF16),
            pltpu.VMEM((width_all, 2, hidden_width), BF16),
            pltpu.VMEM((width_all, 2 * hidden_width), BF16),
            pltpu.VMEM((heads_count - 1, half, tokens_here), BF16),
            pltpu.VMEM((heads_count - 1, half, tokens_here), BF16),
            pltpu.VMEM((count, tokens_here), F32),
            pltpu.VMEM((count, tokens_here), F32),
            pltpu.VMEM((count, cap, half), BF16),
            pltpu.VMEM((heads_count, count, cap, half), BF16),
            pltpu.SemaphoreType.DMA((2, reach)),
            pltpu.SemaphoreType.DMA((2, reach)),
            pltpu.SemaphoreType.DMA((heads_count,)),
            pltpu.SemaphoreType.DMA,
            pltpu.SemaphoreType.DMA((heads_count - 1,)),
            pltpu.SemaphoreType.DMA((heads_count - 1,)),
            pltpu.SemaphoreType.DMA((count,)),
            pltpu.SemaphoreType.DMA((count,)),
            pltpu.SemaphoreType.DMA((heads_count - 1, count)),
            pltpu.SemaphoreType.DMA((heads_count - 1, count)),
        ],
        compiler_params=pltpu.CompilerParams(
            collective_id=0, has_side_effects=True, vmem_limit_bytes=60 * 1024 * 1024
        ),
    )(
        queries,
        keys,
        values,
        residual.T,
        routes.T,
        norm_gain.reshape(heads_count, half),
        out_weight.T,
        expert_weight[0],
    )
    return (hidden.T, active.reshape(1, 1, count * cap, hidden_width))


def solution(mesh):
    in_specs = (
        P(("ctx", "grp"), None),
        P(("ctx", "grp"), "head"),
        P(("ctx", "grp"), "head"),
        P(("ctx", "grp"), "head"),
        P("head", None),
        P(),
        P(("ctx", "grp"), None),
        P("ctx", None, None, "head"),
    )
    out_specs = (P(("ctx", "grp"), "head"), P("ctx", "grp", None, "head"))
    return jax.shard_map(body, mesh=mesh, in_specs=in_specs, out_specs=out_specs, check_vma=False)
```

```python
import functools
import jax
import jax.numpy as jnp
from jax import lax
from jax.experimental import pallas as pl
from jax.experimental.pallas import tpu as pltpu
from jax.sharding import PartitionSpec as P

D = 2880
HD = 64
TOP = 4


MESH = pl.DeviceIdType.MESH
F32 = jnp.float32
BF16 = jnp.bfloat16


def turn_of(step, count):
    return 1 + lax.rem(step + count // 2 - 1, count - 1)


def in_pair(values, group, lanes):
    zeros = jnp.zeros((values.shape[0], HD), values.dtype)
    if values.shape[1] == HD:
        return jnp.concatenate([values, zeros], 1), jnp.concatenate([zeros, values], 1)
    first = group % 2 == 0
    base = group // 2 * 2 * HD
    pair = values[:, base : base + 2 * HD]
    swapped = jnp.concatenate([pair[:, HD:], pair[:, :HD]], 1)
    low = jnp.where(lanes < HD, pair if first else swapped, jnp.zeros_like(pair))
    high = jnp.where(lanes >= HD, swapped if first else pair, jnp.zeros_like(pair))
    return low, high


def attend(block, reach, q_ref, kbuf, vbuf, att_ref):
    tokens = q_ref.shape[0]
    window = kbuf.shape[0]
    kv_local = kbuf.shape[1] // HD
    pairs = q_ref.shape[1] // (2 * HD * kv_local)
    rows = pairs * tokens
    place = lax.rem(lax.broadcasted_iota(jnp.int32, (rows, window), 0), tokens)
    column = lax.broadcasted_iota(jnp.int32, (rows, window), 1)
    ahead = place + reach * tokens - column
    allowed = (ahead >= 0) & (ahead < reach * tokens) & (column >= (reach - block) * tokens)
    lanes = lax.broadcasted_iota(jnp.int32, (window, 2 * HD), 1)
    left = lax.broadcasted_iota(jnp.int32, (rows, 2 * HD), 1) < HD
    for group in range(kv_local):
        key_pair = in_pair(kbuf[...], group, lanes)
        value_pair = in_pair(vbuf[...], group, lanes)
        first = group * pairs
        queries = jnp.concatenate(
            [
                q_ref[:, (first + p) * 2 * HD : (first + p + 1) * 2 * HD]
                for p in range(pairs)
            ],
            0,
        )
        mixed = jnp.zeros((rows, 2 * HD), F32)
        totals = []
        for side in range(2):
            scores = lax.dot_general(
                queries,
                key_pair[side],
                (((1,), (1,)), ((), ())),
                preferred_element_type=F32,
            )
            scores = jnp.where(allowed, scores * HD ** (-0.5), -1e30)
            row_max = jnp.max(scores, axis=1, keepdims=True)
            weights = jnp.where(allowed, jnp.exp(scores - row_max), 0.0)
            totals.append(jnp.sum(weights, axis=1, keepdims=True))
            mixed = mixed + jnp.dot(
                weights.astype(BF16), value_pair[side], preferred_element_type=F32
            )
        attended = (mixed / jnp.where(left, totals[0], totals[1])).astype(BF16)
        for p in range(pairs):
            att_ref[:, (first + p) * 2 * HD : (first + p + 1) * 2 * HD] = attended[
                p * tokens : (p + 1) * tokens
            ]


def layer_kernel(
    count,
    cap,
    reach,
    q_ref,
    k_ref,
    v_ref,
    res_ref,
    routes_ref,
    gain_ref,
    ow_hbm,
    w_hbm,
    hid_ref,
    act_ref,
    kbuf,
    vbuf,
    att_ref,
    ow,
    paired,
    w,
    psend,
    precv,
    hits_ref,
    before_ref,
    sbuf,
    rbuf,
    ksend_sem,
    krecv_sem,
    ow_sem,
    w_sem,
    psend_sem,
    precv_sem,
    send_sem,
    recv_sem,
    xsend_sem,
    xrecv_sem,
):
    me = lax.axis_index("ctx")
    head = lax.axis_index("head")
    heads = rbuf.shape[0]
    others = [lax.rem(head + j, heads) for j in range(1, heads)]
    half, tokens = hid_ref.shape
    width = act_ref.shape[2]

    def ow_copy(which, slot):
        rows = pl.ds(pl.multiple_of(which * half, 16), half)
        return pltpu.make_async_copy(ow_hbm.at[rows], ow.at[slot], ow_sem.at[slot])

    for j in range(1, heads):
        ow_copy(others[j - 1], j).start()
    ow_copy(head, 0).start()
    pltpu.make_async_copy(w_hbm, paired, w_sem).start()

    barrier = pltpu.get_barrier_semaphore()
    for other in others:
        pl.semaphore_signal(barrier, inc=1, device_id={"head": other}, device_id_type=MESH)

    def greet(step, carry):
        peer = lax.rem(me + step, count)
        pl.semaphore_signal(barrier, inc=1, device_id={"ctx": peer}, device_id_type=MESH)
        return carry

    lax.fori_loop(1, count, greet, 0)

    groups = lax.axis_size("grp")
    block = me * groups + lax.axis_index("grp")
    blocks = count * groups

    def at_block(index):
        return {"ctx": index // groups, "grp": lax.rem(index, groups)}

    for j in range(1, reach + 1):
        for peer in (lax.rem(block + j, blocks), lax.rem(block + blocks - j, blocks)):
            pl.semaphore_signal(barrier, inc=1, device_id=at_block(peer), device_id_type=MESH)

    def window_copies(j):
        place = pl.ds((reach - j) * tokens, tokens)
        target = at_block(lax.rem(block + j, blocks))
        return [
            pltpu.make_async_remote_copy(
                src_ref=source,
                dst_ref=buffer.at[place],
                send_sem=ksend_sem.at[n, j - 1],
                recv_sem=krecv_sem.at[n, j - 1],
                device_id=target,
                device_id_type=MESH,
            )
            for n, (source, buffer) in enumerate(((k_ref, kbuf), (v_ref, vbuf)))
        ]

    pl.semaphore_wait(barrier, count - 1 + heads - 1 + 2 * reach)
    for j in range(1, reach + 1):

        @pl.when(block + j < blocks)
        def _(j=j):
            for copy in window_copies(j):
                copy.start()

    kbuf[reach * tokens :, :] = k_ref[...]
    vbuf[reach * tokens :, :] = v_ref[...]

    def project(slot):
        return lax.dot_general(
            ow[slot], att_ref[...], (((1,), (1,)), ((), ())), preferred_element_type=F32
        ).astype(BF16)

    def exchange(j):
        return pltpu.make_async_remote_copy(
            src_ref=psend.at[j - 1],
            dst_ref=precv.at[j - 1],
            send_sem=psend_sem.at[j - 1],
            recv_sem=precv_sem.at[j - 1],
            device_id={"head": others[j - 1]},
            device_id_type=MESH,
        )

    for j in range(1, reach + 1):

        @pl.when(block >= j)
        def _(j=j):
            for copy in window_copies(j):
                copy.wait_recv()

        @pl.when(block < j)
        def _(j=j):
            place = pl.ds((reach - j) * tokens, tokens)
            kbuf[place, :] = jnp.zeros((tokens, kbuf.shape[1]), BF16)
            vbuf[place, :] = jnp.zeros((tokens, vbuf.shape[1]), BF16)

        @pl.when(block + j < blocks)
        def _(j=j):
            for copy in window_copies(j):
                copy.wait_send()

    attend(block, reach, q_ref, kbuf, vbuf, att_ref)

    for j in range(1, heads):
        ow_copy(others[j - 1], j).wait()
        psend[j - 1] = project(j)
        exchange(j).start()
    ow_copy(head, 0).wait()
    projected = project(0).astype(F32)

    expert_ids = lax.broadcasted_iota(jnp.int32, (count, tokens), 0)
    hits = jnp.zeros((count, tokens), F32)
    for k in range(routes_ref.shape[0]):
        hits = hits + jnp.where(routes_ref[k : k + 1, :] == expert_ids, 1.0, 0.0)
    earlier = jnp.where(
        lax.broadcasted_iota(jnp.int32, (tokens, tokens), 0)
        < lax.broadcasted_iota(jnp.int32, (tokens, tokens), 1),
        1.0,
        0.0,
    ).astype(BF16)
    hits_ref[...] = hits
    before_ref[...] = jnp.dot(hits.astype(BF16), earlier, preferred_element_type=F32)
    residual = res_ref[pl.ds(pl.multiple_of(head * half, 16), half), :].astype(F32)

    for j in range(1, heads):
        exchange(j).wait()
        projected = projected + precv[j - 1].astype(F32)
    hid_ref[...] = (residual + projected).astype(BF16)

    slots = lax.broadcasted_iota(jnp.int32, (cap, tokens), 0).astype(F32)

    def rows_for(expert):
        wanted = hits_ref[pl.ds(expert, 1), :] > 0.5
        picks = jnp.where((slots == before_ref[pl.ds(expert, 1), :]) & wanted, 1.0, 0.0)
        return lax.dot_general(
            picks.astype(BF16),
            hid_ref[...],
            (((1,), (1,)), ((), ())),
            preferred_element_type=F32,
        ).astype(BF16)

    def routed(step):
        turn = turn_of(step, count)
        return pltpu.make_async_remote_copy(
            src_ref=sbuf.at[turn],
            dst_ref=rbuf.at[head, me],
            send_sem=send_sem.at[turn],
            recv_sem=recv_sem.at[me],
            device_id={"ctx": lax.rem(me + turn, count)},
            device_id_type=MESH,
        )

    def landed(source):
        return pltpu.make_async_remote_copy(
            src_ref=rbuf.at[head, source],
            dst_ref=rbuf.at[head, source],
            send_sem=send_sem.at[0],
            recv_sem=recv_sem.at[source],
            device_id={"head": others[0]},
            device_id_type=MESH,
        )

    def crossed(j, source):
        return pltpu.make_async_remote_copy(
            src_ref=rbuf.at[head, source],
            dst_ref=rbuf.at[head, source],
            send_sem=xsend_sem.at[j - 1, source],
            recv_sem=xrecv_sem.at[j - 1, source],
            device_id={"head": others[j - 1]},
            device_id_type=MESH,
        )

    def cross(source):
        for j in range(1, heads):
            crossed(j, source).start()

    def mirror(source):
        for j in range(1, heads):
            origin = lax.rem(head + heads - j, heads)
            pltpu.make_async_remote_copy(
                src_ref=rbuf.at[origin, source],
                dst_ref=rbuf.at[origin, source],
                send_sem=xsend_sem.at[j - 1, source],
                recv_sem=xrecv_sem.at[j - 1, source],
                device_id={"head": others[j - 1]},
                device_id_type=MESH,
            ).wait_recv()

    def dispatch(step, carry):
        turn = turn_of(step, count)
        sbuf[turn] = rows_for(lax.rem(me + turn, count))
        routed(step).start()
        return carry

    lax.fori_loop(0, count - 1, dispatch, 0)
    rbuf[head, me] = rows_for(me)
    cross(me)
    pltpu.make_async_copy(w_hbm, paired, w_sem).wait()

    def unpair(step, carry):
        rows = pl.ds(pl.multiple_of(step * 32, 32), 32)
        pair = jnp.swapaxes(paired[rows], 0, 1)
        w[rows, :width] = pair[0]
        w[rows, width:] = pair[1]
        return carry

    lax.fori_loop(0, w.shape[0] // 32, unpair, 0)

    def expert(source):
        squares = jnp.zeros((cap, 1), F32)
        parts = []
        for part in range(heads):
            rows = rbuf[part, source].astype(F32)
            squares = squares + jnp.sum(rows * rows, axis=1, keepdims=True)
            parts.append((rows * gain_ref[part : part + 1, :]).astype(BF16))
        inverse_rms = lax.rsqrt(squares / (heads * half) + 1e-05)

        def product(low):
            total = jnp.zeros((cap, width), F32)
            for part in range(heads):
                total = total + jnp.dot(
                    parts[part],
                    w[part * half : (part + 1) * half, low : low + width],
                    preferred_element_type=F32,
                )
            return total

        gate = product(0) * inverse_rms
        up = product(width) * inverse_rms
        act_ref[source] = (gate * jax.nn.sigmoid(1.702 * gate) * (up + 1.0)).astype(BF16)

    def receive(step, carry):
        source = lax.rem(me + count - turn_of(step, count), count)
        landed(source).wait_recv()
        cross(source)
        before = jnp.where(
            step == 0, me, lax.rem(me + count - turn_of(jnp.maximum(step - 1, 0), count), count)
        )
        mirror(before)
        expert(before)
        return carry

    lax.fori_loop(0, count - 1, receive, 0)
    last = lax.rem(me + count - turn_of(count - 2, count), count)
    mirror(last)
    expert(last)

    def drain(step, carry):
        routed(step).wait_send()
        for j in range(1, heads):
            crossed(j, lax.rem(me + step + 1, count)).wait_send()
        return carry

    lax.fori_loop(0, count - 1, drain, 0)
    for j in range(1, heads):
        crossed(j, me).wait_send()


def line_kernel(
    count,
    cap,
    reach,
    late,
    q_hbm,
    k_hbm,
    v_hbm,
    res_hbm,
    routes_ref,
    gain_ref,
    ow_hbm,
    w_hbm,
    hid_hbm,
    act_hbm,
    q_ref,
    kbuf,
    vbuf,
    res_ref,
    att_ref,
    ow,
    paired,
    w,
    gains,
    psend,
    precv,
    meta,
    zbuf,
    ysend,
    rows,
    cross,
    acc,
    sums,
    out,
    in_sem,
    ksend_sem,
    krecv_sem,
    ow_sem,
    w_sem,
    psend_sem,
    precv_sem,
    msend_sem,
    mrecv_sem,
    zsend_sem,
    zrecv_sem,
    ysend_sem,
    yrecv_sem,
    xsend_sem,
    xrecv_sem,
    hid_sem,
    out_sem,
):
    me = lax.axis_index("ctx")
    head = lax.axis_index("head")
    other = 1 - head
    length = count // 2
    place = me // 2
    side = lax.rem(me, 2)
    half, tokens = hid_hbm.shape
    width = act_hbm.shape[2]
    parts = late + 2
    piece = rows.shape[4]
    rest = half - late * piece
    groups = lax.axis_size("grp")
    block = me * groups + lax.axis_index("grp")
    blocks = count * groups

    def at_block(index):
        return {"ctx": index // groups, "grp": lax.rem(index, groups)}

    def on_line(position):
        return {"ctx": position * 2 + side}

    partner = {"ctx": place * 2 + 1 - side}
    across = {"head": other}

    barrier = pltpu.get_barrier_semaphore()
    expected = 2
    for peer in (partner, across):
        pl.semaphore_signal(barrier, inc=1, device_id=peer, device_id_type=MESH)

    def greet(there, peer):
        @pl.when(there)
        def _():
            pl.semaphore_signal(barrier, inc=1, device_id=peer, device_id_type=MESH)

        return jnp.where(there, 1, 0)

    expected = expected + greet(place > 0, on_line(place - 1))
    expected = expected + greet(place + 1 < length, on_line(place + 1))
    for j in range(1, reach + 1):
        expected = expected + greet(block + j < blocks, at_block(block + j))
        expected = expected + greet(block >= j, at_block(block - j))

    def span(which, start, size):
        return pl.ds(pl.multiple_of(which * half + start, 16), size)

    late_size = late * piece
    far_start = (late + 1) * piece
    mine = pl.ds(reach * tokens, tokens)
    own_spot = pl.ds(0, half)
    early_spot = pl.ds(far_start, rest)
    late_spot = pl.ds(parts * piece, late_size)
    local = [
        pltpu.make_async_copy(k_hbm, kbuf.at[mine], in_sem.at[0]),
        pltpu.make_async_copy(v_hbm, vbuf.at[mine], in_sem.at[1]),
        pltpu.make_async_copy(q_hbm, q_ref, in_sem.at[2]),
    ]
    res_copies = [
        pltpu.make_async_copy(res_hbm.at[span(head, 0, half)], res_ref.at[own_spot], in_sem.at[3]),
        pltpu.make_async_copy(
            res_hbm.at[span(other, late_size, rest)], res_ref.at[early_spot], in_sem.at[4]
        ),
    ]
    w_copies = [
        pltpu.make_async_copy(w_hbm.at[span(which, start, size)], paired.at[spot], w_sem.at[n])
        for n, (which, start, size, spot) in enumerate(
            (
                (head, 0, half, own_spot),
                (other, late_size, rest, early_spot),
                (other, 0, late_size, late_spot),
            )
        )
    ]
    ow_copies = [
        pltpu.make_async_copy(ow_hbm.at[span(which, 0, half)], ow.at[n], ow_sem.at[n])
        for n, which in enumerate((other, head))
    ]
    for copy in local + w_copies + ow_copies + res_copies:
        copy.start()

    def remote(source, target, send, recv, device):
        return pltpu.make_async_remote_copy(
            src_ref=source,
            dst_ref=target,
            send_sem=send,
            recv_sem=recv,
            device_id=device,
            device_id_type=MESH,
        )

    def window_copies(j):
        rows_at = pl.ds((reach - j) * tokens, tokens)
        target = at_block(block + j)
        return [
            remote(source, buffer.at[rows_at], ksend_sem.at[n, j - 1], krecv_sem.at[n, j - 1], target)
            for n, (source, buffer) in enumerate(((k_hbm, kbuf), (v_hbm, vbuf)))
        ]

    expert_ids = lax.broadcasted_iota(jnp.int32, (count, tokens), 0)
    hits = jnp.zeros((count, tokens), F32)
    for k in range(routes_ref.shape[0]):
        hits = hits + jnp.where(routes_ref[k : k + 1, :] == expert_ids, 1.0, 0.0)
    earlier = jnp.where(
        lax.broadcasted_iota(jnp.int32, (tokens, tokens), 0)
        < lax.broadcasted_iota(jnp.int32, (tokens, tokens), 1),
        1.0,
        0.0,
    ).astype(BF16)
    before = jnp.dot(hits.astype(BF16), earlier, preferred_element_type=F32)
    meta[place] = jnp.where(hits > 0.5, before, -1.0)

    gain = gain_ref[...].reshape(1, 2 * half)
    gains[...] = jnp.zeros(gains.shape, F32)
    order = [(0, n) for n in range(late + 1)] + [(1, late)] + [(1, n) for n in range(late)]
    for n, (far, index) in enumerate(order):
        size = piece if index < late else rest
        left = gain[:, index * piece : index * piece + size]
        right = gain[:, half + index * piece : half + index * piece + size]
        gains[n : n + 1, :size] = jnp.where(head == far, left, right)
    if rest < piece:
        blank = piece - rest
        for start in (half, far_start + rest):
            zbuf[:, start : start + blank, :] = jnp.zeros((length, blank, tokens), BF16)

    pl.semaphore_wait(barrier, expected)
    for j in range(1, reach + 1):

        @pl.when(block + j < blocks)
        def _(j=j):
            for copy in window_copies(j):
                copy.start()

    def meta_copy(owner, up):
        to = jnp.where(up == 1, place + 1, place - 1)
        spot = meta.at[owner]
        return remote(spot, spot, msend_sem.at[up, owner], mrecv_sem.at[owner], on_line(to))

    def has_next(up):
        return jnp.where(up == 1, place + 1 < length, place > 0)

    for up in range(2):

        @pl.when(has_next(up))
        def _(up=up):
            meta_copy(place, up).start()

    for copy in w_copies:
        copy.wait()

    def unpair(step, carry):
        at = pl.ds(pl.multiple_of(step * 32, 32), 32)
        pair = jnp.swapaxes(paired[at], 0, 1)
        w[at, :width] = pair[0]
        w[at, width:] = pair[1]
        return carry

    lax.fori_loop(0, w.shape[0] // 32, unpair, 0)
    if rest < piece:
        for start in (half, far_start + rest):
            w[start : start + blank, :] = jnp.zeros((blank, 2 * width), BF16)

    for j in range(1, reach + 1):

        @pl.when(block < j)
        def _(j=j):
            rows_at = pl.ds((reach - j) * tokens, tokens)
            kbuf[rows_at, :] = jnp.zeros((tokens, kbuf.shape[1]), BF16)
            vbuf[rows_at, :] = jnp.zeros((tokens, vbuf.shape[1]), BF16)

    for copy in local:
        copy.wait()
    for j in range(1, reach + 1):

        @pl.when(block >= j)
        def _(j=j):
            for copy in window_copies(j):
                copy.wait_recv()

    attend(block, reach, q_ref, kbuf, vbuf, att_ref)

    def part(index, size=piece):
        return pl.ds(pl.multiple_of(index * piece, 16), size)

    def sized(index, action):
        @pl.when(index < late)
        def _():
            action(piece)

        @pl.when(index >= late)
        def _():
            action(rest)

    def project(slot, index, size):
        return lax.dot_general(
            ow[slot, part(index, size), :],
            att_ref[...],
            (((1,), (1,)), ((), ())),
            preferred_element_type=F32,
        ).astype(BF16)

    def exchange(index, size):
        return remote(
            psend.at[part(index, size)],
            precv.at[part(index, size)],
            psend_sem,
            precv_sem.at[index],
            across,
        )

    for copy in ow_copies:
        copy.wait()

    def offer(index, carry):
        psend[part(index), :] = project(0, index, piece)
        exchange(index, piece).start()
        return carry

    lax.fori_loop(0, late, offer, 0)
    for n in range(2):
        psend[part(late + n, rest), :] = project(n, late, rest)
        exchange(late + n, rest).start()

    def keep(index, carry):
        zbuf[place, part(index), :] = project(1, index, piece)
        return carry

    lax.fori_loop(0, late, keep, 0)
    zbuf[place, part(late, rest), :] = psend[part(late + 1, rest), :]
    zbuf[place, part(late + 1, rest), :] = psend[part(late, rest), :]
    for copy in res_copies:
        copy.wait()

    def line_copy(owner, index, up, size):
        to = jnp.where(up == 1, place + 1, place - 1)
        spot = zbuf.at[owner, part(index, size)]
        return remote(
            spot, spot, zsend_sem.at[up, owner], zrecv_sem.at[owner, index], on_line(to)
        )

    def reduce(index, size):
        at = part(index, size)
        exchange(index, size).wait_recv()
        total = zbuf[place, at, :].astype(F32) + precv[at, :].astype(F32)
        zbuf[place, at, :] = (res_ref[at, :].astype(F32) + total).astype(BF16)
        for up in range(2):

            @pl.when(has_next(up))
            def _(up=up):
                line_copy(place, index, up, size).start()

    slots = lax.broadcasted_iota(jnp.int32, (cap, tokens), 0).astype(F32)

    def y_copy(owner, index):
        return remote(
            ysend.at[owner, index],
            rows.at[owner, index, 1],
            ysend_sem,
            yrecv_sem.at[owner, index],
            partner,
        )

    def x_copy(owner, index, which):
        return remote(
            rows.at[owner, index, which],
            cross.at[owner, index, which],
            xsend_sem,
            xrecv_sem.at[owner, index, which],
            across,
        )

    def pick(owner, index):
        def picks(expert):
            wanted = meta[owner, pl.ds(expert, 1), :]
            return jnp.where(slots == wanted, 1.0, 0.0)

        both = jnp.concatenate([picks(place * 2 + 1 - side), picks(me)], 0).astype(BF16)
        found = lax.dot_general(
            both,
            zbuf[owner, part(index), :],
            (((1,), (1,)), ((), ())),
            preferred_element_type=F32,
        )
        ysend[owner, index] = found[:cap].astype(BF16)
        y_copy(owner, index).start()
        rows[owner, index, 0] = found[cap:].astype(BF16)

        @pl.when(index < late)
        def _():
            x_copy(owner, index, 0).start()

    def gather(buffer, owner, index, at, fresh):
        raw = buffer[owner, index].astype(F32).reshape(2 * cap, piece)
        squares = jnp.sum(raw * raw, axis=1, keepdims=True)
        left = (raw * gains[pl.ds(at, 1), :]).astype(BF16)
        sums[owner] = jnp.where(fresh, 0.0, sums[owner]) + squares
        for low in (0, width):
            product = jnp.dot(
                left, w[part(at), low : low + width], preferred_element_type=F32
            )
            held = acc[owner, :, low : low + width]
            acc[owner, :, low : low + width] = jnp.where(fresh, 0.0, held) + product

    def result(owner, which):
        source = owner * 2 + jnp.where(which == 0, side, 1 - side)
        return pltpu.make_async_copy(out.at[owner, which], act_hbm.at[source], out_sem)

    def owner_of(step, up):
        return jnp.where(up == 1, place + step, place - step)

    def exists(step, up):
        owner = owner_of(step, up)
        return (owner >= 0) & (owner < length) & (step + 1 - up > 0)

    def each(step, action):
        def one(up, carry):
            @pl.when(exists(step, up))
            def _():
                action(owner_of(step, up), up)

            return carry

        lax.fori_loop(0, 2, one, 0)

    def meet(owner, index):
        y_copy(owner, index).wait_recv()

        @pl.when(index < late)
        def _():
            x_copy(owner, index, 1).start()

        gather(rows, owner, index, index, index == 0)

    def take(owner):
        def add(index, carry):
            for which in range(2):
                x_copy(owner, index, which).wait_recv()
            gather(cross, owner, index, parts + index, False)
            return carry

        lax.fori_loop(0, late, add, 0)

    def close(owner):
        inverse_rms = lax.rsqrt(sums[owner][:, :1] / (2 * half) + 1e-05)
        gate = acc[owner, :, :width] * inverse_rms
        up = acc[owner, :, width:] * inverse_rms
        active = gate * jax.nn.sigmoid(1.702 * gate) * (up + 1.0)
        out[owner] = active.reshape(2, cap, width).astype(BF16)
        for which in range(2):
            result(owner, which).start()

    hid_copy = pltpu.make_async_copy(zbuf.at[place, own_spot], hid_hbm, hid_sem)

    lag = 2

    def turn(step, index):
        late_turn = index < lag
        met_step = jnp.where(late_turn, step - 1, step)
        met_index = jnp.where(late_turn, index + parts - lag, index - lag)
        ending = jnp.where(step < length, parts - 1, lag - 1)
        closing = (step > 0) & (index == ending)

        @pl.when(step == 0)
        def _():
            sized(index, lambda size: reduce(index, size))

        def collect(owner, up):
            @pl.when(step > 0)
            def _():
                @pl.when(index == 0)
                def _():
                    meta_copy(owner, 1 - up).wait_recv()

                    @pl.when(has_next(1 - up))
                    def _():
                        meta_copy(owner, 1 - up).start()

                def pass_on(size):
                    line_copy(owner, index, 1 - up, size).wait_recv()

                    @pl.when(has_next(1 - up))
                    def _():
                        line_copy(owner, index, 1 - up, size).start()

                sized(index, pass_on)

            pick(owner, index)

        each(step, collect)

        @pl.when((step == 1) & (index == 0))
        def _():
            hid_copy.start()

        @pl.when(closing)
        def _():
            each(step - 1, lambda owner, up: take(owner))

        @pl.when(met_step >= 0)
        def _():
            each(met_step, lambda owner, up: meet(owner, met_index))

        @pl.when(closing)
        def _():
            each(step - 1, lambda owner, up: close(owner))

    def advance(step, carry):
        def one(index, carry):
            turn(step, index)
            return carry

        lax.fori_loop(0, jnp.where(step < length, parts, lag), one, 0)
        return carry

    lax.fori_loop(0, length + 1, advance, 0)

    y_whole = remote(ysend, ysend, ysend_sem, yrecv_sem.at[0, 0], partner)
    x_whole = remote(cross, cross, xsend_sem, xrecv_sem.at[0, 0, 0], across)
    y_whole.wait_send()
    x_whole.wait_send()

    def drain(owner, carry):
        for up in range(2):
            came = jnp.where(up == 1, owner <= place, owner >= place)

            @pl.when(has_next(up) & came)
            def _(up=up):
                meta_copy(owner, up).wait_send()
                sent = zbuf.at[owner, pl.ds(0, half + rest)]
                remote(
                    sent, sent, zsend_sem.at[up, owner], zrecv_sem.at[owner, 0], across
                ).wait_send()

        return carry

    lax.fori_loop(0, length, drain, 0)
    pltpu.make_async_copy(out, out, out_sem).wait()
    hid_copy.wait()
    sent = psend.at[pl.ds(0, half + rest)]
    remote(sent, sent, psend_sem, precv_sem.at[0], across).wait_send()

    for j in range(1, reach + 1):

        @pl.when(block + j < blocks)
        def _(j=j):
            for copy in window_copies(j):
                copy.wait_send()


def place_kernel(hid_in, act_in, hid_out, act_out, hid, act, in_sem, out_sem):
    pieces = act_in.shape[0]
    parts = max(n for n in range(1, pieces + 1) if hid_in.shape[0] % (16 * n) == 0)
    size = hid_in.shape[0] // parts
    spots = [(hid_in, hid, hid_out, pl.ds(n * size, size)) for n in range(parts)]
    spots += [(act_in, act, act_out, n) for n in range(pieces)]
    loads = [
        pltpu.make_async_copy(source.at[at], held.at[at], in_sem.at[n])
        for n, (source, held, _, at) in enumerate(spots)
    ]
    stores = [
        pltpu.make_async_copy(held.at[at], target.at[at], out_sem.at[n])
        for n, (_, held, target, at) in enumerate(spots)
    ]
    for copy in loads:
        copy.start()
    for load, store in zip(loads, stores):
        load.wait()
        store.start()
    for copy in stores:
        copy.wait()


def placed(hidden, active):
    in_hbm = pl.BlockSpec(memory_space=pl.ANY)
    pieces = active.shape[0]
    return pl.pallas_call(
        place_kernel,
        out_shape=(
            jax.ShapeDtypeStruct(hidden.shape, hidden.dtype),
            jax.ShapeDtypeStruct(active.shape, active.dtype),
        ),
        in_specs=[in_hbm] * 2,
        out_specs=(in_hbm, in_hbm),
        scratch_shapes=[
            pltpu.VMEM(hidden.shape, hidden.dtype),
            pltpu.VMEM(active.shape, active.dtype),
            pltpu.SemaphoreType.DMA((2 * pieces,)),
            pltpu.SemaphoreType.DMA((2 * pieces,)),
        ],
    )(hidden, active)


def along_line(
    count, cap, reach, queries, keys, values, residual, routes, norm_gain, out_weight, expert_weight
):
    tokens = queries.shape[0]
    width_all = residual.shape[1]
    half = width_all // 2
    length = count // 2
    width = expert_weight.shape[3]
    piece = min(384, half // 32 * 16)
    late = (half - 16) // piece
    parts = late + 2
    total = parts + late
    in_vmem = pl.BlockSpec(memory_space=pltpu.VMEM)
    in_hbm = pl.BlockSpec(memory_space=pl.ANY)
    dma = pltpu.SemaphoreType.DMA
    return pl.pallas_call(
        functools.partial(line_kernel, count, cap, reach, late),
        out_shape=(
            jax.ShapeDtypeStruct((half, tokens), BF16),
            jax.ShapeDtypeStruct((count, cap, width), BF16),
        ),
        in_specs=[in_hbm] * 4 + [in_vmem] * 2 + [in_hbm] * 2,
        out_specs=(in_hbm, in_hbm),
        scratch_shapes=[
            pltpu.VMEM(queries.shape, BF16),
            pltpu.VMEM(((reach + 1) * tokens, keys.shape[1]), BF16),
            pltpu.VMEM(((reach + 1) * tokens, values.shape[1]), BF16),
            pltpu.VMEM((parts * piece, tokens), BF16),
            pltpu.VMEM(queries.shape, BF16),
            pltpu.VMEM((2, half, out_weight.shape[0]), BF16),
            pltpu.VMEM((total * piece, 2, width), BF16),
            pltpu.VMEM((total * piece, 2 * width), BF16),
            pltpu.VMEM((total, piece), F32),
            pltpu.VMEM((parts * piece, tokens), BF16),
            pltpu.VMEM((parts * piece, tokens), BF16),
            pltpu.VMEM((length, count, tokens), F32),
            pltpu.VMEM((length, parts * piece, tokens), BF16),
            pltpu.VMEM((length, parts, cap, piece), BF16),
            pltpu.VMEM((length, parts, 2, cap, piece), BF16),
            pltpu.VMEM((length, late, 2, cap, piece), BF16),
            pltpu.VMEM((length, 2 * cap, 2 * width), F32),
            pltpu.VMEM((length, 2 * cap, 128), F32),
            pltpu.VMEM((length, 2, cap, width), BF16),
            dma((5,)),
            dma((2, reach)),
            dma((2, reach)),
            dma((2,)),
            dma((3,)),
            dma,
            dma((parts,)),
            dma((2, length)),
            dma((length,)),
            dma((2, length)),
            dma((length, parts)),
            dma,
            dma((length, parts)),
            dma,
            dma((length, late, 2)),
            dma,
            dma,
        ],
        compiler_params=pltpu.CompilerParams(
            collective_id=1, has_side_effects=True, vmem_limit_bytes=60 * 1024 * 1024
        ),
    )(
        queries,
        keys,
        values,
        residual.T,
        routes.T,
        norm_gain,
        out_weight.T,
        expert_weight[0],
    )


def body(residual, queries, keys, values, out_weight, norm_gain, routes, expert_weight):
    tokens_here = queries.shape[0]
    heads_count = lax.axis_size("head")
    reach = max(1, lax.axis_size("ctx") // 16) * lax.axis_size("grp")
    width_all = residual.shape[1]
    half = width_all // heads_count
    count = lax.axis_size("ctx")
    experts_all = expert_weight.shape[0] * count
    routed = tokens_here * TOP
    cap = min(tokens_here, routed // experts_all + max(1, routed // (8 * experts_all)))
    hidden_width = expert_weight.shape[3]
    if heads_count == 2 and count % 2 == 0 and experts_all == count and 2 * cap >= tokens_here:
        hidden, active = along_line(
            count,
            cap,
            reach,
            queries,
            keys,
            values,
            residual,
            routes,
            norm_gain,
            out_weight,
            expert_weight,
        )
        hidden, active = placed(hidden, active)
        return (hidden.T, active.reshape(1, 1, count * cap, hidden_width))
    in_vmem = pl.BlockSpec(memory_space=pltpu.VMEM)
    in_hbm = pl.BlockSpec(memory_space=pl.ANY)
    hidden, active = pl.pallas_call(
        functools.partial(layer_kernel, count, cap, reach),
        out_shape=(
            jax.ShapeDtypeStruct((half, tokens_here), BF16),
            jax.ShapeDtypeStruct((count, cap, hidden_width), BF16),
        ),
        in_specs=[in_vmem] * 6 + [in_hbm] * 2,
        out_specs=(in_vmem, in_vmem),
        scratch_shapes=[
            pltpu.VMEM(((reach + 1) * tokens_here, keys.shape[1]), BF16),
            pltpu.VMEM(((reach + 1) * tokens_here, values.shape[1]), BF16),
            pltpu.VMEM(queries.shape, BF16),
            pltpu.VMEM((heads_count, half, out_weight.shape[0]), BF16),
            pltpu.VMEM((width_all, 2, hidden_width), BF16),
            pltpu.VMEM((width_all, 2 * hidden_width), BF16),
            pltpu.VMEM((heads_count - 1, half, tokens_here), BF16),
            pltpu.VMEM((heads_count - 1, half, tokens_here), BF16),
            pltpu.VMEM((count, tokens_here), F32),
            pltpu.VMEM((count, tokens_here), F32),
            pltpu.VMEM((count, cap, half), BF16),
            pltpu.VMEM((heads_count, count, cap, half), BF16),
            pltpu.SemaphoreType.DMA((2, reach)),
            pltpu.SemaphoreType.DMA((2, reach)),
            pltpu.SemaphoreType.DMA((heads_count,)),
            pltpu.SemaphoreType.DMA,
            pltpu.SemaphoreType.DMA((heads_count - 1,)),
            pltpu.SemaphoreType.DMA((heads_count - 1,)),
            pltpu.SemaphoreType.DMA((count,)),
            pltpu.SemaphoreType.DMA((count,)),
            pltpu.SemaphoreType.DMA((heads_count - 1, count)),
            pltpu.SemaphoreType.DMA((heads_count - 1, count)),
        ],
        compiler_params=pltpu.CompilerParams(
            collective_id=0, has_side_effects=True, vmem_limit_bytes=60 * 1024 * 1024
        ),
    )(
        queries,
        keys,
        values,
        residual.T,
        routes.T,
        norm_gain.reshape(heads_count, half),
        out_weight.T,
        expert_weight[0],
    )
    return (hidden.T, active.reshape(1, 1, count * cap, hidden_width))


def solution(mesh):
    in_specs = (
        P(("ctx", "grp"), None),
        P(("ctx", "grp"), "head"),
        P(("ctx", "grp"), "head"),
        P(("ctx", "grp"), "head"),
        P("head", None),
        P(),
        P(("ctx", "grp"), None),
        P("ctx", None, None, "head"),
    )
    out_specs = (P(("ctx", "grp"), "head"), P("ctx", "grp", None, "head"))
    return jax.shard_map(body, mesh=mesh, in_specs=in_specs, out_specs=out_specs, check_vma=False)
```

```python
import functools
import jax
import jax.numpy as jnp
from jax import lax
from jax.experimental import pallas as pl
from jax.experimental.pallas import tpu as pltpu
from jax.sharding import PartitionSpec as P

D = 2880
HD = 64
TOP = 4
PIECE = 3 * 128


MESH = pl.DeviceIdType.MESH
F32 = jnp.float32
BF16 = jnp.bfloat16


def turn_of(step, count):
    return 1 + lax.rem(step + count // 2 - 1, count - 1)


def in_pair(values, group, lanes):
    zeros = jnp.zeros((values.shape[0], HD), values.dtype)
    if values.shape[1] == HD:
        return jnp.concatenate([values, zeros], 1), jnp.concatenate([zeros, values], 1)
    first = group % 2 == 0
    base = group // 2 * 2 * HD
    pair = values[:, base : base + 2 * HD]
    swapped = jnp.concatenate([pair[:, HD:], pair[:, :HD]], 1)
    low = jnp.where(lanes < HD, pair if first else swapped, jnp.zeros_like(pair))
    high = jnp.where(lanes >= HD, swapped if first else pair, jnp.zeros_like(pair))
    return low, high


def attend(block, reach, q_ref, kbuf, vbuf, att_ref):
    tokens = q_ref.shape[0]
    window = kbuf.shape[0]
    kv_local = kbuf.shape[1] // HD
    pairs = q_ref.shape[1] // (2 * HD * kv_local)
    rows = pairs * tokens
    place = lax.rem(lax.broadcasted_iota(jnp.int32, (rows, window), 0), tokens)
    column = lax.broadcasted_iota(jnp.int32, (rows, window), 1)
    ahead = place + reach * tokens - column
    allowed = (ahead >= 0) & (ahead < reach * tokens) & (column >= (reach - block) * tokens)
    lanes = lax.broadcasted_iota(jnp.int32, (window, 2 * HD), 1)
    left = lax.broadcasted_iota(jnp.int32, (rows, 2 * HD), 1) < HD
    for group in range(kv_local):
        key_pair = in_pair(kbuf[...], group, lanes)
        value_pair = in_pair(vbuf[...], group, lanes)
        first = group * pairs
        queries = jnp.concatenate(
            [
                q_ref[:, (first + p) * 2 * HD : (first + p + 1) * 2 * HD]
                for p in range(pairs)
            ],
            0,
        )
        mixed = jnp.zeros((rows, 2 * HD), F32)
        totals = []
        for side in range(2):
            scores = lax.dot_general(
                queries,
                key_pair[side],
                (((1,), (1,)), ((), ())),
                preferred_element_type=F32,
            )
            scores = jnp.where(allowed, scores * HD ** (-0.5), -1e30)
            row_max = jnp.max(scores, axis=1, keepdims=True)
            weights = jnp.where(allowed, jnp.exp(scores - row_max), 0.0)
            totals.append(jnp.sum(weights, axis=1, keepdims=True))
            mixed = mixed + jnp.dot(
                weights.astype(BF16), value_pair[side], preferred_element_type=F32
            )
        attended = (mixed / jnp.where(left, totals[0], totals[1])).astype(BF16)
        for p in range(pairs):
            att_ref[:, (first + p) * 2 * HD : (first + p + 1) * 2 * HD] = attended[
                p * tokens : (p + 1) * tokens
            ]


def layer_kernel(
    count,
    cap,
    reach,
    q_ref,
    k_ref,
    v_ref,
    res_ref,
    routes_ref,
    gain_ref,
    ow_hbm,
    w_hbm,
    hid_ref,
    act_ref,
    kbuf,
    vbuf,
    att_ref,
    ow,
    paired,
    w,
    psend,
    precv,
    hits_ref,
    before_ref,
    sbuf,
    rbuf,
    ksend_sem,
    krecv_sem,
    ow_sem,
    w_sem,
    psend_sem,
    precv_sem,
    send_sem,
    recv_sem,
    xsend_sem,
    xrecv_sem,
):
    me = lax.axis_index("ctx")
    head = lax.axis_index("head")
    heads = rbuf.shape[0]
    others = [lax.rem(head + j, heads) for j in range(1, heads)]
    half, tokens = hid_ref.shape
    width = act_ref.shape[2]

    def ow_copy(which, slot):
        rows = pl.ds(pl.multiple_of(which * half, 16), half)
        return pltpu.make_async_copy(ow_hbm.at[rows], ow.at[slot], ow_sem.at[slot])

    for j in range(1, heads):
        ow_copy(others[j - 1], j).start()
    ow_copy(head, 0).start()
    pltpu.make_async_copy(w_hbm, paired, w_sem).start()

    barrier = pltpu.get_barrier_semaphore()
    for other in others:
        pl.semaphore_signal(barrier, inc=1, device_id={"head": other}, device_id_type=MESH)

    def greet(step, carry):
        peer = lax.rem(me + step, count)
        pl.semaphore_signal(barrier, inc=1, device_id={"ctx": peer}, device_id_type=MESH)
        return carry

    lax.fori_loop(1, count, greet, 0)

    groups = lax.axis_size("grp")
    block = me * groups + lax.axis_index("grp")
    blocks = count * groups

    def at_block(index):
        return {"ctx": index // groups, "grp": lax.rem(index, groups)}

    for j in range(1, reach + 1):
        for peer in (lax.rem(block + j, blocks), lax.rem(block + blocks - j, blocks)):
            pl.semaphore_signal(barrier, inc=1, device_id=at_block(peer), device_id_type=MESH)

    def window_copies(j):
        place = pl.ds((reach - j) * tokens, tokens)
        target = at_block(lax.rem(block + j, blocks))
        return [
            pltpu.make_async_remote_copy(
                src_ref=source,
                dst_ref=buffer.at[place],
                send_sem=ksend_sem.at[n, j - 1],
                recv_sem=krecv_sem.at[n, j - 1],
                device_id=target,
                device_id_type=MESH,
            )
            for n, (source, buffer) in enumerate(((k_ref, kbuf), (v_ref, vbuf)))
        ]

    pl.semaphore_wait(barrier, count - 1 + heads - 1 + 2 * reach)
    for j in range(1, reach + 1):

        @pl.when(block + j < blocks)
        def _(j=j):
            for copy in window_copies(j):
                copy.start()

    kbuf[reach * tokens :, :] = k_ref[...]
    vbuf[reach * tokens :, :] = v_ref[...]

    def project(slot):
        return lax.dot_general(
            ow[slot], att_ref[...], (((1,), (1,)), ((), ())), preferred_element_type=F32
        ).astype(BF16)

    def exchange(j):
        return pltpu.make_async_remote_copy(
            src_ref=psend.at[j - 1],
            dst_ref=precv.at[j - 1],
            send_sem=psend_sem.at[j - 1],
            recv_sem=precv_sem.at[j - 1],
            device_id={"head": others[j - 1]},
            device_id_type=MESH,
        )

    for j in range(1, reach + 1):

        @pl.when(block >= j)
        def _(j=j):
            for copy in window_copies(j):
                copy.wait_recv()

        @pl.when(block < j)
        def _(j=j):
            place = pl.ds((reach - j) * tokens, tokens)
            kbuf[place, :] = jnp.zeros((tokens, kbuf.shape[1]), BF16)
            vbuf[place, :] = jnp.zeros((tokens, vbuf.shape[1]), BF16)

        @pl.when(block + j < blocks)
        def _(j=j):
            for copy in window_copies(j):
                copy.wait_send()

    attend(block, reach, q_ref, kbuf, vbuf, att_ref)

    for j in range(1, heads):
        ow_copy(others[j - 1], j).wait()
        psend[j - 1] = project(j)
        exchange(j).start()
    ow_copy(head, 0).wait()
    projected = project(0).astype(F32)

    expert_ids = lax.broadcasted_iota(jnp.int32, (count, tokens), 0)
    hits = jnp.zeros((count, tokens), F32)
    for k in range(routes_ref.shape[0]):
        hits = hits + jnp.where(routes_ref[k : k + 1, :] == expert_ids, 1.0, 0.0)
    earlier = jnp.where(
        lax.broadcasted_iota(jnp.int32, (tokens, tokens), 0)
        < lax.broadcasted_iota(jnp.int32, (tokens, tokens), 1),
        1.0,
        0.0,
    ).astype(BF16)
    hits_ref[...] = hits
    before_ref[...] = jnp.dot(hits.astype(BF16), earlier, preferred_element_type=F32)
    residual = res_ref[pl.ds(pl.multiple_of(head * half, 16), half), :].astype(F32)

    for j in range(1, heads):
        exchange(j).wait()
        projected = projected + precv[j - 1].astype(F32)
    hid_ref[...] = (residual + projected).astype(BF16)

    slots = lax.broadcasted_iota(jnp.int32, (cap, tokens), 0).astype(F32)

    def rows_for(expert):
        wanted = hits_ref[pl.ds(expert, 1), :] > 0.5
        picks = jnp.where((slots == before_ref[pl.ds(expert, 1), :]) & wanted, 1.0, 0.0)
        return lax.dot_general(
            picks.astype(BF16),
            hid_ref[...],
            (((1,), (1,)), ((), ())),
            preferred_element_type=F32,
        ).astype(BF16)

    def routed(step):
        turn = turn_of(step, count)
        return pltpu.make_async_remote_copy(
            src_ref=sbuf.at[turn],
            dst_ref=rbuf.at[head, me],
            send_sem=send_sem.at[turn],
            recv_sem=recv_sem.at[me],
            device_id={"ctx": lax.rem(me + turn, count)},
            device_id_type=MESH,
        )

    def landed(source):
        return pltpu.make_async_remote_copy(
            src_ref=rbuf.at[head, source],
            dst_ref=rbuf.at[head, source],
            send_sem=send_sem.at[0],
            recv_sem=recv_sem.at[source],
            device_id={"head": others[0]},
            device_id_type=MESH,
        )

    def crossed(j, source):
        return pltpu.make_async_remote_copy(
            src_ref=rbuf.at[head, source],
            dst_ref=rbuf.at[head, source],
            send_sem=xsend_sem.at[j - 1, source],
            recv_sem=xrecv_sem.at[j - 1, source],
            device_id={"head": others[j - 1]},
            device_id_type=MESH,
        )

    def cross(source):
        for j in range(1, heads):
            crossed(j, source).start()

    def mirror(source):
        for j in range(1, heads):
            origin = lax.rem(head + heads - j, heads)
            pltpu.make_async_remote_copy(
                src_ref=rbuf.at[origin, source],
                dst_ref=rbuf.at[origin, source],
                send_sem=xsend_sem.at[j - 1, source],
                recv_sem=xrecv_sem.at[j - 1, source],
                device_id={"head": others[j - 1]},
                device_id_type=MESH,
            ).wait_recv()

    def dispatch(step, carry):
        turn = turn_of(step, count)
        sbuf[turn] = rows_for(lax.rem(me + turn, count))
        routed(step).start()
        return carry

    lax.fori_loop(0, count - 1, dispatch, 0)
    rbuf[head, me] = rows_for(me)
    cross(me)
    pltpu.make_async_copy(w_hbm, paired, w_sem).wait()

    def unpair(step, carry):
        rows = pl.ds(pl.multiple_of(step * 32, 32), 32)
        pair = jnp.swapaxes(paired[rows], 0, 1)
        w[rows, :width] = pair[0]
        w[rows, width:] = pair[1]
        return carry

    lax.fori_loop(0, w.shape[0] // 32, unpair, 0)

    def expert(source):
        squares = jnp.zeros((cap, 1), F32)
        parts = []
        for part in range(heads):
            rows = rbuf[part, source].astype(F32)
            squares = squares + jnp.sum(rows * rows, axis=1, keepdims=True)
            parts.append((rows * gain_ref[part : part + 1, :]).astype(BF16))
        inverse_rms = lax.rsqrt(squares / (heads * half) + 1e-05)

        def product(low):
            total = jnp.zeros((cap, width), F32)
            for part in range(heads):
                total = total + jnp.dot(
                    parts[part],
                    w[part * half : (part + 1) * half, low : low + width],
                    preferred_element_type=F32,
                )
            return total

        gate = product(0) * inverse_rms
        up = product(width) * inverse_rms
        act_ref[source] = (gate * jax.nn.sigmoid(1.702 * gate) * (up + 1.0)).astype(BF16)

    def receive(step, carry):
        source = lax.rem(me + count - turn_of(step, count), count)
        landed(source).wait_recv()
        cross(source)
        before = jnp.where(
            step == 0, me, lax.rem(me + count - turn_of(jnp.maximum(step - 1, 0), count), count)
        )
        mirror(before)
        expert(before)
        return carry

    lax.fori_loop(0, count - 1, receive, 0)
    last = lax.rem(me + count - turn_of(count - 2, count), count)
    mirror(last)
    expert(last)

    def drain(step, carry):
        routed(step).wait_send()
        for j in range(1, heads):
            crossed(j, lax.rem(me + step + 1, count)).wait_send()
        return carry

    lax.fori_loop(0, count - 1, drain, 0)
    for j in range(1, heads):
        crossed(j, me).wait_send()


def line_kernel(
    count,
    cap,
    reach,
    late,
    q_hbm,
    k_hbm,
    v_hbm,
    res_hbm,
    routes_ref,
    gain_ref,
    ow_hbm,
    w_hbm,
    hid_hbm,
    act_hbm,
    q_ref,
    kbuf,
    vbuf,
    res_ref,
    att_ref,
    ow,
    paired,
    w,
    gains,
    psend,
    precv,
    meta,
    zbuf,
    ysend,
    rows,
    cross,
    acc,
    sums,
    out,
    in_sem,
    ksend_sem,
    krecv_sem,
    ow_sem,
    w_sem,
    psend_sem,
    precv_sem,
    msend_sem,
    mrecv_sem,
    zsend_sem,
    zrecv_sem,
    ysend_sem,
    yrecv_sem,
    xsend_sem,
    xrecv_sem,
    hid_sem,
    out_sem,
):
    me = lax.axis_index("ctx")
    head = lax.axis_index("head")
    other = 1 - head
    length = count // 2
    place = me // 2
    side = lax.rem(me, 2)
    half, tokens = hid_hbm.shape
    width = act_hbm.shape[2]
    parts = late + 2
    piece = rows.shape[4]
    rest = half - late * piece
    groups = lax.axis_size("grp")
    block = me * groups + lax.axis_index("grp")
    blocks = count * groups

    def at_block(index):
        return {"ctx": index // groups, "grp": lax.rem(index, groups)}

    def on_line(position):
        return {"ctx": position * 2 + side}

    partner = {"ctx": place * 2 + 1 - side}
    across = {"head": other}

    barrier = pltpu.get_barrier_semaphore()
    expected = 2
    for peer in (partner, across):
        pl.semaphore_signal(barrier, inc=1, device_id=peer, device_id_type=MESH)

    def greet(there, peer):
        @pl.when(there)
        def _():
            pl.semaphore_signal(barrier, inc=1, device_id=peer, device_id_type=MESH)

        return jnp.where(there, 1, 0)

    expected = expected + greet(place > 0, on_line(place - 1))
    expected = expected + greet(place + 1 < length, on_line(place + 1))
    for j in range(1, reach + 1):
        expected = expected + greet(block + j < blocks, at_block(block + j))
        expected = expected + greet(block >= j, at_block(block - j))

    def span(which, start, size):
        return pl.ds(pl.multiple_of(which * half + start, 16), size)

    late_size = late * piece
    far_start = (late + 1) * piece
    mine = pl.ds(reach * tokens, tokens)
    own_spot = pl.ds(0, half)
    early_spot = pl.ds(far_start, rest)
    late_spot = pl.ds(parts * piece, late_size)
    local = [
        pltpu.make_async_copy(k_hbm, kbuf.at[mine], in_sem.at[0]),
        pltpu.make_async_copy(v_hbm, vbuf.at[mine], in_sem.at[1]),
        pltpu.make_async_copy(q_hbm, q_ref, in_sem.at[2]),
    ]
    res_copies = [
        pltpu.make_async_copy(res_hbm.at[span(head, 0, half)], res_ref.at[own_spot], in_sem.at[3]),
        pltpu.make_async_copy(
            res_hbm.at[span(other, late_size, rest)], res_ref.at[early_spot], in_sem.at[4]
        ),
    ]
    w_copies = [
        pltpu.make_async_copy(w_hbm.at[span(which, start, size)], paired.at[spot], w_sem.at[n])
        for n, (which, start, size, spot) in enumerate(
            (
                (head, 0, half, own_spot),
                (other, late_size, rest, early_spot),
                (other, 0, late_size, late_spot),
            )
        )
    ]
    ow_copies = [
        pltpu.make_async_copy(ow_hbm.at[span(which, 0, half)], ow.at[n], ow_sem.at[n])
        for n, which in enumerate((other, head))
    ]
    for copy in local + ow_copies + res_copies + w_copies:
        copy.start()

    def remote(source, target, send, recv, device):
        return pltpu.make_async_remote_copy(
            src_ref=source,
            dst_ref=target,
            send_sem=send,
            recv_sem=recv,
            device_id=device,
            device_id_type=MESH,
        )

    def window_copies(j):
        rows_at = pl.ds((reach - j) * tokens, tokens)
        target = at_block(block + j)
        return [
            remote(source, buffer.at[rows_at], ksend_sem.at[n, j - 1], krecv_sem.at[n, j - 1], target)
            for n, (source, buffer) in enumerate(((k_hbm, kbuf), (v_hbm, vbuf)))
        ]

    expert_ids = lax.broadcasted_iota(jnp.int32, (count, tokens), 0)
    hits = jnp.zeros((count, tokens), F32)
    for k in range(routes_ref.shape[0]):
        hits = hits + jnp.where(routes_ref[k : k + 1, :] == expert_ids, 1.0, 0.0)
    earlier = jnp.where(
        lax.broadcasted_iota(jnp.int32, (tokens, tokens), 0)
        < lax.broadcasted_iota(jnp.int32, (tokens, tokens), 1),
        1.0,
        0.0,
    ).astype(BF16)
    before = jnp.dot(hits.astype(BF16), earlier, preferred_element_type=F32)
    meta[place] = jnp.where(hits > 0.5, before, -1.0)

    gain = gain_ref[...].reshape(1, 2 * half)
    gains[...] = jnp.zeros(gains.shape, F32)
    order = [(0, n) for n in range(late + 1)] + [(1, late)] + [(1, n) for n in range(late)]
    for n, (far, index) in enumerate(order):
        size = piece if index < late else rest
        left = gain[:, index * piece : index * piece + size]
        right = gain[:, half + index * piece : half + index * piece + size]
        gains[n : n + 1, :size] = jnp.where(head == far, left, right)
    if rest < piece:
        blank = piece - rest
        for start in (half, far_start + rest):
            zbuf[:, start : start + blank, :] = jnp.zeros((length, blank, tokens), BF16)
            paired[start : start + blank] = jnp.zeros((blank, 2, width), BF16)

    pl.semaphore_wait(barrier, expected)
    for j in range(1, reach + 1):

        @pl.when(block + j < blocks)
        def _(j=j):
            for copy in window_copies(j):
                copy.start()

    def meta_copy(owner, up):
        to = jnp.where(up == 1, place + 1, place - 1)
        spot = meta.at[owner]
        return remote(spot, spot, msend_sem.at[up, owner], mrecv_sem.at[owner], on_line(to))

    def has_next(up):
        return jnp.where(up == 1, place + 1 < length, place > 0)

    for up in range(2):

        @pl.when(has_next(up))
        def _(up=up):
            meta_copy(place, up).start()

    for j in range(1, reach + 1):

        @pl.when(block < j)
        def _(j=j):
            rows_at = pl.ds((reach - j) * tokens, tokens)
            kbuf[rows_at, :] = jnp.zeros((tokens, kbuf.shape[1]), BF16)
            vbuf[rows_at, :] = jnp.zeros((tokens, vbuf.shape[1]), BF16)

    for copy in local:
        copy.wait()
    for j in range(1, reach + 1):

        @pl.when(block >= j)
        def _(j=j):
            for copy in window_copies(j):
                copy.wait_recv()

    attend(block, reach, q_ref, kbuf, vbuf, att_ref)

    def part(index, size=piece):
        return pl.ds(pl.multiple_of(index * piece, 16), size)

    def sized(index, action):
        @pl.when(index < late)
        def _():
            action(piece)

        @pl.when(index >= late)
        def _():
            action(rest)

    def project(slot, index, size):
        return lax.dot_general(
            ow[slot, part(index, size), :],
            att_ref[...],
            (((1,), (1,)), ((), ())),
            preferred_element_type=F32,
        ).astype(BF16)

    def exchange(index, size):
        return remote(
            psend.at[part(index, size)],
            precv.at[part(index, size)],
            psend_sem,
            precv_sem.at[index],
            across,
        )

    for copy in ow_copies:
        copy.wait()

    def offer(index, carry):
        psend[part(index), :] = project(0, index, piece)
        exchange(index, piece).start()
        return carry

    lax.fori_loop(0, late, offer, 0)
    for n in range(2):
        psend[part(late + n, rest), :] = project(n, late, rest)
        exchange(late + n, rest).start()

    def keep(index, carry):
        zbuf[place, part(index), :] = project(1, index, piece)
        return carry

    lax.fori_loop(0, late, keep, 0)
    zbuf[place, part(late, rest), :] = psend[part(late + 1, rest), :]
    zbuf[place, part(late + 1, rest), :] = psend[part(late, rest), :]
    for copy in res_copies + w_copies:
        copy.wait()

    def unpair(index):
        def one(step, carry):
            at = pl.ds(pl.multiple_of(index * piece + step * 32, 32), 32)
            pair = jnp.swapaxes(paired[at], 0, 1)
            w[at, :width] = pair[0]
            w[at, width:] = pair[1]
            return carry

        lax.fori_loop(0, piece // 32, one, 0)


    def line_copy(owner, index, up, size):
        to = jnp.where(up == 1, place + 1, place - 1)
        spot = zbuf.at[owner, part(index, size)]
        return remote(
            spot, spot, zsend_sem.at[up, owner], zrecv_sem.at[owner, index], on_line(to)
        )

    def reduce(index, size):
        at = part(index, size)
        exchange(index, size).wait_recv()
        total = zbuf[place, at, :].astype(F32) + precv[at, :].astype(F32)
        zbuf[place, at, :] = (res_ref[at, :].astype(F32) + total).astype(BF16)
        for up in range(2):

            @pl.when(has_next(up))
            def _(up=up):
                line_copy(place, index, up, size).start()

    slots = lax.broadcasted_iota(jnp.int32, (cap, tokens), 0).astype(F32)

    def y_copy(owner, index):
        return remote(
            ysend.at[owner, index],
            rows.at[owner, index, 1],
            ysend_sem,
            yrecv_sem.at[owner, index],
            partner,
        )

    def x_copy(owner, index, which):
        return remote(
            rows.at[owner, index, which],
            cross.at[owner, index, which],
            xsend_sem,
            xrecv_sem.at[owner, index, which],
            across,
        )

    def pick(owner, index):
        def picks(expert):
            wanted = meta[owner, pl.ds(expert, 1), :]
            return jnp.where(slots == wanted, 1.0, 0.0)

        both = jnp.concatenate([picks(place * 2 + 1 - side), picks(me)], 0).astype(BF16)
        found = lax.dot_general(
            both,
            zbuf[owner, part(index), :],
            (((1,), (1,)), ((), ())),
            preferred_element_type=F32,
        )
        ysend[owner, index] = found[:cap].astype(BF16)
        y_copy(owner, index).start()
        rows[owner, index, 0] = found[cap:].astype(BF16)

        @pl.when(index < late)
        def _():
            x_copy(owner, index, 0).start()

    def gather(buffer, owner, index, at, fresh):
        raw = buffer[owner, index].astype(F32).reshape(2 * cap, piece)
        squares = jnp.sum(raw * raw, axis=1, keepdims=True)
        left = (raw * gains[pl.ds(at, 1), :]).astype(BF16)
        sums[owner] = jnp.where(fresh, 0.0, sums[owner]) + squares
        for low in (0, width):
            product = jnp.dot(
                left, w[part(at), low : low + width], preferred_element_type=F32
            )
            held = acc[owner, :, low : low + width]
            acc[owner, :, low : low + width] = jnp.where(fresh, 0.0, held) + product

    def result(owner, which):
        source = owner * 2 + jnp.where(which == 0, side, 1 - side)
        return pltpu.make_async_copy(out.at[owner, which], act_hbm.at[source], out_sem)

    def owner_of(step, up):
        return jnp.where(up == 1, place + step, place - step)

    def exists(step, up):
        owner = owner_of(step, up)
        return (owner >= 0) & (owner < length) & (step + 1 - up > 0)

    def each(step, action):
        def one(up, carry):
            @pl.when(exists(step, up))
            def _():
                action(owner_of(step, up), up)

            return carry

        lax.fori_loop(0, 2, one, 0)

    def meet(owner, index):
        y_copy(owner, index).wait_recv()

        @pl.when(index < late)
        def _():
            x_copy(owner, index, 1).start()

        gather(rows, owner, index, index, index == 0)

    def take(owner):
        def add(index, carry):
            for which in range(2):
                x_copy(owner, index, which).wait_recv()
            gather(cross, owner, index, parts + index, False)
            return carry

        lax.fori_loop(0, late, add, 0)

    def close(owner):
        inverse_rms = lax.rsqrt(sums[owner][:, :1] / (2 * half) + 1e-05)
        gate = acc[owner, :, :width] * inverse_rms
        up = acc[owner, :, width:] * inverse_rms
        active = gate * jax.nn.sigmoid(1.702 * gate) * (up + 1.0)
        out[owner] = active.reshape(2, cap, width).astype(BF16)
        for which in range(2):
            result(owner, which).start()

    hid_copy = pltpu.make_async_copy(zbuf.at[place, own_spot], hid_hbm, hid_sem)

    lag = 2

    def turn(step, index):
        late_turn = index < lag
        met_step = jnp.where(late_turn, step - 1, step)
        met_index = jnp.where(late_turn, index + parts - lag, index - lag)
        ending = jnp.where(step < length, parts - 1, lag - 1)
        closing = (step > 0) & (index == ending)

        @pl.when(step == 0)
        def _():
            sized(index, lambda size: reduce(index, size))

        def collect(owner, up):
            @pl.when(step > 0)
            def _():
                @pl.when(index == 0)
                def _():
                    meta_copy(owner, 1 - up).wait_recv()

                    @pl.when(has_next(1 - up))
                    def _():
                        meta_copy(owner, 1 - up).start()

                def pass_on(size):
                    line_copy(owner, index, 1 - up, size).wait_recv()

                    @pl.when(has_next(1 - up))
                    def _():
                        line_copy(owner, index, 1 - up, size).start()

                sized(index, pass_on)

            pick(owner, index)

        each(step, collect)

        @pl.when(step == 0)
        def _():
            for n in range(2):
                which = index * 2 + n

                @pl.when(which < w.shape[0] // piece)
                def _(which=which):
                    unpair(which)

        @pl.when((step == 1) & (index == 0))
        def _():
            hid_copy.start()

        @pl.when(closing)
        def _():
            each(step - 1, lambda owner, up: take(owner))

        @pl.when(met_step >= 0)
        def _():
            each(met_step, lambda owner, up: meet(owner, met_index))

        @pl.when(closing)
        def _():
            each(step - 1, lambda owner, up: close(owner))

    def advance(step, carry):
        def one(index, carry):
            turn(step, index)
            return carry

        lax.fori_loop(0, jnp.where(step < length, parts, lag), one, 0)
        return carry

    lax.fori_loop(0, length + 1, advance, 0)

    y_whole = remote(ysend, ysend, ysend_sem, yrecv_sem.at[0, 0], partner)
    x_whole = remote(cross, cross, xsend_sem, xrecv_sem.at[0, 0, 0], across)
    y_whole.wait_send()
    x_whole.wait_send()

    def drain(owner, carry):
        for up in range(2):
            came = jnp.where(up == 1, owner <= place, owner >= place)

            @pl.when(has_next(up) & came)
            def _(up=up):
                meta_copy(owner, up).wait_send()
                sent = zbuf.at[owner, pl.ds(0, half + rest)]
                remote(
                    sent, sent, zsend_sem.at[up, owner], zrecv_sem.at[owner, 0], across
                ).wait_send()

        return carry

    lax.fori_loop(0, length, drain, 0)
    pltpu.make_async_copy(out, out, out_sem).wait()
    hid_copy.wait()
    sent = psend.at[pl.ds(0, half + rest)]
    remote(sent, sent, psend_sem, precv_sem.at[0], across).wait_send()

    for j in range(1, reach + 1):

        @pl.when(block + j < blocks)
        def _(j=j):
            for copy in window_copies(j):
                copy.wait_send()


def place_kernel(hid_in, act_in, hid_out, act_out, hid, act, in_sem, out_sem):
    pieces = 4
    parts = 2
    size = hid_in.shape[0] // parts
    spots = [(hid_in, hid, hid_out, pl.ds(n * size, size)) for n in range(parts)]
    spots += [(act_in, act, act_out, pl.ds(n * (act_in.shape[0] // pieces), act_in.shape[0] // pieces)) for n in range(pieces)]
    loads = [
        pltpu.make_async_copy(source.at[at], held.at[at], in_sem.at[n])
        for n, (source, held, _, at) in enumerate(spots)
    ]
    stores = [
        pltpu.make_async_copy(held.at[at], target.at[at], out_sem.at[n])
        for n, (_, held, target, at) in enumerate(spots)
    ]
    for copy in loads:
        copy.start()
    for load, store in zip(loads, stores):
        load.wait()
        store.start()
    for copy in stores:
        copy.wait()


def placed(hidden, active):
    in_hbm = pl.BlockSpec(memory_space=pl.ANY)
    pieces = active.shape[0]
    return pl.pallas_call(
        place_kernel,
        out_shape=(
            jax.ShapeDtypeStruct(hidden.shape, hidden.dtype),
            jax.ShapeDtypeStruct(active.shape, active.dtype),
        ),
        in_specs=[in_hbm] * 2,
        out_specs=(in_hbm, in_hbm),
        scratch_shapes=[
            pltpu.VMEM(hidden.shape, hidden.dtype),
            pltpu.VMEM(active.shape, active.dtype),
            pltpu.SemaphoreType.DMA((2 * pieces,)),
            pltpu.SemaphoreType.DMA((2 * pieces,)),
        ],
    )(hidden, active)


def along_line(
    count, cap, reach, queries, keys, values, residual, routes, norm_gain, out_weight, expert_weight
):
    tokens = queries.shape[0]
    width_all = residual.shape[1]
    half = width_all // 2
    length = count // 2
    width = expert_weight.shape[3]
    piece = PIECE
    late = (half - 16) // piece
    parts = late + 2
    total = parts + late
    in_vmem = pl.BlockSpec(memory_space=pltpu.VMEM)
    in_hbm = pl.BlockSpec(memory_space=pl.ANY)
    dma = pltpu.SemaphoreType.DMA
    return pl.pallas_call(
        functools.partial(line_kernel, count, cap, reach, late),
        out_shape=(
            jax.ShapeDtypeStruct((half, tokens), BF16),
            jax.ShapeDtypeStruct((count, cap, width), BF16),
        ),
        in_specs=[in_hbm] * 4 + [in_vmem] * 2 + [in_hbm] * 2,
        out_specs=(in_hbm, in_hbm),
        scratch_shapes=[
            pltpu.VMEM(queries.shape, BF16),
            pltpu.VMEM(((reach + 1) * tokens, keys.shape[1]), BF16),
            pltpu.VMEM(((reach + 1) * tokens, values.shape[1]), BF16),
            pltpu.VMEM((parts * piece, tokens), BF16),
            pltpu.VMEM(queries.shape, BF16),
            pltpu.VMEM((2, half, out_weight.shape[0]), BF16),
            pltpu.VMEM((total * piece, 2, width), BF16),
            pltpu.VMEM((total * piece, 2 * width), BF16),
            pltpu.VMEM((total, piece), F32),
            pltpu.VMEM((parts * piece, tokens), BF16),
            pltpu.VMEM((parts * piece, tokens), BF16),
            pltpu.VMEM((length, count, tokens), F32),
            pltpu.VMEM((length, parts * piece, tokens), BF16),
            pltpu.VMEM((length, parts, cap, piece), BF16),
            pltpu.VMEM((length, parts, 2, cap, piece), BF16),
            pltpu.VMEM((length, late, 2, cap, piece), BF16),
            pltpu.VMEM((length, 2 * cap, 2 * width), F32),
            pltpu.VMEM((length, 2 * cap, 128), F32),
            pltpu.VMEM((length, 2, cap, width), BF16),
            dma((5,)),
            dma((2, reach)),
            dma((2, reach)),
            dma((2,)),
            dma((3,)),
            dma,
            dma((parts,)),
            dma((2, length)),
            dma((length,)),
            dma((2, length)),
            dma((length, parts)),
            dma,
            dma((length, parts)),
            dma,
            dma((length, late, 2)),
            dma,
            dma,
        ],
        compiler_params=pltpu.CompilerParams(
            collective_id=1, has_side_effects=True, vmem_limit_bytes=60 * 1024 * 1024
        ),
    )(
        queries,
        keys,
        values,
        residual.T,
        routes.T,
        norm_gain,
        out_weight.T,
        expert_weight[0],
    )


def body(residual, queries, keys, values, out_weight, norm_gain, routes, expert_weight):
    tokens_here = queries.shape[0]
    heads_count = lax.axis_size("head")
    reach = max(1, lax.axis_size("ctx") // 16) * lax.axis_size("grp")
    width_all = residual.shape[1]
    half = width_all // heads_count
    count = lax.axis_size("ctx")
    experts_all = expert_weight.shape[0] * count
    routed = tokens_here * TOP
    cap = min(tokens_here, routed // experts_all + max(1, routed // (8 * experts_all)))
    hidden_width = expert_weight.shape[3]
    if heads_count == 2 and count % 2 == 0 and experts_all == count and 2 * cap >= tokens_here and half >= 2 * PIECE:
        hidden, active = along_line(
            count,
            cap,
            reach,
            queries,
            keys,
            values,
            residual,
            routes,
            norm_gain,
            out_weight,
            expert_weight,
        )
        hidden, active = placed(hidden, active)
        return (hidden.T, active.reshape(1, 1, count * cap, hidden_width))
    in_vmem = pl.BlockSpec(memory_space=pltpu.VMEM)
    in_hbm = pl.BlockSpec(memory_space=pl.ANY)
    hidden, active = pl.pallas_call(
        functools.partial(layer_kernel, count, cap, reach),
        out_shape=(
            jax.ShapeDtypeStruct((half, tokens_here), BF16),
            jax.ShapeDtypeStruct((count, cap, hidden_width), BF16),
        ),
        in_specs=[in_vmem] * 6 + [in_hbm] * 2,
        out_specs=(in_vmem, in_vmem),
        scratch_shapes=[
            pltpu.VMEM(((reach + 1) * tokens_here, keys.shape[1]), BF16),
            pltpu.VMEM(((reach + 1) * tokens_here, values.shape[1]), BF16),
            pltpu.VMEM(queries.shape, BF16),
            pltpu.VMEM((heads_count, half, out_weight.shape[0]), BF16),
            pltpu.VMEM((width_all, 2, hidden_width), BF16),
            pltpu.VMEM((width_all, 2 * hidden_width), BF16),
            pltpu.VMEM((heads_count - 1, half, tokens_here), BF16),
            pltpu.VMEM((heads_count - 1, half, tokens_here), BF16),
            pltpu.VMEM((count, tokens_here), F32),
            pltpu.VMEM((count, tokens_here), F32),
            pltpu.VMEM((count, cap, half), BF16),
            pltpu.VMEM((heads_count, count, cap, half), BF16),
            pltpu.SemaphoreType.DMA((2, reach)),
            pltpu.SemaphoreType.DMA((2, reach)),
            pltpu.SemaphoreType.DMA((heads_count,)),
            pltpu.SemaphoreType.DMA,
            pltpu.SemaphoreType.DMA((heads_count - 1,)),
            pltpu.SemaphoreType.DMA((heads_count - 1,)),
            pltpu.SemaphoreType.DMA((count,)),
            pltpu.SemaphoreType.DMA((count,)),
            pltpu.SemaphoreType.DMA((heads_count - 1, count)),
            pltpu.SemaphoreType.DMA((heads_count - 1, count)),
        ],
        compiler_params=pltpu.CompilerParams(
            collective_id=0, has_side_effects=True, vmem_limit_bytes=60 * 1024 * 1024
        ),
    )(
        queries,
        keys,
        values,
        residual.T,
        routes.T,
        norm_gain.reshape(heads_count, half),
        out_weight.T,
        expert_weight[0],
    )
    return (hidden.T, active.reshape(1, 1, count * cap, hidden_width))


def solution(mesh):
    in_specs = (
        P(("ctx", "grp"), None),
        P(("ctx", "grp"), "head"),
        P(("ctx", "grp"), "head"),
        P(("ctx", "grp"), "head"),
        P("head", None),
        P(),
        P(("ctx", "grp"), None),
        P("ctx", None, None, "head"),
    )
    out_specs = (P(("ctx", "grp"), "head"), P("ctx", "grp", None, "head"))
    return jax.shard_map(body, mesh=mesh, in_specs=in_specs, out_specs=out_specs, check_vma=False)
```

```python
import functools
import jax
import jax.numpy as jnp
from jax import lax
from jax.experimental import pallas as pl
from jax.experimental.pallas import tpu as pltpu
from jax.sharding import PartitionSpec as P

D = 2880
HD = 64
TOP = 4
PIECE = 3 * 128


MESH = pl.DeviceIdType.MESH
F32 = jnp.float32
BF16 = jnp.bfloat16


def turn_of(step, count):
    return 1 + lax.rem(step + count // 2 - 1, count - 1)


def in_pair(values, group, lanes):
    zeros = jnp.zeros((values.shape[0], HD), values.dtype)
    if values.shape[1] == HD:
        return jnp.concatenate([values, zeros], 1), jnp.concatenate([zeros, values], 1)
    first = group % 2 == 0
    base = group // 2 * 2 * HD
    pair = values[:, base : base + 2 * HD]
    swapped = jnp.concatenate([pair[:, HD:], pair[:, :HD]], 1)
    low = jnp.where(lanes < HD, pair if first else swapped, jnp.zeros_like(pair))
    high = jnp.where(lanes >= HD, swapped if first else pair, jnp.zeros_like(pair))
    return low, high


def attend(block, reach, q_ref, kbuf, vbuf, att_ref):
    tokens = q_ref.shape[0]
    window = kbuf.shape[0]
    kv_local = kbuf.shape[1] // HD
    pairs = q_ref.shape[1] // (2 * HD * kv_local)
    rows = pairs * tokens
    place = lax.rem(lax.broadcasted_iota(jnp.int32, (rows, window), 0), tokens)
    column = lax.broadcasted_iota(jnp.int32, (rows, window), 1)
    ahead = place + reach * tokens - column
    allowed = (ahead >= 0) & (ahead < reach * tokens) & (column >= (reach - block) * tokens)
    lanes = lax.broadcasted_iota(jnp.int32, (window, 2 * HD), 1)
    left = lax.broadcasted_iota(jnp.int32, (rows, 2 * HD), 1) < HD
    for group in range(kv_local):
        key_pair = in_pair(kbuf[...], group, lanes)
        value_pair = in_pair(vbuf[...], group, lanes)
        first = group * pairs
        queries = jnp.concatenate(
            [
                q_ref[:, (first + p) * 2 * HD : (first + p + 1) * 2 * HD]
                for p in range(pairs)
            ],
            0,
        )
        mixed = jnp.zeros((rows, 2 * HD), F32)
        totals = []
        for side in range(2):
            scores = lax.dot_general(
                queries,
                key_pair[side],
                (((1,), (1,)), ((), ())),
                preferred_element_type=F32,
            )
            scores = jnp.where(allowed, scores * HD ** (-0.5), -1e30)
            row_max = jnp.max(scores, axis=1, keepdims=True)
            weights = jnp.where(allowed, jnp.exp(scores - row_max), 0.0)
            totals.append(jnp.sum(weights, axis=1, keepdims=True))
            mixed = mixed + jnp.dot(
                weights.astype(BF16), value_pair[side], preferred_element_type=F32
            )
        attended = (mixed / jnp.where(left, totals[0], totals[1])).astype(BF16)
        for p in range(pairs):
            att_ref[:, (first + p) * 2 * HD : (first + p + 1) * 2 * HD] = attended[
                p * tokens : (p + 1) * tokens
            ]


def layer_kernel(
    count,
    cap,
    reach,
    q_ref,
    k_ref,
    v_ref,
    res_ref,
    routes_ref,
    gain_ref,
    ow_hbm,
    w_hbm,
    hid_ref,
    act_ref,
    kbuf,
    vbuf,
    att_ref,
    ow,
    paired,
    w,
    psend,
    precv,
    hits_ref,
    before_ref,
    sbuf,
    rbuf,
    ksend_sem,
    krecv_sem,
    ow_sem,
    w_sem,
    psend_sem,
    precv_sem,
    send_sem,
    recv_sem,
    xsend_sem,
    xrecv_sem,
):
    me = lax.axis_index("ctx")
    head = lax.axis_index("head")
    heads = rbuf.shape[0]
    others = [lax.rem(head + j, heads) for j in range(1, heads)]
    half, tokens = hid_ref.shape
    width = act_ref.shape[2]

    def ow_copy(which, slot):
        rows = pl.ds(pl.multiple_of(which * half, 16), half)
        return pltpu.make_async_copy(ow_hbm.at[rows], ow.at[slot], ow_sem.at[slot])

    for j in range(1, heads):
        ow_copy(others[j - 1], j).start()
    ow_copy(head, 0).start()
    pltpu.make_async_copy(w_hbm, paired, w_sem).start()

    barrier = pltpu.get_barrier_semaphore()
    for other in others:
        pl.semaphore_signal(barrier, inc=1, device_id={"head": other}, device_id_type=MESH)

    def greet(step, carry):
        peer = lax.rem(me + step, count)
        pl.semaphore_signal(barrier, inc=1, device_id={"ctx": peer}, device_id_type=MESH)
        return carry

    lax.fori_loop(1, count, greet, 0)

    groups = lax.axis_size("grp")
    block = me * groups + lax.axis_index("grp")
    blocks = count * groups

    def at_block(index):
        return {"ctx": index // groups, "grp": lax.rem(index, groups)}

    for j in range(1, reach + 1):
        for peer in (lax.rem(block + j, blocks), lax.rem(block + blocks - j, blocks)):
            pl.semaphore_signal(barrier, inc=1, device_id=at_block(peer), device_id_type=MESH)

    def window_copies(j):
        place = pl.ds((reach - j) * tokens, tokens)
        target = at_block(lax.rem(block + j, blocks))
        return [
            pltpu.make_async_remote_copy(
                src_ref=source,
                dst_ref=buffer.at[place],
                send_sem=ksend_sem.at[n, j - 1],
                recv_sem=krecv_sem.at[n, j - 1],
                device_id=target,
                device_id_type=MESH,
            )
            for n, (source, buffer) in enumerate(((k_ref, kbuf), (v_ref, vbuf)))
        ]

    pl.semaphore_wait(barrier, count - 1 + heads - 1 + 2 * reach)
    for j in range(1, reach + 1):

        @pl.when(block + j < blocks)
        def _(j=j):
            for copy in window_copies(j):
                copy.start()

    kbuf[reach * tokens :, :] = k_ref[...]
    vbuf[reach * tokens :, :] = v_ref[...]

    def project(slot):
        return lax.dot_general(
            ow[slot], att_ref[...], (((1,), (1,)), ((), ())), preferred_element_type=F32
        ).astype(BF16)

    def exchange(j):
        return pltpu.make_async_remote_copy(
            src_ref=psend.at[j - 1],
            dst_ref=precv.at[j - 1],
            send_sem=psend_sem.at[j - 1],
            recv_sem=precv_sem.at[j - 1],
            device_id={"head": others[j - 1]},
            device_id_type=MESH,
        )

    for j in range(1, reach + 1):

        @pl.when(block >= j)
        def _(j=j):
            for copy in window_copies(j):
                copy.wait_recv()

        @pl.when(block < j)
        def _(j=j):
            place = pl.ds((reach - j) * tokens, tokens)
            kbuf[place, :] = jnp.zeros((tokens, kbuf.shape[1]), BF16)
            vbuf[place, :] = jnp.zeros((tokens, vbuf.shape[1]), BF16)

        @pl.when(block + j < blocks)
        def _(j=j):
            for copy in window_copies(j):
                copy.wait_send()

    attend(block, reach, q_ref, kbuf, vbuf, att_ref)

    for j in range(1, heads):
        ow_copy(others[j - 1], j).wait()
        psend[j - 1] = project(j)
        exchange(j).start()
    ow_copy(head, 0).wait()
    projected = project(0).astype(F32)

    expert_ids = lax.broadcasted_iota(jnp.int32, (count, tokens), 0)
    hits = jnp.zeros((count, tokens), F32)
    for k in range(routes_ref.shape[0]):
        hits = hits + jnp.where(routes_ref[k : k + 1, :] == expert_ids, 1.0, 0.0)
    earlier = jnp.where(
        lax.broadcasted_iota(jnp.int32, (tokens, tokens), 0)
        < lax.broadcasted_iota(jnp.int32, (tokens, tokens), 1),
        1.0,
        0.0,
    ).astype(BF16)
    hits_ref[...] = hits
    before_ref[...] = jnp.dot(hits.astype(BF16), earlier, preferred_element_type=F32)
    residual = res_ref[pl.ds(pl.multiple_of(head * half, 16), half), :].astype(F32)

    for j in range(1, heads):
        exchange(j).wait()
        projected = projected + precv[j - 1].astype(F32)
    hid_ref[...] = (residual + projected).astype(BF16)

    slots = lax.broadcasted_iota(jnp.int32, (cap, tokens), 0).astype(F32)

    def rows_for(expert):
        wanted = hits_ref[pl.ds(expert, 1), :] > 0.5
        picks = jnp.where((slots == before_ref[pl.ds(expert, 1), :]) & wanted, 1.0, 0.0)
        return lax.dot_general(
            picks.astype(BF16),
            hid_ref[...],
            (((1,), (1,)), ((), ())),
            preferred_element_type=F32,
        ).astype(BF16)

    def routed(step):
        turn = turn_of(step, count)
        return pltpu.make_async_remote_copy(
            src_ref=sbuf.at[turn],
            dst_ref=rbuf.at[head, me],
            send_sem=send_sem.at[turn],
            recv_sem=recv_sem.at[me],
            device_id={"ctx": lax.rem(me + turn, count)},
            device_id_type=MESH,
        )

    def landed(source):
        return pltpu.make_async_remote_copy(
            src_ref=rbuf.at[head, source],
            dst_ref=rbuf.at[head, source],
            send_sem=send_sem.at[0],
            recv_sem=recv_sem.at[source],
            device_id={"head": others[0]},
            device_id_type=MESH,
        )

    def crossed(j, source):
        return pltpu.make_async_remote_copy(
            src_ref=rbuf.at[head, source],
            dst_ref=rbuf.at[head, source],
            send_sem=xsend_sem.at[j - 1, source],
            recv_sem=xrecv_sem.at[j - 1, source],
            device_id={"head": others[j - 1]},
            device_id_type=MESH,
        )

    def cross(source):
        for j in range(1, heads):
            crossed(j, source).start()

    def mirror(source):
        for j in range(1, heads):
            origin = lax.rem(head + heads - j, heads)
            pltpu.make_async_remote_copy(
                src_ref=rbuf.at[origin, source],
                dst_ref=rbuf.at[origin, source],
                send_sem=xsend_sem.at[j - 1, source],
                recv_sem=xrecv_sem.at[j - 1, source],
                device_id={"head": others[j - 1]},
                device_id_type=MESH,
            ).wait_recv()

    def dispatch(step, carry):
        turn = turn_of(step, count)
        sbuf[turn] = rows_for(lax.rem(me + turn, count))
        routed(step).start()
        return carry

    lax.fori_loop(0, count - 1, dispatch, 0)
    rbuf[head, me] = rows_for(me)
    cross(me)
    pltpu.make_async_copy(w_hbm, paired, w_sem).wait()

    def unpair(step, carry):
        rows = pl.ds(pl.multiple_of(step * 32, 32), 32)
        pair = jnp.swapaxes(paired[rows], 0, 1)
        w[rows, :width] = pair[0]
        w[rows, width:] = pair[1]
        return carry

    lax.fori_loop(0, w.shape[0] // 32, unpair, 0)

    def expert(source):
        squares = jnp.zeros((cap, 1), F32)
        parts = []
        for part in range(heads):
            rows = rbuf[part, source].astype(F32)
            squares = squares + jnp.sum(rows * rows, axis=1, keepdims=True)
            parts.append((rows * gain_ref[part : part + 1, :]).astype(BF16))
        inverse_rms = lax.rsqrt(squares / (heads * half) + 1e-05)

        def product(low):
            total = jnp.zeros((cap, width), F32)
            for part in range(heads):
                total = total + jnp.dot(
                    parts[part],
                    w[part * half : (part + 1) * half, low : low + width],
                    preferred_element_type=F32,
                )
            return total

        gate = product(0) * inverse_rms
        up = product(width) * inverse_rms
        act_ref[source] = (gate * jax.nn.sigmoid(1.702 * gate) * (up + 1.0)).astype(BF16)

    def receive(step, carry):
        source = lax.rem(me + count - turn_of(step, count), count)
        landed(source).wait_recv()
        cross(source)
        before = jnp.where(
            step == 0, me, lax.rem(me + count - turn_of(jnp.maximum(step - 1, 0), count), count)
        )
        mirror(before)
        expert(before)
        return carry

    lax.fori_loop(0, count - 1, receive, 0)
    last = lax.rem(me + count - turn_of(count - 2, count), count)
    mirror(last)
    expert(last)

    def drain(step, carry):
        routed(step).wait_send()
        for j in range(1, heads):
            crossed(j, lax.rem(me + step + 1, count)).wait_send()
        return carry

    lax.fori_loop(0, count - 1, drain, 0)
    for j in range(1, heads):
        crossed(j, me).wait_send()


def line_kernel(
    count,
    cap,
    reach,
    late,
    q_hbm,
    k_hbm,
    v_hbm,
    res_hbm,
    routes_ref,
    gain_ref,
    ow_hbm,
    w_hbm,
    hid_hbm,
    act_hbm,
    q_ref,
    kbuf,
    vbuf,
    res_ref,
    att_ref,
    ow,
    paired,
    w,
    gains,
    psend,
    precv,
    meta,
    zbuf,
    ysend,
    rows,
    cross,
    acc,
    sums,
    out,
    in_sem,
    ksend_sem,
    krecv_sem,
    ow_sem,
    w_sem,
    psend_sem,
    precv_sem,
    msend_sem,
    mrecv_sem,
    zsend_sem,
    zrecv_sem,
    ysend_sem,
    yrecv_sem,
    xsend_sem,
    xrecv_sem,
    hid_sem,
    out_sem,
):
    me = lax.axis_index("ctx")
    head = lax.axis_index("head")
    other = 1 - head
    length = count // 2
    place = me // 2
    side = lax.rem(me, 2)
    half, tokens = hid_hbm.shape
    width = act_hbm.shape[2]
    parts = late + 2
    piece = rows.shape[4]
    rest = half - late * piece
    groups = lax.axis_size("grp")
    block = me * groups + lax.axis_index("grp")
    blocks = count * groups

    def at_block(index):
        return {"ctx": index // groups, "grp": lax.rem(index, groups)}

    def on_line(position):
        return {"ctx": position * 2 + side}

    partner = {"ctx": place * 2 + 1 - side}
    across = {"head": other}

    barrier = pltpu.get_barrier_semaphore()
    expected = 2
    for peer in (partner, across):
        pl.semaphore_signal(barrier, inc=1, device_id=peer, device_id_type=MESH)

    def greet(there, peer):
        @pl.when(there)
        def _():
            pl.semaphore_signal(barrier, inc=1, device_id=peer, device_id_type=MESH)

        return jnp.where(there, 1, 0)

    expected = expected + greet(place > 0, on_line(place - 1))
    expected = expected + greet(place + 1 < length, on_line(place + 1))
    for j in range(1, reach + 1):
        expected = expected + greet(block + j < blocks, at_block(block + j))
        expected = expected + greet(block >= j, at_block(block - j))

    def span(which, start, size):
        return pl.ds(pl.multiple_of(which * half + start, 16), size)

    late_size = late * piece
    far_start = (late + 1) * piece
    mine = pl.ds(reach * tokens, tokens)
    own_spot = pl.ds(0, half)
    early_spot = pl.ds(far_start, rest)
    late_spot = pl.ds(parts * piece, late_size)
    local = [
        pltpu.make_async_copy(k_hbm, kbuf.at[mine], in_sem.at[0]),
        pltpu.make_async_copy(v_hbm, vbuf.at[mine], in_sem.at[1]),
        pltpu.make_async_copy(q_hbm, q_ref, in_sem.at[2]),
    ]
    res_copies = [
        pltpu.make_async_copy(res_hbm.at[span(head, 0, half)], res_ref.at[own_spot], in_sem.at[3]),
        pltpu.make_async_copy(
            res_hbm.at[span(other, late_size, rest)], res_ref.at[early_spot], in_sem.at[4]
        ),
    ]
    w_copies = [
        pltpu.make_async_copy(w_hbm.at[span(which, start, size)], paired.at[spot], w_sem.at[n])
        for n, (which, start, size, spot) in enumerate(
            (
                (head, 0, half, own_spot),
                (other, late_size, rest, early_spot),
                (other, 0, late_size, late_spot),
            )
        )
    ]
    ow_copies = [
        pltpu.make_async_copy(ow_hbm.at[span(which, 0, half)], ow.at[n], ow_sem.at[n])
        for n, which in enumerate((other, head))
    ]
    for copy in local + ow_copies + res_copies + w_copies:
        copy.start()

    def remote(source, target, send, recv, device):
        return pltpu.make_async_remote_copy(
            src_ref=source,
            dst_ref=target,
            send_sem=send,
            recv_sem=recv,
            device_id=device,
            device_id_type=MESH,
        )

    def window_copies(j):
        rows_at = pl.ds((reach - j) * tokens, tokens)
        target = at_block(block + j)
        return [
            remote(source, buffer.at[rows_at], ksend_sem.at[n, j - 1], krecv_sem.at[n, j - 1], target)
            for n, (source, buffer) in enumerate(((k_hbm, kbuf), (v_hbm, vbuf)))
        ]

    expert_ids = lax.broadcasted_iota(jnp.int32, (count, tokens), 0)
    hits = jnp.zeros((count, tokens), F32)
    for k in range(routes_ref.shape[0]):
        hits = hits + jnp.where(routes_ref[k : k + 1, :] == expert_ids, 1.0, 0.0)
    earlier = jnp.where(
        lax.broadcasted_iota(jnp.int32, (tokens, tokens), 0)
        < lax.broadcasted_iota(jnp.int32, (tokens, tokens), 1),
        1.0,
        0.0,
    ).astype(BF16)
    before = jnp.dot(hits.astype(BF16), earlier, preferred_element_type=F32)
    meta[place] = jnp.where(hits > 0.5, before, -1.0)

    gain = gain_ref[...].reshape(1, 2 * half)
    gains[...] = jnp.zeros(gains.shape, F32)
    order = [(0, n) for n in range(late + 1)] + [(1, late)] + [(1, n) for n in range(late)]
    for n, (far, index) in enumerate(order):
        size = piece if index < late else rest
        left = gain[:, index * piece : index * piece + size]
        right = gain[:, half + index * piece : half + index * piece + size]
        gains[n : n + 1, :size] = jnp.where(head == far, left, right)
    if rest < piece:
        blank = piece - rest
        for start in (half, far_start + rest):
            zbuf[:, start : start + blank, :] = jnp.zeros((length, blank, tokens), BF16)
            paired[start : start + blank] = jnp.zeros((blank, 2, width), BF16)

    pl.semaphore_wait(barrier, expected)
    for j in range(1, reach + 1):

        @pl.when(block + j < blocks)
        def _(j=j):
            for copy in window_copies(j):
                copy.start()

    def meta_copy(owner, up):
        to = jnp.where(up == 1, place + 1, place - 1)
        spot = meta.at[owner]
        return remote(spot, spot, msend_sem.at[up, owner], mrecv_sem.at[owner], on_line(to))

    def has_next(up):
        return jnp.where(up == 1, place + 1 < length, place > 0)

    for up in range(2):

        @pl.when(has_next(up))
        def _(up=up):
            meta_copy(place, up).start()

    for j in range(1, reach + 1):

        @pl.when(block < j)
        def _(j=j):
            rows_at = pl.ds((reach - j) * tokens, tokens)
            kbuf[rows_at, :] = jnp.zeros((tokens, kbuf.shape[1]), BF16)
            vbuf[rows_at, :] = jnp.zeros((tokens, vbuf.shape[1]), BF16)

    for copy in local:
        copy.wait()
    for j in range(1, reach + 1):

        @pl.when(block >= j)
        def _(j=j):
            for copy in window_copies(j):
                copy.wait_recv()

    attend(block, reach, q_ref, kbuf, vbuf, att_ref)

    def part(index, size=piece):
        return pl.ds(pl.multiple_of(index * piece, 16), size)

    def sized(index, action):
        @pl.when(index < late)
        def _():
            action(piece)

        @pl.when(index >= late)
        def _():
            action(rest)

    def project(slot, index, size):
        return lax.dot_general(
            ow[slot, part(index, size), :],
            att_ref[...],
            (((1,), (1,)), ((), ())),
            preferred_element_type=F32,
        ).astype(BF16)

    def exchange(index, size):
        return remote(
            psend.at[part(index, size)],
            precv.at[part(index, size)],
            psend_sem,
            precv_sem.at[index],
            across,
        )

    for copy in ow_copies:
        copy.wait()

    def offer(index, carry):
        psend[part(index), :] = project(0, index, piece)
        exchange(index, piece).start()
        return carry

    lax.fori_loop(0, late, offer, 0)
    for n in range(2):
        psend[part(late + n, rest), :] = project(n, late, rest)
        exchange(late + n, rest).start()

    def keep(index, carry):
        zbuf[place, part(index), :] = project(1, index, piece)
        return carry

    lax.fori_loop(0, late, keep, 0)
    zbuf[place, part(late, rest), :] = psend[part(late + 1, rest), :]
    zbuf[place, part(late + 1, rest), :] = psend[part(late, rest), :]
    for copy in res_copies + w_copies:
        copy.wait()

    def unpair(index):
        def one(step, carry):
            at = pl.ds(pl.multiple_of(index * piece + step * 32, 32), 32)
            pair = jnp.swapaxes(paired[at], 0, 1)
            w[at, :width] = pair[0]
            w[at, width:] = pair[1]
            return carry

        lax.fori_loop(0, piece // 32, one, 0)


    def line_copy(owner, index, up, size):
        to = jnp.where(up == 1, place + 1, place - 1)
        spot = zbuf.at[owner, part(index, size)]
        return remote(
            spot, spot, zsend_sem.at[up, owner], zrecv_sem.at[owner, index], on_line(to)
        )

    def reduce(index, size):
        at = part(index, size)
        exchange(index, size).wait_recv()
        total = zbuf[place, at, :].astype(F32) + precv[at, :].astype(F32)
        zbuf[place, at, :] = (res_ref[at, :].astype(F32) + total).astype(BF16)
        for up in range(2):

            @pl.when(has_next(up))
            def _(up=up):
                line_copy(place, index, up, size).start()

    slots = lax.broadcasted_iota(jnp.int32, (cap, tokens), 0).astype(F32)

    def y_copy(owner, index):
        return remote(
            ysend.at[owner, index],
            rows.at[owner, index, 1],
            ysend_sem,
            yrecv_sem.at[owner, index],
            partner,
        )

    def x_copy(owner, index, which):
        return remote(
            rows.at[owner, index, which],
            cross.at[owner, index, which],
            xsend_sem,
            xrecv_sem.at[owner, index, which],
            across,
        )

    def pick(owner, index):
        def picks(expert):
            wanted = meta[owner, pl.ds(expert, 1), :]
            return jnp.where(slots == wanted, 1.0, 0.0)

        both = jnp.concatenate([picks(place * 2 + 1 - side), picks(me)], 0).astype(BF16)
        found = lax.dot_general(
            both,
            zbuf[owner, part(index), :],
            (((1,), (1,)), ((), ())),
            preferred_element_type=F32,
        )
        ysend[owner, index] = found[:cap].astype(BF16)
        y_copy(owner, index).start()
        rows[owner, index, 0] = found[cap:].astype(BF16)

        @pl.when(index < late)
        def _():
            x_copy(owner, index, 0).start()

    def gather(buffer, owner, index, at, fresh):
        raw = buffer[owner, index].astype(F32).reshape(2 * cap, piece)
        squares = jnp.sum(raw * raw, axis=1, keepdims=True)
        left = (raw * gains[pl.ds(at, 1), :]).astype(BF16)
        sums[owner] = jnp.where(fresh, 0.0, sums[owner]) + squares
        for low in (0, width):
            product = jnp.dot(
                left, w[part(at), low : low + width], preferred_element_type=F32
            )
            held = acc[owner, :, low : low + width]
            acc[owner, :, low : low + width] = jnp.where(fresh, 0.0, held) + product

    def result(owner, which):
        source = owner * 2 + jnp.where(which == 0, side, 1 - side)
        return pltpu.make_async_copy(out.at[owner, which], act_hbm.at[source], out_sem)

    def owner_of(step, up):
        return jnp.where(up == 1, place + step, place - step)

    def exists(step, up):
        owner = owner_of(step, up)
        return (owner >= 0) & (owner < length) & (step + 1 - up > 0)

    def each(step, action):
        for up in range(2):

            @pl.when(exists(step, up))
            def _(up=up):
                action(owner_of(step, up), up)

    def meet(owner, index):
        y_copy(owner, index).wait_recv()

        @pl.when(index < late)
        def _():
            x_copy(owner, index, 1).start()

        gather(rows, owner, index, index, index == 0)

    def take(owner):
        def add(index, carry):
            for which in range(2):
                x_copy(owner, index, which).wait_recv()
            gather(cross, owner, index, parts + index, False)
            return carry

        lax.fori_loop(0, late, add, 0)

    def close(owner):
        inverse_rms = lax.rsqrt(sums[owner][:, :1] / (2 * half) + 1e-05)
        gate = acc[owner, :, :width] * inverse_rms
        up = acc[owner, :, width:] * inverse_rms
        active = gate * jax.nn.sigmoid(1.702 * gate) * (up + 1.0)
        out[owner] = active.reshape(2, cap, width).astype(BF16)
        for which in range(2):
            result(owner, which).start()

    hid_copy = pltpu.make_async_copy(zbuf.at[place, own_spot], hid_hbm, hid_sem)

    lag = 2

    def turn(step, index):
        late_turn = index < lag
        met_step = jnp.where(late_turn, step - 1, step)
        met_index = jnp.where(late_turn, index + parts - lag, index - lag)
        ending = jnp.where(step < length, parts - 1, lag - 1)
        closing = (step > 0) & (index == ending)

        @pl.when(step == 0)
        def _():
            sized(index, lambda size: reduce(index, size))

        def collect(owner, up):
            @pl.when(step > 0)
            def _():
                @pl.when(index == 0)
                def _():
                    meta_copy(owner, 1 - up).wait_recv()

                    @pl.when(has_next(1 - up))
                    def _():
                        meta_copy(owner, 1 - up).start()

                def pass_on(size):
                    line_copy(owner, index, 1 - up, size).wait_recv()

                    @pl.when(has_next(1 - up))
                    def _():
                        line_copy(owner, index, 1 - up, size).start()

                sized(index, pass_on)

            pick(owner, index)

        each(step, collect)

        @pl.when(step == 0)
        def _():
            for n in range(2):
                which = index * 2 + n

                @pl.when(which < w.shape[0] // piece)
                def _(which=which):
                    unpair(which)

        @pl.when((step == 1) & (index == 0))
        def _():
            hid_copy.start()

        @pl.when(closing)
        def _():
            each(step - 1, lambda owner, up: take(owner))

        @pl.when(met_step >= 0)
        def _():
            each(met_step, lambda owner, up: meet(owner, met_index))

        @pl.when(closing)
        def _():
            each(step - 1, lambda owner, up: close(owner))

    def advance(step, carry):
        def one(index, carry):
            turn(step, index)
            return carry

        lax.fori_loop(0, jnp.where(step < length, parts, lag), one, 0)
        return carry

    lax.fori_loop(0, length + 1, advance, 0)

    y_whole = remote(ysend, ysend, ysend_sem, yrecv_sem.at[0, 0], partner)
    x_whole = remote(cross, cross, xsend_sem, xrecv_sem.at[0, 0, 0], across)
    y_whole.wait_send()
    x_whole.wait_send()

    def drain(owner, carry):
        for up in range(2):
            came = jnp.where(up == 1, owner <= place, owner >= place)

            @pl.when(has_next(up) & came)
            def _(up=up):
                meta_copy(owner, up).wait_send()
                sent = zbuf.at[owner, pl.ds(0, half + rest)]
                remote(
                    sent, sent, zsend_sem.at[up, owner], zrecv_sem.at[owner, 0], across
                ).wait_send()

        return carry

    lax.fori_loop(0, length, drain, 0)
    pltpu.make_async_copy(out, out, out_sem).wait()
    hid_copy.wait()
    sent = psend.at[pl.ds(0, half + rest)]
    remote(sent, sent, psend_sem, precv_sem.at[0], across).wait_send()

    for j in range(1, reach + 1):

        @pl.when(block + j < blocks)
        def _(j=j):
            for copy in window_copies(j):
                copy.wait_send()


def place_kernel(hid_in, act_in, hid_out, act_out, hid, act, in_sem, out_sem):
    pieces = 4
    parts = 2
    size = hid_in.shape[0] // parts
    spots = [(hid_in, hid, hid_out, pl.ds(n * size, size)) for n in range(parts)]
    spots += [(act_in, act, act_out, pl.ds(n * (act_in.shape[0] // pieces), act_in.shape[0] // pieces)) for n in range(pieces)]
    loads = [
        pltpu.make_async_copy(source.at[at], held.at[at], in_sem.at[n])
        for n, (source, held, _, at) in enumerate(spots)
    ]
    stores = [
        pltpu.make_async_copy(held.at[at], target.at[at], out_sem.at[n])
        for n, (_, held, target, at) in enumerate(spots)
    ]
    for copy in loads:
        copy.start()
    for load, store in zip(loads, stores):
        load.wait()
        store.start()
    for copy in stores:
        copy.wait()


def placed(hidden, active):
    in_hbm = pl.BlockSpec(memory_space=pl.ANY)
    pieces = active.shape[0]
    return pl.pallas_call(
        place_kernel,
        out_shape=(
            jax.ShapeDtypeStruct(hidden.shape, hidden.dtype),
            jax.ShapeDtypeStruct(active.shape, active.dtype),
        ),
        in_specs=[in_hbm] * 2,
        out_specs=(in_hbm, in_hbm),
        scratch_shapes=[
            pltpu.VMEM(hidden.shape, hidden.dtype),
            pltpu.VMEM(active.shape, active.dtype),
            pltpu.SemaphoreType.DMA((2 * pieces,)),
            pltpu.SemaphoreType.DMA((2 * pieces,)),
        ],
    )(hidden, active)


def along_line(
    count, cap, reach, queries, keys, values, residual, routes, norm_gain, out_weight, expert_weight
):
    tokens = queries.shape[0]
    width_all = residual.shape[1]
    half = width_all // 2
    length = count // 2
    width = expert_weight.shape[3]
    piece = PIECE
    late = (half - 16) // piece
    parts = late + 2
    total = parts + late
    in_vmem = pl.BlockSpec(memory_space=pltpu.VMEM)
    in_hbm = pl.BlockSpec(memory_space=pl.ANY)
    dma = pltpu.SemaphoreType.DMA
    return pl.pallas_call(
        functools.partial(line_kernel, count, cap, reach, late),
        out_shape=(
            jax.ShapeDtypeStruct((half, tokens), BF16),
            jax.ShapeDtypeStruct((count, cap, width), BF16),
        ),
        in_specs=[in_hbm] * 4 + [in_vmem] * 2 + [in_hbm] * 2,
        out_specs=(in_hbm, in_hbm),
        scratch_shapes=[
            pltpu.VMEM(queries.shape, BF16),
            pltpu.VMEM(((reach + 1) * tokens, keys.shape[1]), BF16),
            pltpu.VMEM(((reach + 1) * tokens, values.shape[1]), BF16),
            pltpu.VMEM((parts * piece, tokens), BF16),
            pltpu.VMEM(queries.shape, BF16),
            pltpu.VMEM((2, half, out_weight.shape[0]), BF16),
            pltpu.VMEM((total * piece, 2, width), BF16),
            pltpu.VMEM((total * piece, 2 * width), BF16),
            pltpu.VMEM((total, piece), F32),
            pltpu.VMEM((parts * piece, tokens), BF16),
            pltpu.VMEM((parts * piece, tokens), BF16),
            pltpu.VMEM((length, count, tokens), F32),
            pltpu.VMEM((length, parts * piece, tokens), BF16),
            pltpu.VMEM((length, parts, cap, piece), BF16),
            pltpu.VMEM((length, parts, 2, cap, piece), BF16),
            pltpu.VMEM((length, late, 2, cap, piece), BF16),
            pltpu.VMEM((length, 2 * cap, 2 * width), F32),
            pltpu.VMEM((length, 2 * cap, 128), F32),
            pltpu.VMEM((length, 2, cap, width), BF16),
            dma((5,)),
            dma((2, reach)),
            dma((2, reach)),
            dma((2,)),
            dma((3,)),
            dma,
            dma((parts,)),
            dma((2, length)),
            dma((length,)),
            dma((2, length)),
            dma((length, parts)),
            dma,
            dma((length, parts)),
            dma,
            dma((length, late, 2)),
            dma,
            dma,
        ],
        compiler_params=pltpu.CompilerParams(
            collective_id=1, has_side_effects=True, vmem_limit_bytes=60 * 1024 * 1024
        ),
    )(
        queries,
        keys,
        values,
        residual.T,
        routes.T,
        norm_gain,
        out_weight.T,
        expert_weight[0],
    )


def body(residual, queries, keys, values, out_weight, norm_gain, routes, expert_weight):
    tokens_here = queries.shape[0]
    heads_count = lax.axis_size("head")
    reach = max(1, lax.axis_size("ctx") // 16) * lax.axis_size("grp")
    width_all = residual.shape[1]
    half = width_all // heads_count
    count = lax.axis_size("ctx")
    experts_all = expert_weight.shape[0] * count
    routed = tokens_here * TOP
    cap = min(tokens_here, routed // experts_all + max(1, routed // (8 * experts_all)))
    hidden_width = expert_weight.shape[3]
    if heads_count == 2 and count % 2 == 0 and experts_all == count and 2 * cap >= tokens_here and half >= 2 * PIECE:
        hidden, active = along_line(
            count,
            cap,
            reach,
            queries,
            keys,
            values,
            residual,
            routes,
            norm_gain,
            out_weight,
            expert_weight,
        )
        hidden, active = placed(hidden, active)
        return (hidden.T, active.reshape(1, 1, count * cap, hidden_width))
    in_vmem = pl.BlockSpec(memory_space=pltpu.VMEM)
    in_hbm = pl.BlockSpec(memory_space=pl.ANY)
    hidden, active = pl.pallas_call(
        functools.partial(layer_kernel, count, cap, reach),
        out_shape=(
            jax.ShapeDtypeStruct((half, tokens_here), BF16),
            jax.ShapeDtypeStruct((count, cap, hidden_width), BF16),
        ),
        in_specs=[in_vmem] * 6 + [in_hbm] * 2,
        out_specs=(in_vmem, in_vmem),
        scratch_shapes=[
            pltpu.VMEM(((reach + 1) * tokens_here, keys.shape[1]), BF16),
            pltpu.VMEM(((reach + 1) * tokens_here, values.shape[1]), BF16),
            pltpu.VMEM(queries.shape, BF16),
            pltpu.VMEM((heads_count, half, out_weight.shape[0]), BF16),
            pltpu.VMEM((width_all, 2, hidden_width), BF16),
            pltpu.VMEM((width_all, 2 * hidden_width), BF16),
            pltpu.VMEM((heads_count - 1, half, tokens_here), BF16),
            pltpu.VMEM((heads_count - 1, half, tokens_here), BF16),
            pltpu.VMEM((count, tokens_here), F32),
            pltpu.VMEM((count, tokens_here), F32),
            pltpu.VMEM((count, cap, half), BF16),
            pltpu.VMEM((heads_count, count, cap, half), BF16),
            pltpu.SemaphoreType.DMA((2, reach)),
            pltpu.SemaphoreType.DMA((2, reach)),
            pltpu.SemaphoreType.DMA((heads_count,)),
            pltpu.SemaphoreType.DMA,
            pltpu.SemaphoreType.DMA((heads_count - 1,)),
            pltpu.SemaphoreType.DMA((heads_count - 1,)),
            pltpu.SemaphoreType.DMA((count,)),
            pltpu.SemaphoreType.DMA((count,)),
            pltpu.SemaphoreType.DMA((heads_count - 1, count)),
            pltpu.SemaphoreType.DMA((heads_count - 1, count)),
        ],
        compiler_params=pltpu.CompilerParams(
            collective_id=0, has_side_effects=True, vmem_limit_bytes=60 * 1024 * 1024
        ),
    )(
        queries,
        keys,
        values,
        residual.T,
        routes.T,
        norm_gain.reshape(heads_count, half),
        out_weight.T,
        expert_weight[0],
    )
    return (hidden.T, active.reshape(1, 1, count * cap, hidden_width))


def solution(mesh):
    in_specs = (
        P(("ctx", "grp"), None),
        P(("ctx", "grp"), "head"),
        P(("ctx", "grp"), "head"),
        P(("ctx", "grp"), "head"),
        P("head", None),
        P(),
        P(("ctx", "grp"), None),
        P("ctx", None, None, "head"),
    )
    out_specs = (P(("ctx", "grp"), "head"), P("ctx", "grp", None, "head"))
    return jax.shard_map(body, mesh=mesh, in_specs=in_specs, out_specs=out_specs, check_vma=False)
```
